256 devices in a mesh: dp: 2 (over core), ctx: 32 (over y, z), grp: 4 (over x).
Axes of the slice: x: 4, y: 4, z: 8, core: 2. Of those that a mesh axis runs over, the one named last changes fastest.
Arguments:
- projected: bfloat16 [4, 8192, 3, 4096], P('dp', 'ctx', None, 'grp'), may hold values from -6 to 6
- short_w: float32 [3, 3, 4096], P(None, None, 'grp'), may hold values from -2.5 to 2.5
- medium_h: bfloat16 [256, 128], P('grp'), may hold values from -3 to 3
- out_w: bfloat16 [4096, 4096], P('ctx', 'grp'), may hold values from -0.09375 to 0.09375
- grad_out: bfloat16 [4, 8192, 4096], P('dp', 'ctx', 'grp'), may hold values from -6 to 6
Outputs:
- block_out: bfloat16 [4, 8192, 4096], P('dp', 'ctx', 'grp')
- grad_projected: bfloat16 [4, 8192, 3, 4096], P('dp', 'ctx', None, 'grp')
- filter_grad: float32 [256, 128], P('grp')
- short_grad: float32 [3, 3, 4096], P(None, None, 'grp')
The draws below stay inside these ranges and needn't reach their ends.
All inputs are finite; a program needn't handle non-finite values.
Results may differ from the reference program's by a relative error of at most 0.0064.
Values may be sent and summed in bfloat16 or wider, within the bound.
A program may use at most 128 MiB of HBM per device.

```python
import math
import jax
import jax.numpy as jnp
from jax import lax

D = 4096
G = 256
TAPS = 128
SHORT = 3
LEN = 8192
SEQS = 4


def draw_medium_h(key, part):
    noise_key, rate_key = jax.random.split(key)
    noise = jnp.clip(jax.random.normal(noise_key, (G, TAPS), jnp.float32), -4.0, 4.0)
    spans = jnp.exp(jax.random.uniform(rate_key, (G, 1), jnp.float32, math.log(4.0), math.log(512.0)))
    positions = jnp.arange(TAPS, dtype=jnp.float32)[None, :]
    values = noise * jnp.exp(-positions / spans) * jnp.sqrt(2.0 / spans + 1.0 / TAPS)
    return values.astype(jnp.bfloat16)


def level_of(key, shape, cuts, low, largest):
    factor_of, own = 1.0, jax.random.fold_in(key, 6)
    for axis_at, blocks in cuts:
        steps = jnp.exp(jax.random.uniform(jax.random.fold_in(own, axis_at), (blocks,), jnp.float32, low / len(cuts), largest / len(cuts)))
        factor_of = factor_of * jnp.repeat(steps, shape[axis_at] // blocks).reshape([-1 if axis == axis_at else 1 for axis in range(len(shape))])
    return factor_of


def normal_values(rng, shape, deviation, limit, pieces=(), kind=jnp.bfloat16):
    entries = jax.random.normal(rng, shape, jnp.float32) * deviation
    if len(pieces) > 0:
        entries = level_of(rng, shape, pieces, -0.22, 0.18) * entries
    return jnp.clip(entries, min=-limit, max=limit).astype(kind)


def setup_inputs(seed: int = 0) -> dict:
    splits = jax.random.split(jax.random.key(seed), 6)
    return {
        "projected": normal_values(splits[0], (SEQS, LEN, 3, D), 1.0, 6.0, ((0, 2), (1, 32), (3, 4))),
        "short_w": normal_values(splits[1], (3, SHORT, D), 0.4, 2.5, ((2, 4),), jnp.float32),
        "medium_h": draw_medium_h(jax.random.fold_in(splits[5], 71), 0),
        "out_w": normal_values(splits[3], (D, D), D ** -0.5, 0.09375, ((0, 32), (1, 4))),
        "grad_out": normal_values(splits[4], (SEQS, LEN, D), 1.0, 6.0, ((0, 2), (1, 32), (2, 4))),
    }


def windows(padded, block_rows, reach):
    seqs_here = padded.shape[0]
    block_count = (padded.shape[1] - reach) // block_rows
    extended = jnp.pad(padded, ((0, 0), (0, block_rows - reach), (0, 0), (0, 0)))
    leading = extended[:, :block_count * block_rows].reshape(seqs_here, block_count, block_rows, padded.shape[2], padded.shape[3])
    second = extended[:, block_rows:].reshape(seqs_here, block_count, block_rows, padded.shape[2], padded.shape[3])[:, :, :reach]
    return jnp.concatenate([leading, second], axis=2)

def banded(filters, block_rows):
    groups_here = filters.shape[0]
    tap_count = filters.shape[1]
    line_width = block_rows + tap_count
    padded_line = jnp.concatenate([filters, jnp.zeros((groups_here, block_rows), filters.dtype)], axis=1)
    tiled = jnp.broadcast_to(padded_line[:, None, :], (groups_here, block_rows, line_width)).reshape(groups_here, block_rows * line_width)
    return tiled[:, :block_rows * (line_width - 1)].reshape(groups_here, block_rows, line_width - 1)

def band_conv(padded, matrix, block_rows):
    reach = matrix.shape[2] - block_rows
    windowed = windows(padded, block_rows, reach)
    result = jnp.einsum('gtj,sbjgc->sbtgc', matrix.astype(jnp.float32), windowed.astype(jnp.float32))
    return result.reshape(padded.shape[0], padded.shape[1] - reach, padded.shape[2] * padded.shape[3])

def lag_sums(grad_blocks, windowed, tap_count):
    products = jnp.einsum('sbtgc,sbjgc->gtj', grad_blocks.astype(jnp.float32), windowed.astype(jnp.float32))
    groups_here = products.shape[0]
    block_rows = products.shape[1]
    line_width = products.shape[2]
    flat_rows = jnp.pad(products.reshape(groups_here, block_rows * line_width), ((0, 0), (0, block_rows)))
    skewed = flat_rows.reshape(groups_here, block_rows, line_width + 1)[:, :, :tap_count]
    return lax.optimization_barrier(jnp.sum(skewed, axis=1))[:, ::-1]

def featurize(padded, weights):
    short_reach = weights.shape[1] - 1
    axis_rows = padded.ndim - 3
    row_count = padded.shape[axis_rows] - short_reach
    total = None
    for offset in range(weights.shape[1]):
        start = short_reach - offset
        term = weights[:, offset, :] * lax.slice_in_dim(padded, start, start + row_count, axis=axis_rows)
        total = term if total is None else total + term
    return total

def adjoint(padded, weights):
    short_reach = weights.shape[1] - 1
    axis_rows = padded.ndim - 3
    row_count = padded.shape[axis_rows] - short_reach
    total = None
    for offset in range(weights.shape[1]):
        term = weights[:, offset, :] * lax.slice_in_dim(padded, offset, offset + row_count, axis=axis_rows)
        total = term if total is None else total + term
    return total

def short_sums(feature_grad, padded, short_taps):
    axis_rows = padded.ndim - 3
    row_count = feature_grad.shape[axis_rows]
    short_reach = short_taps - 1
    axes_summed = tuple(range(feature_grad.ndim - 2))
    terms = []
    for offset in range(short_taps):
        start = short_reach - offset
        shifted = lax.slice_in_dim(padded, start, start + row_count, axis=axis_rows)
        terms.append(lax.optimization_barrier(jnp.sum(feature_grad * shifted, axis=axes_summed)))
    return jnp.stack(terms, axis=1)

def reference(projected, short_w, medium_h, out_w, grad_out):
    tap_count = medium_h.shape[1]
    reach = tap_count - 1
    short_taps = short_w.shape[1]
    short_reach = short_taps - 1
    groups = medium_h.shape[0]
    group_size = D // groups
    block_rows = math.gcd(LEN, 128)
    causal = banded(medium_h[:, ::-1], block_rows)
    anticausal = banded(medium_h, block_rows)

    def one_sequence(carry, inputs):
        sequence, cotangent = inputs
        padded_input = jnp.pad(sequence.astype(jnp.float32), ((short_reach, 0), (0, 0), (0, 0)))
        features = featurize(padded_input, short_w)
        query = features[:, 0]
        keys = features[:, 1]
        values = features[:, 2]
        product = (keys * values).astype(jnp.bfloat16)
        product_pad = jnp.pad(product, ((reach, 0), (0, 0))).reshape(1, LEN + reach, groups, group_size)
        mixed = band_conv(product_pad, causal, block_rows)[0]
        gated = (query * mixed).astype(jnp.bfloat16)
        block_out = jnp.dot(gated, out_w, preferred_element_type=jnp.float32).astype(jnp.bfloat16)
        gated_grad = lax.optimization_barrier(jnp.dot(cotangent, out_w.T, preferred_element_type=jnp.float32).astype(jnp.bfloat16)).astype(jnp.float32)
        query_grad = gated_grad * mixed
        mix_grad = (gated_grad * query).astype(jnp.bfloat16)
        mix_pad = jnp.pad(mix_grad, ((0, reach), (0, 0))).reshape(1, LEN + reach, groups, group_size)
        product_grad = band_conv(mix_pad, anticausal, block_rows)[0]
        filter_part = lag_sums(mix_grad.reshape(1, LEN // block_rows, block_rows, groups, group_size), windows(product_pad, block_rows, reach), tap_count)
        feature_grad = jnp.stack([query_grad, product_grad * values, product_grad * keys], axis=1).astype(jnp.bfloat16)
        feature_float = feature_grad.astype(jnp.float32)
        grad_pad = jnp.pad(feature_float, ((0, short_reach), (0, 0), (0, 0)))
        input_grad = adjoint(grad_pad, short_w).astype(jnp.bfloat16)
        short_part = short_sums(feature_float, padded_input, short_taps)
        return ((carry[0] + filter_part, carry[1] + short_part), (block_out, input_grad))
    start_sums = (jnp.zeros((groups, tap_count), jnp.float32), jnp.zeros((3, short_taps, D), jnp.float32))
    sums, stacked = lax.scan(one_sequence, start_sums, (projected, grad_out))
    filter_grad = sums[0] / math.sqrt(SEQS * LEN * group_size)
    short_grad = sums[1] / math.sqrt(SEQS * LEN)
    return (stacked[0], stacked[1], filter_grad, short_grad)
```

```python
import functools
import math

import jax
import jax.numpy as jnp
from jax import lax
from jax.experimental import pallas as pl
from jax.experimental.pallas import tpu as pltpu
from jax.sharding import PartitionSpec as P

BF = jnp.bfloat16
F32 = jnp.float32
LANES = 128
BLOCK = 128
HALO = 16
MESH = pl.DeviceIdType.MESH


def from_behind(block, axis, distance):
    devices = range(lax.axis_size(axis))
    route = [(i - distance, i) for i in devices if i - distance in devices]
    return lax.ppermute(block, axis, route)


def fill(scratch, front, rows):
    scratch[0:HALO, :] = front.astype(F32)
    scratch[HALO : HALO + rows.shape[0], :] = rows.astype(F32)


def feature(scratch, taps, stream, count):
    total = None
    for offset in range(taps.shape[1]):
        start = HALO - offset
        term = taps[stream, offset : offset + 1, :] * scratch[start : start + count, :]
        total = term if total is None else total + term
    return total


def band_rows(lines, band):
    groups = lines.shape[0]
    for g in range(groups):
        line = jnp.broadcast_to(lines[g : g + 1, :], (BLOCK, lines.shape[1]))
        turned = pltpu.roll(line, 0, 1, stride=1, stride_axis=0)
        band[g * BLOCK : (g + 1) * BLOCK, :] = turned.astype(BF)


def group_of_lane(shape, groups):
    lane = lax.broadcasted_iota(jnp.int32, shape, len(shape) - 1)
    return (lane % LANES) // (LANES // groups)


def own_group(wide, groups):
    owner = group_of_lane((BLOCK, wide.shape[1]), groups)
    kept = wide[0:BLOCK]
    for g in range(1, groups):
        kept = jnp.where(owner == g, wide[g * BLOCK : (g + 1) * BLOCK], kept)
    return kept


def window_pair(padded, start):
    return jnp.concatenate(
        [padded[s, start : start + 2 * BLOCK, :] for s in range(padded.shape[0])], axis=1
    )


def tail_kernel(front_ref, rows_ref, taps_ref, out_ref, scratch):
    for s in range(rows_ref.shape[0]):
        found = []
        for stream in (1, 2):
            fill(scratch, front_ref[s, stream], rows_ref[s, stream])
            found.append(feature(scratch, taps_ref, stream, BLOCK))
        out_ref[s] = (found[0] * found[1]).astype(BF)


def forward_kernel(
    front_ref, rows_ref, taps_ref, lines_ref, behind_ref,
    gated_ref, mixed_ref, product_ref, scratch, padded, queries, band,
):
    seqs, row_count = rows_ref.shape[0], rows_ref.shape[2]
    groups = lines_ref.shape[0]
    band_rows(lines_ref[...], band)
    for s in range(seqs):
        found = []
        for stream in range(3):
            fill(scratch, front_ref[s, stream], rows_ref[s, stream])
            found.append(feature(scratch, taps_ref, stream, row_count))
        queries[s] = found[0]
        product = (found[1] * found[2]).astype(BF)
        product_ref[s] = product
        padded[s, 0:BLOCK, :] = behind_ref[s]
        padded[s, BLOCK : BLOCK + row_count, :] = product
    for b in range(row_count // BLOCK):
        here = slice(b * BLOCK, (b + 1) * BLOCK)
        wide = jnp.dot(
            band[...], window_pair(padded, b * BLOCK), preferred_element_type=F32
        )
        kept = own_group(wide, groups)
        for s in range(seqs):
            mixed = kept[:, s * LANES : (s + 1) * LANES]
            mixed_ref[s, here, :] = mixed
            gated_ref[s, here, :] = (queries[s, here, :] * mixed).astype(BF)


def mix_kernel(
    cotangent_ref, front_ref, rows_ref, taps_ref, lines_ref, mixed_ref,
    mix_ref, head_ref, scratch, band,
):
    seqs, row_count = rows_ref.shape[0], rows_ref.shape[2]
    groups = lines_ref.shape[0]
    band_rows(lines_ref[...], band)
    for s in range(seqs):
        fill(scratch, front_ref[s, 0], rows_ref[s, 0])
        query = feature(scratch, taps_ref, 0, row_count)
        mix_ref[s] = (cotangent_ref[s].astype(F32) * query).astype(BF)
    wide = jnp.dot(band[...], window_pair(mix_ref, 0), preferred_element_type=F32)
    kept = own_group(wide, groups)
    for s in range(seqs):
        pulled = kept[0:HALO, s * LANES : (s + 1) * LANES]
        found = []
        for stream in (1, 2):
            fill(scratch, front_ref[s, stream], rows_ref[s, stream, 0:HALO])
            found.append(feature(scratch, taps_ref, stream, HALO))
        head_ref[s, 0] = (cotangent_ref[s, 0:HALO, :].astype(F32) * mixed_ref[s, 0:HALO, :]).astype(BF)
        head_ref[s, 1] = (pulled * found[1]).astype(BF)
        head_ref[s, 2] = (pulled * found[0]).astype(BF)


def filter_kernel(mix_ref, product_ref, behind_ref, sums_ref, padded):
    seqs, row_count = product_ref.shape[0], product_ref.shape[1]
    groups = sums_ref.shape[0]
    blocks = row_count // BLOCK
    for s in range(seqs):
        padded[s, 0:BLOCK, :] = behind_ref[s]
        padded[s, BLOCK : BLOCK + row_count, :] = product_ref[s]
    rows = lax.broadcasted_iota(jnp.int32, (BLOCK, BLOCK), 0)
    columns = lax.broadcasted_iota(jnp.int32, (BLOCK, BLOCK), 1)
    upturn = (rows + columns == BLOCK - 1).astype(BF)
    parts, wins = [], []
    for s in range(seqs):
        for b in range(blocks):
            parts.append(mix_ref[s, b * BLOCK : (b + 1) * BLOCK, :])
            wins.append(padded[s, b * BLOCK : (b + 2) * BLOCK, :])
    grads = jnp.dot(upturn, jnp.concatenate(parts, axis=1), preferred_element_type=F32)
    windows = jnp.concatenate(wins, axis=1)
    owner = group_of_lane(grads.shape, groups)
    stacked = jnp.concatenate(
        [jnp.where(owner == g, grads, 0.0).astype(BF) for g in range(groups)], axis=0
    )
    lags = lax.dot_general(
        stacked, windows, (((1,), (1,)), ((), ())), preferred_element_type=F32
    )
    for g in range(groups):
        turned = pltpu.roll(lags[g * BLOCK : (g + 1) * BLOCK], 0, 1, stride=1, stride_axis=0)
        sums_ref[g : g + 1, :] = jnp.sum(turned[:, BLOCK:], axis=0, keepdims=True)


def backward_kernel(
    cotangent_ref, front_ref, rows_ref, taps_ref, lines_ref, mixed_ref,
    mix_ref, ahead_ref, next_ref, grad_ref, short_ref, scratch, padded, pulled, later, band,
):
    seqs, row_count = rows_ref.shape[0], rows_ref.shape[2]
    groups = lines_ref.shape[0]
    taps = taps_ref.shape[1]
    band_rows(lines_ref[...], band)
    for s in range(seqs):
        padded[s, 0:row_count, :] = mix_ref[s]
        padded[s, row_count : row_count + BLOCK, :] = ahead_ref[s]
    for b in range(row_count // BLOCK):
        wide = jnp.dot(
            band[...], window_pair(padded, b * BLOCK), preferred_element_type=F32
        )
        kept = own_group(wide, groups)
        for s in range(seqs):
            pulled[s, b * BLOCK : (b + 1) * BLOCK, :] = kept[:, s * LANES : (s + 1) * LANES]
    short_ref[...] = jnp.zeros_like(short_ref)
    for s in range(seqs):
        for stream in range(3):
            if stream == 0:
                grad = cotangent_ref[s].astype(F32) * mixed_ref[s]
            else:
                other = 3 - stream
                fill(scratch, front_ref[s, other], rows_ref[s, other])
                grad = pulled[s] * feature(scratch, taps_ref, other, row_count)
            grad = grad.astype(BF).astype(F32)
            fill(scratch, front_ref[s, stream], rows_ref[s, stream])
            later[0:row_count, :] = grad
            later[row_count : row_count + HALO, :] = next_ref[s, stream].astype(F32)
            total = None
            for offset in range(taps):
                term = taps_ref[stream, offset : offset + 1, :] * later[offset : offset + row_count, :]
                total = term if total is None else total + term
                at = HALO - offset
                row = stream * taps + offset
                short_ref[0, row : row + 1, :] += jnp.sum(
                    grad * scratch[at : at + row_count, :], axis=0, keepdims=True
                )
            grad_ref[s, stream] = total.astype(BF)


def reduce_kernel(x_ref, o_ref, zbuf, part, ybuf, whole, zs, zr, ys, yr, os, orr):
    pieces = x_ref.shape[0]
    me, core = lax.axis_index("ctx"), lax.axis_index("dp")
    line, place = me // pieces, me % pieces
    lines = lax.axis_size("ctx") // pieces
    peers = lines * 2
    mine = line * 2 + core

    def along(step):
        return {"ctx": line * pieces + (place + step) % pieces}

    def across(step):
        other = (mine + step) % peers
        return {"ctx": (other // 2) * pieces + place, "dp": other % 2}

    barrier = pltpu.get_barrier_semaphore()
    for step in range(1, pieces):
        pl.semaphore_signal(barrier, inc=1, device_id=along(step), device_id_type=MESH)
    for step in range(1, peers):
        pl.semaphore_signal(barrier, inc=1, device_id=across(step), device_id_type=MESH)
    pl.semaphore_wait(barrier, pieces + peers - 2)

    def first(step):
        return pltpu.make_async_remote_copy(
            src_ref=x_ref.at[(place + step) % pieces], dst_ref=zbuf.at[place],
            send_sem=zs.at[step], recv_sem=zr.at[step],
            device_id=along(step), device_id_type=MESH,
        )

    def second(step):
        return pltpu.make_async_remote_copy(
            src_ref=part, dst_ref=ybuf.at[mine], send_sem=ys.at[step], recv_sem=yr.at[step],
            device_id=across(step), device_id_type=MESH,
        )

    def third(step):
        return pltpu.make_async_remote_copy(
            src_ref=whole, dst_ref=o_ref.at[place], send_sem=os.at[step], recv_sem=orr.at[step],
            device_id=along(step), device_id_type=MESH,
        )

    for step in range(1, pieces):
        first(step).start()
    zbuf[place] = x_ref[place]
    for step in range(1, pieces):
        first(step).wait_recv()
    total = zbuf[0]
    for k in range(1, pieces):
        total = total + zbuf[k]
    part[...] = total
    for step in range(1, peers):
        second(step).start()
    ybuf[mine] = total
    for step in range(1, peers):
        second(step).wait_recv()
    total = ybuf[0]
    for k in range(1, peers):
        total = total + ybuf[k]
    whole[...] = total
    for step in range(1, pieces):
        third(step).start()
    o_ref[place] = total
    for step in range(1, pieces):
        third(step).wait_recv()
    for step in range(1, pieces):
        first(step).wait_send()
        third(step).wait_send()
    for step in range(1, peers):
        second(step).wait_send()


def tiled(kernel, ins, outs, scratch, arrays, tiles, flops=0):
    read = sum(math.prod(a.shape) * a.dtype.itemsize for a in arrays)
    return pl.pallas_call(
        kernel,
        grid=(tiles,),
        in_specs=[pl.BlockSpec(block, index) for block, index in ins],
        out_specs=[pl.BlockSpec(block, index) for block, index, _, _ in outs],
        out_shape=[jax.ShapeDtypeStruct(shape, kind) for _, _, shape, kind in outs],
        scratch_shapes=scratch,
        cost_estimate=pl.CostEstimate(flops=flops, bytes_accessed=read, transcendentals=0),
        compiler_params=pltpu.CompilerParams(vmem_limit_bytes=48 << 20),
    )(*arrays)


def shards(projected, short_w, medium_h, out_w, grad_out):
    seqs, row_count, _, chans = projected.shape
    taps = medium_h.shape[1]
    groups_here = medium_h.shape[0]
    tiles = chans // LANES
    groups = groups_here // tiles
    rows = jnp.swapaxes(projected, 1, 2)

    lines_behind = jnp.pad(medium_h[:, ::-1].astype(F32), ((0, 0), (1, 2 * BLOCK - taps - 1)))
    lines_ahead = jnp.pad(medium_h.astype(F32), ((0, 0), (0, 2 * BLOCK - taps)))

    lane3 = lambda i: (0, 0, i)
    lane4 = lambda i: (0, 0, 0, i)
    front_spec = ((seqs, 3, HALO, LANES), lane4)
    rows_spec = ((seqs, 3, row_count, LANES), lane4)
    taps_spec = ((3, short_w.shape[1], LANES), lane3)
    lines_spec = ((groups, 2 * BLOCK), lambda i: (i, 0))
    edge_spec = ((seqs, BLOCK, LANES), lane3)
    full_spec = ((seqs, row_count, LANES), lane3)
    full = (seqs, row_count, chans)
    line_rows = pltpu.VMEM((row_count + HALO, LANES), F32)
    long_rows = pltpu.VMEM((seqs, row_count + BLOCK, LANES), BF)
    bands = pltpu.VMEM((groups * BLOCK, 2 * BLOCK), BF)

    front = from_behind(rows[:, :, row_count - HALO :], "ctx", 1)
    tail = tiled(
        tail_kernel,
        [
            ((seqs, 3, HALO, LANES), lambda i: (0, 0, (row_count - BLOCK) // HALO - 1, i)),
            ((seqs, 3, BLOCK, LANES), lambda i: (0, 0, row_count // BLOCK - 1, i)),
            taps_spec,
        ],
        [(*edge_spec, (seqs, BLOCK, chans), BF)],
        [line_rows],
        (rows, rows, short_w),
        tiles,
    )[0]
    behind = from_behind(tail, "ctx", 1)
    gated, mixed, product = tiled(
        forward_kernel,
        [front_spec, rows_spec, taps_spec, lines_spec, edge_spec],
        [(*full_spec, full, BF), (*full_spec, full, F32), (*full_spec, full, BF)],
        [line_rows, long_rows, pltpu.VMEM((seqs, row_count, LANES), F32), bands],
        (front, rows, short_w, lines_behind, behind),
        tiles,
    )

    whole_w = lax.all_gather(out_w, "ctx", axis=0, tiled=True)
    whole_gated = lax.all_gather(gated, "grp", axis=2, tiled=True)
    flat_gated = whole_gated.reshape(seqs * row_count, whole_gated.shape[2])
    block_out = jnp.dot(flat_gated, whole_w, preferred_element_type=F32).astype(BF).reshape(full)
    input_part = lax.dot_general(
        grad_out.reshape(seqs * row_count, chans), whole_w, (((1,), (1,)), ((), ())), preferred_element_type=F32
    )
    summed = lax.psum_scatter(input_part, "grp", scatter_dimension=1, tiled=True)
    cotangent = summed.astype(BF).reshape(full)

    mix, head = tiled(
        mix_kernel,
        [full_spec, front_spec, rows_spec, taps_spec, lines_spec, full_spec],
        [(*full_spec, full, BF), (*front_spec, (seqs, 3, HALO, chans), BF)],
        [line_rows, bands],
        (cotangent, front, rows, short_w, lines_ahead, mixed),
        tiles,
    )
    ahead = from_behind(mix[:, :BLOCK], "ctx", -1)
    later = from_behind(head, "ctx", -1)
    filter_part = tiled(
        filter_kernel,
        [full_spec, full_spec, edge_spec],
        [((groups, LANES), lambda i: (i, 0), (groups_here, taps), F32)],
        [long_rows],
        (mix, product, behind),
        tiles,
    )[0]
    grad, short_part = tiled(
        backward_kernel,
        [full_spec, front_spec, rows_spec, taps_spec, lines_spec, full_spec, full_spec, edge_spec, front_spec],
        [(*rows_spec, rows.shape, BF), ((1, HALO, LANES), lambda i: (i, 0, 0), (tiles, HALO, LANES), F32)],
        [line_rows, long_rows, pltpu.VMEM((seqs, row_count, LANES), F32), line_rows, bands],
        (cotangent, front, rows, short_w, lines_ahead, mixed, mix, ahead, later),
        tiles,
    )

    pieces = 8
    packed = jnp.concatenate([filter_part, short_part.reshape(tiles * HALO, LANES)], axis=0)
    depth = packed.shape[0] // pieces
    piece = (depth, LANES)
    sums = pl.pallas_call(
        reduce_kernel,
        out_shape=jax.ShapeDtypeStruct((pieces, *piece), F32),
        in_specs=[pl.BlockSpec(memory_space=pltpu.VMEM)],
        out_specs=pl.BlockSpec(memory_space=pltpu.VMEM),
        scratch_shapes=[pltpu.VMEM((pieces, *piece), F32), pltpu.VMEM(piece, F32)] * 2
        + [pltpu.SemaphoreType.DMA((8,))] * 6,
        compiler_params=pltpu.CompilerParams(collective_id=1, has_side_effects=True),
    )(packed.reshape(pieces, *piece)).reshape(packed.shape)

    seq_total = seqs * lax.axis_size("dp")
    length_total = row_count * lax.axis_size("ctx")
    filter_grad = sums[:groups_here, ::-1] / math.sqrt(seq_total * length_total * (LANES // groups))
    streams = sums[groups_here:].reshape(tiles, HALO, LANES)[:, : 3 * short_w.shape[1]]
    short_sum = jnp.swapaxes(streams, 0, 1).reshape(3, short_w.shape[1], chans)
    short_grad = short_sum / math.sqrt(seq_total * length_total)
    return (block_out, jnp.swapaxes(grad, 1, 2), filter_grad, short_grad)


def solution(mesh):
    in_specs = (
        P("dp", "ctx", None, "grp"),
        P(None, None, "grp"),
        P("grp", None),
        P("ctx", "grp"),
        P("dp", "ctx", "grp"),
    )
    out_specs = (
        P("dp", "ctx", "grp"),
        P("dp", "ctx", None, "grp"),
        P("grp", None),
        P(None, None, "grp"),
    )
    return jax.shard_map(shards, mesh=mesh, in_specs=in_specs, out_specs=out_specs, check_vma=False)
```

```python
import functools
import math

import jax
import jax.numpy as jnp
from jax import lax
from jax.experimental import pallas as pl
from jax.experimental.pallas import tpu as pltpu
from jax.sharding import PartitionSpec as P

BF = jnp.bfloat16
F32 = jnp.float32
LANES = 128
BLOCK = 128
HALO = 16
MESH = pl.DeviceIdType.MESH
ALONG_Z = 8


def from_behind(block, axis, distance):
    devices = range(lax.axis_size(axis))
    route = [(i - distance, i) for i in devices if i - distance in devices]
    return lax.ppermute(block, axis, route)


def fill(scratch, front, rows):
    scratch[0:HALO, :] = front.astype(F32)
    scratch[HALO : HALO + rows.shape[0], :] = rows.astype(F32)


def feature(scratch, taps, stream, count):
    total = None
    for offset in range(taps.shape[1]):
        start = HALO - offset
        term = taps[stream, offset : offset + 1, :] * scratch[start : start + count, :]
        total = term if total is None else total + term
    return total


def band_rows(lines, band):
    groups = lines.shape[0]
    for g in range(groups):
        line = jnp.broadcast_to(lines[g : g + 1, :], (BLOCK, lines.shape[1]))
        turned = pltpu.roll(line, 0, 1, stride=1, stride_axis=0)
        band[g * BLOCK : (g + 1) * BLOCK, :] = turned.astype(BF)


def group_of_lane(shape, groups):
    lane = lax.broadcasted_iota(jnp.int32, shape, len(shape) - 1)
    return (lane % LANES) // (LANES // groups)


def own_group(wide, groups):
    owner = group_of_lane((BLOCK, wide.shape[1]), groups)
    kept = wide[0:BLOCK]
    for g in range(1, groups):
        kept = jnp.where(owner == g, wide[g * BLOCK : (g + 1) * BLOCK], kept)
    return kept


def window_pair(padded, start):
    return jnp.concatenate(
        [padded[s, start : start + 2 * BLOCK, :] for s in range(padded.shape[0])], axis=1
    )


def tail_kernel(front_ref, rows_ref, taps_ref, out_ref, scratch):
    for s in range(rows_ref.shape[0]):
        found = []
        for stream in (1, 2):
            fill(scratch, front_ref[s, stream], rows_ref[s, stream])
            found.append(feature(scratch, taps_ref, stream, BLOCK))
        out_ref[s] = (found[0] * found[1]).astype(BF)


def forward_kernel(
    front_ref, rows_ref, taps_ref, lines_ref, behind_ref,
    gated_ref, mixed_ref, product_ref, scratch, padded, queries, band,
):
    seqs, row_count = rows_ref.shape[0], rows_ref.shape[2]
    groups = lines_ref.shape[0]
    band_rows(lines_ref[...], band)
    for s in range(seqs):
        found = []
        for stream in range(3):
            fill(scratch, front_ref[s, stream], rows_ref[s, stream])
            found.append(feature(scratch, taps_ref, stream, row_count))
        queries[s] = found[0]
        product = (found[1] * found[2]).astype(BF)
        product_ref[s] = product
        padded[s, 0:BLOCK, :] = behind_ref[s]
        padded[s, BLOCK : BLOCK + row_count, :] = product
    for b in range(row_count // BLOCK):
        here = slice(b * BLOCK, (b + 1) * BLOCK)
        wide = jnp.dot(
            band[...], window_pair(padded, b * BLOCK), preferred_element_type=F32
        )
        kept = own_group(wide, groups)
        for s in range(seqs):
            mixed = kept[:, s * LANES : (s + 1) * LANES]
            mixed_ref[s, here, :] = mixed
            gated_ref[s, here, :] = (queries[s, here, :] * mixed).astype(BF)


def mix_kernel(
    cotangent_ref, front_ref, rows_ref, taps_ref, lines_ref, mixed_ref,
    mix_ref, head_ref, scratch, band,
):
    seqs, row_count = rows_ref.shape[0], rows_ref.shape[2]
    groups = lines_ref.shape[0]
    band_rows(lines_ref[...], band)
    for s in range(seqs):
        fill(scratch, front_ref[s, 0], rows_ref[s, 0])
        query = feature(scratch, taps_ref, 0, row_count)
        mix_ref[s] = (cotangent_ref[s].astype(F32) * query).astype(BF)
    wide = jnp.dot(band[...], window_pair(mix_ref, 0), preferred_element_type=F32)
    kept = own_group(wide, groups)
    for s in range(seqs):
        pulled = kept[0:HALO, s * LANES : (s + 1) * LANES]
        found = []
        for stream in (1, 2):
            fill(scratch, front_ref[s, stream], rows_ref[s, stream, 0:HALO])
            found.append(feature(scratch, taps_ref, stream, HALO))
        head_ref[s, 0] = (cotangent_ref[s, 0:HALO, :].astype(F32) * mixed_ref[s, 0:HALO, :]).astype(BF)
        head_ref[s, 1] = (pulled * found[1]).astype(BF)
        head_ref[s, 2] = (pulled * found[0]).astype(BF)


def filter_kernel(mix_ref, product_ref, behind_ref, sums_ref, padded):
    seqs, row_count = product_ref.shape[0], product_ref.shape[1]
    groups = sums_ref.shape[0]
    blocks = row_count // BLOCK
    for s in range(seqs):
        padded[s, 0:BLOCK, :] = behind_ref[s]
        padded[s, BLOCK : BLOCK + row_count, :] = product_ref[s]
    rows = lax.broadcasted_iota(jnp.int32, (BLOCK, BLOCK), 0)
    columns = lax.broadcasted_iota(jnp.int32, (BLOCK, BLOCK), 1)
    upturn = (rows + columns == BLOCK - 1).astype(BF)
    parts, wins = [], []
    for s in range(seqs):
        for b in range(blocks):
            parts.append(mix_ref[s, b * BLOCK : (b + 1) * BLOCK, :])
            wins.append(padded[s, b * BLOCK : (b + 2) * BLOCK, :])
    grads = jnp.dot(upturn, jnp.concatenate(parts, axis=1), preferred_element_type=F32)
    windows = jnp.concatenate(wins, axis=1)
    owner = group_of_lane(grads.shape, groups)
    stacked = jnp.concatenate(
        [jnp.where(owner == g, grads, 0.0).astype(BF) for g in range(groups)], axis=0
    )
    lags = lax.dot_general(
        stacked, windows, (((1,), (1,)), ((), ())), preferred_element_type=F32
    )
    for g in range(groups):
        turned = pltpu.roll(lags[g * BLOCK : (g + 1) * BLOCK], 0, 1, stride=1, stride_axis=0)
        sums_ref[g : g + 1, :] = jnp.sum(turned[:, BLOCK:], axis=0, keepdims=True)


def backward_kernel(
    cotangent_ref, front_ref, rows_ref, taps_ref, lines_ref, mixed_ref,
    mix_ref, ahead_ref, next_ref, grad_ref, short_ref, scratch, padded, pulled, later, band,
):
    seqs, row_count = rows_ref.shape[0], rows_ref.shape[2]
    groups = lines_ref.shape[0]
    taps = taps_ref.shape[1]
    band_rows(lines_ref[...], band)
    for s in range(seqs):
        padded[s, 0:row_count, :] = mix_ref[s]
        padded[s, row_count : row_count + BLOCK, :] = ahead_ref[s]
    for b in range(row_count // BLOCK):
        wide = jnp.dot(
            band[...], window_pair(padded, b * BLOCK), preferred_element_type=F32
        )
        kept = own_group(wide, groups)
        for s in range(seqs):
            pulled[s, b * BLOCK : (b + 1) * BLOCK, :] = kept[:, s * LANES : (s + 1) * LANES]
    short_ref[...] = jnp.zeros_like(short_ref)
    for s in range(seqs):
        for stream in range(3):
            if stream == 0:
                grad = cotangent_ref[s].astype(F32) * mixed_ref[s]
            else:
                other = 3 - stream
                fill(scratch, front_ref[s, other], rows_ref[s, other])
                grad = pulled[s] * feature(scratch, taps_ref, other, row_count)
            grad = grad.astype(BF).astype(F32)
            fill(scratch, front_ref[s, stream], rows_ref[s, stream])
            later[0:row_count, :] = grad
            later[row_count : row_count + HALO, :] = next_ref[s, stream].astype(F32)
            total = None
            for offset in range(taps):
                term = taps_ref[stream, offset : offset + 1, :] * later[offset : offset + row_count, :]
                total = term if total is None else total + term
                at = HALO - offset
                row = stream * taps + offset
                short_ref[0, row : row + 1, :] += jnp.sum(
                    grad * scratch[at : at + row_count, :], axis=0, keepdims=True
                )
            grad_ref[s, stream] = total.astype(BF)


def reduce_kernel(x_ref, o_ref, zbuf, part, ybuf, whole, zs, zr, ys, yr, os, orr):
    pieces = x_ref.shape[0]
    me, core = lax.axis_index("ctx"), lax.axis_index("dp")
    line, place = me // pieces, me % pieces
    lines = lax.axis_size("ctx") // pieces
    peers = lines * 2
    mine = line * 2 + core

    def along(step):
        return {"ctx": line * pieces + (place + step) % pieces}

    def across(step):
        other = (mine + step) % peers
        return {"ctx": (other // 2) * pieces + place, "dp": other % 2}

    barrier = pltpu.get_barrier_semaphore()
    for step in range(1, pieces):
        pl.semaphore_signal(barrier, inc=1, device_id=along(step), device_id_type=MESH)
    for step in range(1, peers):
        pl.semaphore_signal(barrier, inc=1, device_id=across(step), device_id_type=MESH)
    pl.semaphore_wait(barrier, pieces + peers - 2)

    def first(step):
        return pltpu.make_async_remote_copy(
            src_ref=x_ref.at[(place + step) % pieces], dst_ref=zbuf.at[place],
            send_sem=zs.at[step], recv_sem=zr.at[step],
            device_id=along(step), device_id_type=MESH,
        )

    def second(step):
        return pltpu.make_async_remote_copy(
            src_ref=part, dst_ref=ybuf.at[mine], send_sem=ys.at[step], recv_sem=yr.at[step],
            device_id=across(step), device_id_type=MESH,
        )

    def third(step):
        return pltpu.make_async_remote_copy(
            src_ref=whole, dst_ref=o_ref.at[place], send_sem=os.at[step], recv_sem=orr.at[step],
            device_id=along(step), device_id_type=MESH,
        )

    for step in range(1, pieces):
        first(step).start()
    zbuf[place] = x_ref[place]
    for step in range(1, pieces):
        first(step).wait_recv()
    total = zbuf[0]
    for k in range(1, pieces):
        total = total + zbuf[k]
    part[...] = total
    for step in range(1, peers):
        second(step).start()
    ybuf[mine] = total
    for step in range(1, peers):
        second(step).wait_recv()
    total = ybuf[0]
    for k in range(1, peers):
        total = total + ybuf[k]
    whole[...] = total
    for step in range(1, pieces):
        third(step).start()
    o_ref[place] = total
    for step in range(1, pieces):
        third(step).wait_recv()
    for step in range(1, pieces):
        first(step).wait_send()
        third(step).wait_send()
    for step in range(1, peers):
        second(step).wait_send()


def exchange_kernel(
    along_z, w_ref, gated_ref, cotangent_ref, out_ref, grad_ref,
    whole, gathered, to_a, to_b, from_a, from_b, to_right, to_left, from_left, from_right,
    kept_right, kept_left, own,
    z_send, z_recv, up_send, up_recv, down_send, down_recv, far_send, far_recv,
    pair_send, pair_recv, x_send, x_recv, sum_send, sum_recv,
):
    ctx, core, x = lax.axis_index("ctx"), lax.axis_index("dp"), lax.axis_index("grp")
    lines, ring = lax.axis_size("ctx") // along_z, lax.axis_size("grp")
    y, z = ctx // along_z, ctx % along_z
    part = w_ref.shape[0] // 2
    total, chans = gated_ref.shape
    half = total // 2

    def at_z(step):
        return {"ctx": y * along_z + (z + along_z + step) % along_z}

    def at_y(step):
        return {"ctx": (y + lines + step) % lines * along_z + z}

    def at_x(step):
        return {"grp": (x + ring + step) % ring}

    partner = {"dp": 1 - core}
    barrier = pltpu.get_barrier_semaphore()
    for device in (at_z(1), at_z(-1), at_y(1), at_y(-1), at_x(1), at_x(-1), partner):
        pl.semaphore_signal(barrier, inc=1, device_id=device, device_id_type=MESH)
    pl.semaphore_wait(barrier, 7)

    def copy(src, dst, send, recv, device):
        return pltpu.make_async_remote_copy(
            src_ref=src, dst_ref=dst, send_sem=send, recv_sem=recv, device_id=device, device_id_type=MESH
        )

    def block(step_y, step_z, carrier):
        row = ((y + lines + step_y) % lines * along_z + (z + along_z + step_z) % along_z) * 2 + carrier
        return whole.at[pl.ds(pl.multiple_of(row * part, part), part), :]

    steps = [0]
    for k in range(1, along_z // 2 + 1):
        steps += [-k, k] if 2 * k < along_z else [-k]
    started = []

    def go(*what):
        started.append(copy(*what))
        started[-1].start()

    def hand_over(kind, step_y, u):
        place = kind * along_z + u
        mine = block(step_y, steps[u], core)
        go(mine, mine, pair_send.at[place], pair_recv.at[place], partner)

    def y_turn(u):
        behind, ahead = block(-1, steps[u], core), block(1, steps[u], core)
        copy(behind, behind, up_send.at[u], up_recv.at[u], at_y(1)).wait_recv()
        if u % 2 == 0:
            go(behind, behind, far_send.at[u], far_recv.at[u], at_y(1))
        hand_over(1, -1, u)
        copy(ahead, ahead, down_send.at[u], down_recv.at[u], at_y(-1)).wait_recv()
        if u % 2 == 1:
            go(ahead, ahead, far_send.at[u], far_recv.at[u], at_y(-1))
        hand_over(2, 1, u)

    def far_turn(u):
        far = block(2, steps[u], core)
        copy(far, far, far_send.at[u], far_recv.at[u], at_y(1)).wait_recv()
        hand_over(3, 2, u)

    chunks = 4
    tall = total // chunks

    def rows_of(c):
        return pl.ds(c * tall, tall)

    def x_start(c):
        src = gated_ref.at[rows_of(c), :]
        go(src, gathered.at[0, rows_of(c), :], x_send.at[0, c], x_recv.at[0, c], at_x(1))
        go(src, gathered.at[1, rows_of(c), :], x_send.at[1, c], x_recv.at[1, c], at_x(-1))

    def x_wait(slot, c):
        here = gathered.at[slot, rows_of(c), :]
        copy(here, here, x_send.at[slot, c], x_recv.at[slot, c], at_x(1)).wait_recv()

    def x_turn(c):
        x_wait(0, c)
        x_wait(1, c)
        slot, to = (0, at_x(1)) if c < chunks // 2 else (1, at_x(-1))
        go(gathered.at[slot, rows_of(c), :], gathered.at[2, rows_of(c), :], x_send.at[2, c], x_recv.at[2, c], to)

    own_part = w_ref.at[pl.ds(pl.multiple_of(core * part, part), part), :]
    x_next = 0
    for c in range(chunks):
        x_start(c)
    for u in range(along_z):
        mine = own_part
        if u > 0:
            mine = block(0, steps[u], core)
            copy(mine, mine, z_send.at[u], z_recv.at[u], at_z(1)).wait_recv()
        for direction in (-1, 1):
            onward = steps[u] + direction
            if onward in steps and (u == 0 or steps[u] * direction > 0):
                v = steps.index(onward)
                go(mine, block(0, steps[u], core), z_send.at[v], z_recv.at[v], at_z(-direction))
        go(mine, block(0, steps[u], core), up_send.at[u], up_recv.at[u], at_y(1))
        go(mine, block(0, steps[u], core), down_send.at[u], down_recv.at[u], at_y(-1))
        if u > 0:
            hand_over(0, 0, u)
            y_turn(u - 1)
        if u > 1:
            far_turn(u - 2)
        if u % 2 == 1 and x_next < chunks:
            x_turn(x_next)
            x_next += 1
    whole[pl.ds(pl.multiple_of(ctx * 2 * part, 2 * part), 2 * part), :] = w_ref[...]
    y_turn(along_z - 1)
    for c in range(x_next, chunks):
        x_turn(c)
    for u in range(max(along_z - 2, 0), along_z):
        far_turn(u)
    for kind, step_y in enumerate((0, -1, 1, 2)):
        for u in range(along_z):
            if kind == 0 and u == 0:
                continue
            place = kind * along_z + u
            other = block(step_y, steps[u], 1 - core)
            copy(other, other, pair_send.at[place], pair_recv.at[place], partner).wait_recv()

    wide = min(chans, 256)
    right, left, across = (x + 1) % ring, (x + ring - 1) % ring, (x + 2) % ring

    def columns(j):
        return pl.ds(pl.multiple_of(j * wide, wide), wide)

    def partial(owner, j):
        rows = whole[pl.ds(pl.multiple_of(owner * chans + j * wide, wide), wide), :]
        return lax.dot_general(cotangent_ref[...], rows, (((1,), (1,)), ((), ())), preferred_element_type=F32)

    def far_sums(j, carry):
        found = partial(across, j)
        to_a[:, columns(j)] = found[:half].astype(BF)
        to_b[:, columns(j)] = found[half:].astype(BF)
        return carry

    def near_sums(j, carry):
        found = partial(right, j)
        kept_right[:, columns(j)] = found[:half]
        to_right[half:, columns(j)] = found[half:].astype(BF)
        found = partial(left, j)
        to_left[:half, columns(j)] = found[:half].astype(BF)
        kept_left[:, columns(j)] = found[half:]
        return carry

    def outputs(j, carry):
        own[:, columns(j)] = partial(x, j)
        found = None
        for slot, owner in ((None, x), (0, left), (1, right), (2, across)):
            rows = whole[pl.ds(pl.multiple_of(owner * chans, chans), chans), columns(j)]
            source = gated_ref[...] if slot is None else gathered[slot]
            term = jnp.dot(source, rows, preferred_element_type=F32)
            found = term if found is None else found + term
        out_ref[:, columns(j)] = found.astype(BF)
        return carry

    first, second = pl.ds(0, half), pl.ds(half, half)
    lax.fori_loop(0, chans // wide, far_sums, 0)
    go(to_a, from_a, sum_send.at[0], sum_recv.at[0], at_x(1))
    go(to_b, from_b, sum_send.at[1], sum_recv.at[1], at_x(-1))
    lax.fori_loop(0, chans // wide, near_sums, 0)
    go(to_right.at[second, :], from_left.at[second, :], sum_send.at[2], sum_recv.at[2], at_x(1))
    go(to_left.at[first, :], from_right.at[first, :], sum_send.at[3], sum_recv.at[3], at_x(-1))
    for c in range(chunks):
        x_wait(2, c)
    lax.fori_loop(0, chans // wide, outputs, 0)
    copy(to_a, from_a, sum_send.at[0], sum_recv.at[0], at_x(1)).wait_recv()
    to_right[:half, :] = (kept_right[...] + from_a[...].astype(F32)).astype(BF)
    go(to_right.at[first, :], from_left.at[first, :], sum_send.at[4], sum_recv.at[4], at_x(1))
    copy(to_b, from_b, sum_send.at[1], sum_recv.at[1], at_x(-1)).wait_recv()
    to_left[half:, :] = (kept_left[...] + from_b[...].astype(F32)).astype(BF)
    go(to_left.at[second, :], from_right.at[second, :], sum_send.at[5], sum_recv.at[5], at_x(-1))
    for ref, rows, n in ((from_left, second, 2), (from_right, first, 3), (from_left, first, 4), (from_right, second, 5)):
        here = ref.at[rows, :]
        copy(here, here, sum_send.at[n], sum_recv.at[n], at_x(1)).wait_recv()
    grad_ref[...] = (own[...] + (from_left[...].astype(F32) + from_right[...].astype(F32))).astype(BF)
    for sent in started:
        sent.wait_send()


def exchange(out_w, gated, grad_out):
    total, chans = gated.shape
    depth = out_w.shape[0] * lax.axis_size("ctx")
    half = (total // 2, chans)
    dma = pltpu.SemaphoreType.DMA
    flops = 4 * total * depth * chans
    return pl.pallas_call(
        functools.partial(exchange_kernel, ALONG_Z),
        out_shape=[jax.ShapeDtypeStruct(gated.shape, BF)] * 2,
        in_specs=[pl.BlockSpec(memory_space=pltpu.VMEM)] * 3,
        out_specs=[pl.BlockSpec(memory_space=pltpu.VMEM)] * 2,
        scratch_shapes=[pltpu.VMEM((depth, chans), BF), pltpu.VMEM((3, total, chans), BF)]
        + [pltpu.VMEM(half, BF)] * 4
        + [pltpu.VMEM(gated.shape, BF)] * 4
        + [pltpu.VMEM(half, F32)] * 2
        + [pltpu.VMEM(gated.shape, F32)]
        + [dma((ALONG_Z,))] * 8
        + [dma((4 * ALONG_Z,))] * 2
        + [dma((3, 4))] * 2
        + [dma((6,))] * 2,
        cost_estimate=pl.CostEstimate(flops=flops, bytes_accessed=8 * total * chans, transcendentals=0),
        compiler_params=pltpu.CompilerParams(
            collective_id=2, has_side_effects=True, vmem_limit_bytes=52 << 20
        ),
    )(out_w, gated, grad_out)


def tiled(kernel, ins, outs, scratch, arrays, tiles, flops=0):
    read = sum(math.prod(a.shape) * a.dtype.itemsize for a in arrays)
    return pl.pallas_call(
        kernel,
        grid=(tiles,),
        in_specs=[pl.BlockSpec(block, index) for block, index in ins],
        out_specs=[pl.BlockSpec(block, index) for block, index, _, _ in outs],
        out_shape=[jax.ShapeDtypeStruct(shape, kind) for _, _, shape, kind in outs],
        scratch_shapes=scratch,
        cost_estimate=pl.CostEstimate(flops=flops, bytes_accessed=read, transcendentals=0),
        compiler_params=pltpu.CompilerParams(vmem_limit_bytes=48 << 20),
    )(*arrays)


def shards(projected, short_w, medium_h, out_w, grad_out):
    seqs, row_count, _, chans = projected.shape
    taps = medium_h.shape[1]
    groups_here = medium_h.shape[0]
    tiles = chans // LANES
    groups = groups_here // tiles
    rows = jnp.swapaxes(projected, 1, 2)

    lines_behind = jnp.pad(medium_h[:, ::-1].astype(F32), ((0, 0), (1, 2 * BLOCK - taps - 1)))
    lines_ahead = jnp.pad(medium_h.astype(F32), ((0, 0), (0, 2 * BLOCK - taps)))

    lane3 = lambda i: (0, 0, i)
    lane4 = lambda i: (0, 0, 0, i)
    front_spec = ((seqs, 3, HALO, LANES), lane4)
    rows_spec = ((seqs, 3, row_count, LANES), lane4)
    taps_spec = ((3, short_w.shape[1], LANES), lane3)
    lines_spec = ((groups, 2 * BLOCK), lambda i: (i, 0))
    edge_spec = ((seqs, BLOCK, LANES), lane3)
    full_spec = ((seqs, row_count, LANES), lane3)
    full = (seqs, row_count, chans)
    line_rows = pltpu.VMEM((row_count + HALO, LANES), F32)
    long_rows = pltpu.VMEM((seqs, row_count + BLOCK, LANES), BF)
    bands = pltpu.VMEM((groups * BLOCK, 2 * BLOCK), BF)

    front = from_behind(rows[:, :, row_count - HALO :], "ctx", 1)
    tail = tiled(
        tail_kernel,
        [
            ((seqs, 3, HALO, LANES), lambda i: (0, 0, (row_count - BLOCK) // HALO - 1, i)),
            ((seqs, 3, BLOCK, LANES), lambda i: (0, 0, row_count // BLOCK - 1, i)),
            taps_spec,
        ],
        [(*edge_spec, (seqs, BLOCK, chans), BF)],
        [line_rows],
        (rows, rows, short_w),
        tiles,
    )[0]
    behind = from_behind(tail, "ctx", 1)
    gated, mixed, product = tiled(
        forward_kernel,
        [front_spec, rows_spec, taps_spec, lines_spec, edge_spec],
        [(*full_spec, full, BF), (*full_spec, full, F32), (*full_spec, full, BF)],
        [line_rows, long_rows, pltpu.VMEM((seqs, row_count, LANES), F32), bands],
        (front, rows, short_w, lines_behind, behind),
        tiles,
    )

    flat = (seqs * row_count, chans)
    block_out, cotangent = exchange(out_w, gated.reshape(flat), grad_out.reshape(flat))
    block_out, cotangent = block_out.reshape(full), cotangent.reshape(full)

    mix, head = tiled(
        mix_kernel,
        [full_spec, front_spec, rows_spec, taps_spec, lines_spec, full_spec],
        [(*full_spec, full, BF), (*front_spec, (seqs, 3, HALO, chans), BF)],
        [line_rows, bands],
        (cotangent, front, rows, short_w, lines_ahead, mixed),
        tiles,
    )
    ahead = from_behind(mix[:, :BLOCK], "ctx", -1)
    later = from_behind(head, "ctx", -1)
    filter_part = tiled(
        filter_kernel,
        [full_spec, full_spec, edge_spec],
        [((groups, LANES), lambda i: (i, 0), (groups_here, taps), F32)],
        [long_rows],
        (mix, product, behind),
        tiles,
    )[0]
    grad, short_part = tiled(
        backward_kernel,
        [full_spec, front_spec, rows_spec, taps_spec, lines_spec, full_spec, full_spec, edge_spec, front_spec],
        [(*rows_spec, rows.shape, BF), ((1, HALO, LANES), lambda i: (i, 0, 0), (tiles, HALO, LANES), F32)],
        [line_rows, long_rows, pltpu.VMEM((seqs, row_count, LANES), F32), line_rows, bands],
        (cotangent, front, rows, short_w, lines_ahead, mixed, mix, ahead, later),
        tiles,
    )

    pieces = ALONG_Z
    packed = jnp.concatenate([filter_part, short_part.reshape(tiles * HALO, LANES)], axis=0)
    depth = packed.shape[0] // pieces
    piece = (depth, LANES)
    peers = 2 * (lax.axis_size("ctx") // pieces)
    sums = pl.pallas_call(
        reduce_kernel,
        out_shape=jax.ShapeDtypeStruct((pieces, *piece), F32),
        in_specs=[pl.BlockSpec(memory_space=pltpu.VMEM)],
        out_specs=pl.BlockSpec(memory_space=pltpu.VMEM),
        scratch_shapes=[
            pltpu.VMEM((pieces, *piece), F32), pltpu.VMEM(piece, F32),
            pltpu.VMEM((peers, *piece), F32), pltpu.VMEM(piece, F32),
        ]
        + [pltpu.SemaphoreType.DMA((8,))] * 6,
        compiler_params=pltpu.CompilerParams(collective_id=1, has_side_effects=True),
    )(packed.reshape(pieces, *piece)).reshape(packed.shape)

    seq_total = seqs * lax.axis_size("dp")
    length_total = row_count * lax.axis_size("ctx")
    filter_grad = sums[:groups_here, ::-1] / math.sqrt(seq_total * length_total * (LANES // groups))
    streams = sums[groups_here:].reshape(tiles, HALO, LANES)[:, : 3 * short_w.shape[1]]
    short_sum = jnp.swapaxes(streams, 0, 1).reshape(3, short_w.shape[1], chans)
    short_grad = short_sum / math.sqrt(seq_total * length_total)
    return (block_out, jnp.swapaxes(grad, 1, 2), filter_grad, short_grad)


def solution(mesh):
    in_specs = (
        P("dp", "ctx", None, "grp"),
        P(None, None, "grp"),
        P("grp", None),
        P("ctx", "grp"),
        P("dp", "ctx", "grp"),
    )
    out_specs = (
        P("dp", "ctx", "grp"),
        P("dp", "ctx", None, "grp"),
        P("grp", None),
        P(None, None, "grp"),
    )
    return jax.shard_map(shards, mesh=mesh, in_specs=in_specs, out_specs=out_specs, check_vma=False)
```

```python
import functools
import math

import jax
import jax.numpy as jnp
from jax import lax
from jax.experimental import pallas as pl
from jax.experimental.pallas import tpu as pltpu
from jax.sharding import PartitionSpec as P

BF = jnp.bfloat16
F32 = jnp.float32
LANES = 128
BLOCK = 128
HALO = 16
MESH = pl.DeviceIdType.MESH
ALONG_Z = 8


def fill(scratch, front, rows):
    scratch[0:HALO, :] = front.astype(F32)
    scratch[HALO : HALO + rows.shape[0], :] = rows.astype(F32)


def feature(scratch, taps, stream, count):
    total = None
    for offset in range(taps.shape[1]):
        start = HALO - offset
        term = taps[stream, offset : offset + 1, :] * scratch[start : start + count, :]
        total = term if total is None else total + term
    return total


def band_rows(lines, band, count=BLOCK):
    groups = lines.shape[0]
    for g in range(groups):
        line = jnp.broadcast_to(lines[g : g + 1, :], (count, lines.shape[1]))
        turned = pltpu.roll(line, 0, 1, stride=1, stride_axis=0)
        band[g * count : (g + 1) * count, :] = turned.astype(BF)


def group_of_lane(shape, groups):
    lane = lax.broadcasted_iota(jnp.int32, shape, len(shape) - 1)
    return (lane % LANES) // (LANES // groups)


def own_group(wide, groups, count=BLOCK):
    owner = group_of_lane((count, wide.shape[1]), groups)
    kept = wide[0:count]
    for g in range(1, groups):
        kept = jnp.where(owner == g, wide[g * count : (g + 1) * count], kept)
    return kept


def window_pair(padded, start, lanes=slice(None)):
    return jnp.concatenate(
        [padded[s, start : start + 2 * BLOCK, lanes] for s in range(padded.shape[0])], axis=1
    )


def tail_kernel(front_ref, rows_ref, taps_ref, out_ref, scratch):
    for s in range(rows_ref.shape[0]):
        found = []
        for stream in (1, 2):
            fill(scratch, front_ref[s, stream], rows_ref[s, stream])
            found.append(feature(scratch, taps_ref, stream, BLOCK))
        out_ref[s] = (found[0] * found[1]).astype(BF)


def filter_kernel(mix_ref, padded_ref, sums_ref):
    seqs, row_count = padded_ref.shape[0], padded_ref.shape[1] - BLOCK
    groups = sums_ref.shape[0]
    blocks = row_count // BLOCK
    rows = lax.broadcasted_iota(jnp.int32, (BLOCK, BLOCK), 0)
    columns = lax.broadcasted_iota(jnp.int32, (BLOCK, BLOCK), 1)
    upturn = (rows + columns == BLOCK - 1).astype(BF)
    parts, wins = [], []
    for s in range(seqs):
        for b in range(blocks):
            parts.append(mix_ref[s, b * BLOCK : (b + 1) * BLOCK, :])
            wins.append(padded_ref[s, b * BLOCK : (b + 2) * BLOCK, :])
    grads = jnp.dot(upturn, jnp.concatenate(parts, axis=1), preferred_element_type=F32)
    windows = jnp.concatenate(wins, axis=1)
    owner = group_of_lane(grads.shape, groups)
    stacked = jnp.concatenate(
        [jnp.where(owner == g, grads, 0.0).astype(BF) for g in range(groups)], axis=0
    )
    lags = lax.dot_general(
        stacked, windows, (((1,), (1,)), ((), ())), preferred_element_type=F32
    )
    for g in range(groups):
        turned = pltpu.roll(lags[g * BLOCK : (g + 1) * BLOCK], 0, 1, stride=1, stride_axis=0)
        sums_ref[g : g + 1, :] = jnp.sum(turned[:, BLOCK:], axis=0, keepdims=True)


def backward_kernel(
    cotangent_ref, front_ref, rows_ref, taps_ref, lines_ref, mixed_ref,
    padded_ref, next_ref, grad_ref, short_ref, scratch, pulled, later, band,
):
    seqs, row_count = rows_ref.shape[0], rows_ref.shape[2]
    groups = lines_ref.shape[0]
    taps = taps_ref.shape[1]
    band_rows(lines_ref[...], band)
    for b in range(row_count // BLOCK):
        wide = jnp.dot(
            band[...], window_pair(padded_ref, b * BLOCK), preferred_element_type=F32
        )
        kept = own_group(wide, groups)
        for s in range(seqs):
            pulled[s, b * BLOCK : (b + 1) * BLOCK, :] = kept[:, s * LANES : (s + 1) * LANES]
    short_ref[...] = jnp.zeros_like(short_ref)
    for s in range(seqs):
        for stream in range(3):
            if stream == 0:
                grad = cotangent_ref[s].astype(F32) * mixed_ref[s]
            else:
                other = 3 - stream
                fill(scratch, front_ref[s, other], rows_ref[s, other])
                grad = pulled[s] * feature(scratch, taps_ref, other, row_count)
            grad = grad.astype(BF).astype(F32)
            fill(scratch, front_ref[s, stream], rows_ref[s, stream])
            later[0:row_count, :] = grad
            later[row_count : row_count + HALO, :] = next_ref[s, stream].astype(F32)
            total = None
            for offset in range(taps):
                term = taps_ref[stream, offset : offset + 1, :] * later[offset : offset + row_count, :]
                total = term if total is None else total + term
                at = HALO - offset
                row = stream * taps + offset
                short_ref[0, row : row + 1, :] += jnp.sum(
                    grad * scratch[at : at + row_count, :], axis=0, keepdims=True
                )
            grad_ref[s, stream] = total.astype(BF)


def reduce_kernel(x_ref, o_ref, zbuf, part, ybuf, whole, zs, zr, ys, yr, os, orr):
    pieces = x_ref.shape[0]
    me, core = lax.axis_index("ctx"), lax.axis_index("dp")
    line, place = me // pieces, me % pieces
    lines = lax.axis_size("ctx") // pieces
    peers = lines * 2
    mine = line * 2 + core

    def along(step):
        return {"ctx": line * pieces + (place + step) % pieces}

    def across(step):
        other = (mine + step) % peers
        return {"ctx": (other // 2) * pieces + place, "dp": other % 2}

    barrier = pltpu.get_barrier_semaphore()
    for step in range(1, pieces):
        pl.semaphore_signal(barrier, inc=1, device_id=along(step), device_id_type=MESH)
    for step in range(1, peers):
        pl.semaphore_signal(barrier, inc=1, device_id=across(step), device_id_type=MESH)
    pl.semaphore_wait(barrier, pieces + peers - 2)

    def first(step):
        return pltpu.make_async_remote_copy(
            src_ref=x_ref.at[(place + step) % pieces], dst_ref=zbuf.at[place],
            send_sem=zs.at[step], recv_sem=zr.at[step],
            device_id=along(step), device_id_type=MESH,
        )

    def second(step):
        return pltpu.make_async_remote_copy(
            src_ref=part, dst_ref=ybuf.at[mine], send_sem=ys.at[step], recv_sem=yr.at[step],
            device_id=across(step), device_id_type=MESH,
        )

    def third(step):
        return pltpu.make_async_remote_copy(
            src_ref=whole, dst_ref=o_ref.at[place], send_sem=os.at[step], recv_sem=orr.at[step],
            device_id=along(step), device_id_type=MESH,
        )

    for step in range(1, pieces):
        first(step).start()
    zbuf[place] = x_ref[place]
    for step in range(1, pieces):
        first(step).wait_recv()
    total = zbuf[0]
    for k in range(1, pieces):
        total = total + zbuf[k]
    part[...] = total
    for step in range(1, peers):
        second(step).start()
    ybuf[mine] = total
    for step in range(1, peers):
        second(step).wait_recv()
    total = ybuf[0]
    for k in range(1, peers):
        total = total + ybuf[k]
    whole[...] = total
    for step in range(1, pieces):
        third(step).start()
    o_ref[place] = total
    for step in range(1, pieces):
        third(step).wait_recv()
    for step in range(1, pieces):
        first(step).wait_send()
        third(step).wait_send()
    for step in range(1, peers):
        second(step).wait_send()


def exchange_kernel(
    along_z, w_ref, rows_ref, taps_ref, behind_ref, ahead_ref, tail_ref, cotangent_ref,
    out_ref, grad_ref, mixed_ref, product_ref, mix_ref, front_ref, later_ref,
    whole, gated, gathered, turned, queries, to_a, to_b, from_a, from_b,
    to_right, to_left, from_left, from_right, kept_right, kept_left, own, head,
    scratch, band, low_band,
    z_send, z_recv, up_send, up_recv, down_send, down_recv, far_send, far_recv,
    pair_send, pair_recv, x_send, x_recv, sum_send, sum_recv, halo_send, halo_recv,
):
    ctx, core, x = lax.axis_index("ctx"), lax.axis_index("dp"), lax.axis_index("grp")
    size, ring = lax.axis_size("ctx"), lax.axis_size("grp")
    lines = size // along_z
    y, z = ctx // along_z, ctx % along_z
    part = w_ref.shape[0] // 2
    total, chans = gated.shape
    half = total // 2
    seqs, row_count = rows_ref.shape[0], rows_ref.shape[2]
    tiles = chans // LANES
    groups = behind_ref.shape[0] // tiles

    def at_z(step):
        return {"ctx": y * along_z + (z + along_z + step) % along_z}

    def at_y(step):
        return {"ctx": (y + lines + step) % lines * along_z + z}

    def at_x(step):
        return {"grp": (x + ring + step) % ring}

    def at_ctx(step):
        return {"ctx": (ctx + size + step) % size}

    partner = {"dp": 1 - core}
    barrier = pltpu.get_barrier_semaphore()
    greeted = (at_z(1), at_z(-1), at_y(1), at_y(-1), at_x(1), at_x(-1), at_ctx(1), at_ctx(-1), partner)
    for device in greeted:
        pl.semaphore_signal(barrier, inc=1, device_id=device, device_id_type=MESH)
    pl.semaphore_wait(barrier, len(greeted))

    def copy(src, dst, send, recv, device):
        return pltpu.make_async_remote_copy(
            src_ref=src, dst_ref=dst, send_sem=send, recv_sem=recv, device_id=device, device_id_type=MESH
        )

    started = []

    def go(*what):
        started.append(copy(*what))
        started[-1].start()

    def arrive(here, send, recv, device):
        copy(here, here, send, recv, device).wait_recv()

    def halo(n, src, dst, device):
        go(src, dst, halo_send.at[n], halo_recv.at[n], device)

    def halo_wait(n, here, device, edge):
        arrive(here, halo_send.at[n], halo_recv.at[n], device)

        @pl.when(ctx == edge)
        def _():
            here[...] = jnp.zeros(here.shape, here.dtype)

    def lanes_of(i):
        return pl.ds(pl.multiple_of(i * LANES, LANES), LANES)

    def lines_of(ref, i):
        return ref[pl.ds(pl.multiple_of(i * groups, groups), groups), :]

    def block(step_y, step_z, carrier):
        row = ((y + lines + step_y) % lines * along_z + (z + along_z + step_z) % along_z) * 2 + carrier
        return whole.at[pl.ds(pl.multiple_of(row * part, part), part), :]

    steps = [0]
    for k in range(1, along_z // 2 + 1):
        steps += [-k, k] if 2 * k < along_z else [-k]

    def hand_over(kind, step_y, u):
        place = kind * along_z + u
        mine = block(step_y, steps[u], core)
        go(mine, mine, pair_send.at[place], pair_recv.at[place], partner)

    def z_turn(u):
        mine = w_ref.at[pl.ds(pl.multiple_of(core * part, part), part), :]
        if u > 0:
            mine = block(0, steps[u], core)
            arrive(mine, z_send.at[u], z_recv.at[u], at_z(1))
        for direction in (-1, 1):
            onward = steps[u] + direction
            if onward in steps and (u == 0 or steps[u] * direction > 0):
                v = steps.index(onward)
                go(mine, block(0, steps[u], core), z_send.at[v], z_recv.at[v], at_z(-direction))
        go(mine, block(0, steps[u], core), up_send.at[u], up_recv.at[u], at_y(1))
        go(mine, block(0, steps[u], core), down_send.at[u], down_recv.at[u], at_y(-1))
        if u > 0:
            hand_over(0, 0, u)

    def y_turn(u):
        behind, ahead = block(-1, steps[u], core), block(1, steps[u], core)
        arrive(behind, up_send.at[u], up_recv.at[u], at_y(1))
        if u % 2 == 0:
            go(behind, behind, far_send.at[u], far_recv.at[u], at_y(1))
        hand_over(1, -1, u)
        arrive(ahead, down_send.at[u], down_recv.at[u], at_y(-1))
        if u % 2 == 1:
            go(ahead, ahead, far_send.at[u], far_recv.at[u], at_y(-1))
        hand_over(2, 1, u)

    def far_turn(u):
        arrive(block(2, steps[u], core), far_send.at[u], far_recv.at[u], at_y(1))
        hand_over(3, 2, u)

    pieces = [(b, s) for b in (1, 0) for s in range(seqs)]

    def flat_rows(b, s):
        return pl.ds((b * seqs + s) * BLOCK, BLOCK)

    def x_start(c):
        here = flat_rows(*pieces[c])
        src = gated.at[here, :]
        go(src, gathered.at[0, here, :], x_send.at[0, c], x_recv.at[0, c], at_x(1))
        go(src, gathered.at[1, here, :], x_send.at[1, c], x_recv.at[1, c], at_x(-1))

    def x_wait(slot, c):
        arrive(gathered.at[slot, flat_rows(*pieces[c]), :], x_send.at[slot, c], x_recv.at[slot, c], at_x(1))

    def x_turn(c):
        x_wait(0, c)
        x_wait(1, c)
        here = flat_rows(*pieces[c])
        slot, to = (0, at_x(1)) if c < len(pieces) // 2 else (1, at_x(-1))
        go(gathered.at[slot, here, :], gathered.at[2, here, :], x_send.at[2, c], x_recv.at[2, c], to)

    def mix_block(i, b):
        wide = jnp.dot(band[i], window_pair(product_ref, b * BLOCK, lanes_of(i)), preferred_element_type=F32)
        kept = own_group(wide, groups)
        for s in range(seqs):
            mixed = kept[:, s * LANES : (s + 1) * LANES]
            here = slice(b * BLOCK, (b + 1) * BLOCK)
            mixed_ref[s, here, lanes_of(i)] = mixed
            gated[flat_rows(b, s), lanes_of(i)] = (queries[s, here, lanes_of(i)] * mixed).astype(BF)

    def taps_of(i):
        return taps_ref[:, :, lanes_of(i)]

    def features_of(i, s, streams, count):
        found = []
        for stream in streams:
            fill(scratch, front_ref[s, stream, :, lanes_of(i)], rows_ref[s, stream, 0:count, lanes_of(i)])
            taps, sum_ = taps_of(i), None
            for offset in range(taps.shape[1]):
                start = HALO - offset
                term = taps[stream, offset : offset + 1, :] * scratch[start : start + count, :]
                sum_ = term if sum_ is None else sum_ + term
            found.append(sum_)
        return found

    def forward(i, carry):
        for s in range(seqs):
            query, key, value = features_of(i, s, range(3), row_count)
            queries[s, :, lanes_of(i)] = query
            product_ref[s, BLOCK:, lanes_of(i)] = (key * value).astype(BF)
        band_rows(lines_of(behind_ref, i), band.at[i])
        mix_block(i, 1)
        return carry

    def forward_first(i, carry):
        mix_block(i, 0)
        return carry

    halo(0, rows_ref.at[:, :, row_count - HALO :, :], front_ref, at_ctx(1))
    z_turn(0)
    halo(1, tail_ref, product_ref.at[:, 0:BLOCK, :], at_ctx(1))
    for b in range(row_count // BLOCK):
        for s in range(seqs):
            turned[flat_rows(b, s), :] = cotangent_ref[s, b * BLOCK : (b + 1) * BLOCK, :]
    for u in range(1, min(3, along_z)):
        z_turn(u)
    halo_wait(0, front_ref, at_ctx(1), 0)
    lax.fori_loop(0, tiles, forward, 0)
    x_start(0)
    x_start(1)
    whole[pl.ds(pl.multiple_of(ctx * 2 * part, 2 * part), 2 * part), :] = w_ref[...]

    def second_half():
        halo_wait(1, product_ref.at[:, 0:BLOCK, :], at_ctx(1), 0)
        lax.fori_loop(0, tiles, forward_first, 0)
        x_start(2)
        x_start(3)

    plan = []
    for u in range(along_z + 2):
        if 3 <= u < along_z:
            plan.append((z_turn, u))
        if 0 <= u - 1 < along_z and u > 0:
            plan.append((y_turn, u - 1))
        if 0 <= u - 2 < along_z and u > 1:
            plan.append((far_turn, u - 2))
        if u == min(4, along_z):
            plan.append((second_half,))
        if u == min(5, along_z + 1):
            plan.append((x_turn, 0))
        if u == min(7, along_z + 1):
            plan.append((x_turn, 1))
        if u == along_z:
            plan.append((x_turn, 2))
    plan.append((x_turn, 3))
    if along_z < 8:
        plan = [p for p in plan if p[0] is not x_turn] + [(x_turn, c) for c in range(4)]
    for what, *which in plan:
        what(*which)
    for kind, step_y in enumerate((0, -1, 1, 2)):
        for u in range(1 if kind == 0 else 0, along_z):
            place = kind * along_z + u
            arrive(block(step_y, steps[u], 1 - core), pair_send.at[place], pair_recv.at[place], partner)

    wide = min(chans, 256)
    right, left, across = (x + 1) % ring, (x + ring - 1) % ring, (x + 2) % ring
    count = chans // wide

    def columns(j):
        return pl.ds(pl.multiple_of(j * wide, wide), wide)

    def partial(owner, j):
        rows = whole[pl.ds(pl.multiple_of(owner * chans + j * wide, wide), wide), :]
        return lax.dot_general(turned[...], rows, (((1,), (1,)), ((), ())), preferred_element_type=F32)

    def far_sums(j, carry):
        found = partial(across, j)
        to_a[:, columns(j)] = found[:half].astype(BF)
        to_b[:, columns(j)] = found[half:].astype(BF)
        return carry

    def near_sums(j, carry):
        found = partial(left, j)
        to_left[:half, columns(j)] = found[:half].astype(BF)
        kept_left[:, columns(j)] = found[half:]
        found = partial(right, j)
        kept_right[:, columns(j)] = found[:half]
        to_right[half:, columns(j)] = found[half:].astype(BF)
        return carry

    def own_sums(j, carry):
        own[:, columns(j)] = partial(x, j)
        return carry

    def outputs(j, carry):
        found = None
        for slot, owner in ((None, x), (0, left), (1, right), (2, across)):
            rows = whole[pl.ds(pl.multiple_of(owner * chans, chans), chans), columns(j)]
            source = gated[...] if slot is None else gathered[slot]
            term = jnp.dot(source, rows, preferred_element_type=F32)
            found = term if found is None else found + term
        for b in range(row_count // BLOCK):
            for s in range(seqs):
                at = (b * seqs + s) * BLOCK
                out_ref[s, b * BLOCK : (b + 1) * BLOCK, columns(j)] = found[at : at + BLOCK].astype(BF)
        return carry

    def piece(ref, at, n):
        return ref.at[pl.ds(at + n * BLOCK, BLOCK), :]

    def send_sum(n, src, dst, device):
        go(src, dst, sum_send.at[n], sum_recv.at[n], device)

    def wait_sum(n, here):
        arrive(here, sum_send.at[n], sum_recv.at[n], at_x(1))

    def relay_a(n):
        wait_sum(n, piece(from_a, 0, n))
        rows = slice(n * BLOCK, (n + 1) * BLOCK)
        to_right[rows, :] = (kept_right[rows, :] + from_a[rows, :].astype(F32)).astype(BF)
        send_sum(4 + n, piece(to_right, 0, n), piece(from_left, 0, n), at_x(1))

    def relay_b(n):
        wait_sum(2 + n, piece(from_b, 0, n))
        rows, there = slice(n * BLOCK, (n + 1) * BLOCK), slice(half + n * BLOCK, half + (n + 1) * BLOCK)
        to_left[there, :] = (kept_left[rows, :] + from_b[rows, :].astype(F32)).astype(BF)
        send_sum(6 + n, piece(to_left, half, n), piece(from_right, half, n), at_x(-1))

    first, second = pl.ds(0, half), pl.ds(half, half)
    lax.fori_loop(0, count, far_sums, 0)
    for n in range(2):
        send_sum(n, piece(to_a, 0, n), piece(from_a, 0, n), at_x(1))
        send_sum(2 + n, piece(to_b, 0, n), piece(from_b, 0, n), at_x(-1))
    lax.fori_loop(0, count, near_sums, 0)
    send_sum(8, to_left.at[first, :], from_right.at[first, :], at_x(-1))
    relay_a(0)
    lax.fori_loop(0, count, own_sums, 0)
    relay_a(1)
    send_sum(9, to_right.at[second, :], from_left.at[second, :], at_x(1))
    relay_b(0)
    relay_b(1)
    for c in range(len(pieces)):
        x_wait(2, c)
    lax.fori_loop(0, count, outputs, 0)

    def finish(b):
        for s in range(seqs):
            at = slice((b * seqs + s) * BLOCK, (b * seqs + s + 1) * BLOCK)
            here = slice(b * BLOCK, (b + 1) * BLOCK)
            found = own[at, :] + (from_left[at, :].astype(F32) + from_right[at, :].astype(F32))
            found = found.astype(BF)
            grad_ref[s, here, :] = found
            mix_ref[s, here, :] = (found.astype(F32) * queries[s, here, :]).astype(BF)

    wait_sum(8, from_right.at[first, :])
    for n in range(2):
        wait_sum(4 + n, piece(from_left, 0, n))
    finish(0)
    halo(2, mix_ref.at[:, 0:BLOCK, :], mix_ref.at[:, row_count:, :], at_ctx(-1))
    wait_sum(9, from_left.at[second, :])
    for n in range(2):
        wait_sum(6 + n, piece(from_right, half, n))
    finish(1)

    def heads(i, carry):
        band_rows(lines_of(ahead_ref, i), low_band, HALO)
        low = jnp.dot(low_band[...], window_pair(mix_ref, 0, lanes_of(i)), preferred_element_type=F32)
        pulled = own_group(low, groups, HALO)
        for s in range(seqs):
            here = pulled[:, s * LANES : (s + 1) * LANES]
            key, value = features_of(i, s, (1, 2), HALO)
            grad = grad_ref[s, 0:HALO, lanes_of(i)].astype(F32)
            head[s, 0, :, lanes_of(i)] = (grad * mixed_ref[s, 0:HALO, lanes_of(i)]).astype(BF)
            head[s, 1, :, lanes_of(i)] = (here * value).astype(BF)
            head[s, 2, :, lanes_of(i)] = (here * key).astype(BF)
        return carry

    lax.fori_loop(0, tiles, heads, 0)
    halo(3, head, later_ref, at_ctx(-1))
    halo_wait(2, mix_ref.at[:, row_count:, :], at_ctx(-1), size - 1)
    halo_wait(3, later_ref, at_ctx(-1), size - 1)
    for sent in started:
        sent.wait_send()


def exchange(out_w, rows, short_w, lines_behind, lines_ahead, tail, grad_out):
    seqs, row_count, chans = grad_out.shape
    total = seqs * row_count
    depth = out_w.shape[0] * lax.axis_size("ctx")
    tiles = chans // LANES
    groups = lines_behind.shape[0] // tiles
    half = (total // 2, chans)
    dma = pltpu.SemaphoreType.DMA
    flops = 4 * total * depth * chans
    padded = (seqs, row_count + BLOCK, chans)
    edge = (seqs, 3, HALO, chans)
    shape = jax.ShapeDtypeStruct
    return pl.pallas_call(
        functools.partial(exchange_kernel, ALONG_Z),
        out_shape=[
            shape(grad_out.shape, BF), shape(grad_out.shape, BF), shape(grad_out.shape, F32),
            shape(padded, BF), shape(padded, BF), shape(edge, BF), shape(edge, BF),
        ],
        in_specs=[pl.BlockSpec(memory_space=pltpu.VMEM)] * 7,
        out_specs=[pl.BlockSpec(memory_space=pltpu.VMEM)] * 7,
        scratch_shapes=[
            pltpu.VMEM((depth, chans), BF),
            pltpu.VMEM((total, chans), BF),
            pltpu.VMEM((3, total, chans), BF),
            pltpu.VMEM((total, chans), BF),
            pltpu.VMEM((seqs, row_count, chans), F32),
        ]
        + [pltpu.VMEM(half, BF)] * 4
        + [pltpu.VMEM((total, chans), BF)] * 4
        + [pltpu.VMEM(half, F32)] * 2
        + [
            pltpu.VMEM((total, chans), F32),
            pltpu.VMEM(edge, BF),
            pltpu.VMEM((row_count + HALO, LANES), F32),
            pltpu.VMEM((tiles, groups * BLOCK, 2 * BLOCK), BF),
            pltpu.VMEM((groups * HALO, 2 * BLOCK), BF),
        ]
        + [dma((ALONG_Z,))] * 8
        + [dma((4 * ALONG_Z,))] * 2
        + [dma((3, 4))] * 2
        + [dma((10,))] * 2
        + [dma((4,))] * 2,
        cost_estimate=pl.CostEstimate(flops=flops, bytes_accessed=8 * total * chans, transcendentals=0),
        compiler_params=pltpu.CompilerParams(
            collective_id=2, has_side_effects=True, vmem_limit_bytes=58 << 20
        ),
    )(out_w, rows, short_w, lines_behind, lines_ahead, tail, grad_out)


def tiled(kernel, ins, outs, scratch, arrays, tiles, flops=0):
    read = sum(math.prod(a.shape) * a.dtype.itemsize for a in arrays)
    return pl.pallas_call(
        kernel,
        grid=(tiles,),
        in_specs=[pl.BlockSpec(block, index) for block, index in ins],
        out_specs=[pl.BlockSpec(block, index) for block, index, _, _ in outs],
        out_shape=[jax.ShapeDtypeStruct(shape, kind) for _, _, shape, kind in outs],
        scratch_shapes=scratch,
        cost_estimate=pl.CostEstimate(flops=flops, bytes_accessed=read, transcendentals=0),
        compiler_params=pltpu.CompilerParams(vmem_limit_bytes=48 << 20),
    )(*arrays)


def shards(projected, short_w, medium_h, out_w, grad_out):
    seqs, row_count, _, chans = projected.shape
    taps = medium_h.shape[1]
    groups_here = medium_h.shape[0]
    tiles = chans // LANES
    groups = groups_here // tiles
    rows = jnp.swapaxes(projected, 1, 2)

    lines_behind = jnp.pad(medium_h[:, ::-1].astype(F32), ((0, 0), (1, 2 * BLOCK - taps - 1)))
    lines_ahead = jnp.pad(medium_h.astype(F32), ((0, 0), (0, 2 * BLOCK - taps)))

    lane3 = lambda i: (0, 0, i)
    lane4 = lambda i: (0, 0, 0, i)
    front_spec = ((seqs, 3, HALO, LANES), lane4)
    rows_spec = ((seqs, 3, row_count, LANES), lane4)
    taps_spec = ((3, short_w.shape[1], LANES), lane3)
    lines_spec = ((groups, 2 * BLOCK), lambda i: (i, 0))
    edge_spec = ((seqs, BLOCK, LANES), lane3)
    full_spec = ((seqs, row_count, LANES), lane3)
    line_rows = pltpu.VMEM((row_count + HALO, LANES), F32)
    padded_spec = ((seqs, row_count + BLOCK, LANES), lane3)
    bands = pltpu.VMEM((groups * BLOCK, 2 * BLOCK), BF)

    tail = tiled(
        tail_kernel,
        [
            ((seqs, 3, HALO, LANES), lambda i: (0, 0, (row_count - BLOCK) // HALO - 1, i)),
            ((seqs, 3, BLOCK, LANES), lambda i: (0, 0, row_count // BLOCK - 1, i)),
            taps_spec,
        ],
        [(*edge_spec, (seqs, BLOCK, chans), BF)],
        [line_rows],
        (rows, rows, short_w),
        tiles,
    )[0]
    block_out, cotangent, mixed, product, mix, front, later = exchange(
        out_w, rows, short_w, lines_behind, lines_ahead, tail, grad_out
    )
    filter_part = tiled(
        filter_kernel,
        [full_spec, padded_spec],
        [((groups, LANES), lambda i: (i, 0), (groups_here, taps), F32)],
        [],
        (mix, product),
        tiles,
    )[0]
    grad, short_part = tiled(
        backward_kernel,
        [full_spec, front_spec, rows_spec, taps_spec, lines_spec, full_spec, padded_spec, front_spec],
        [(*rows_spec, rows.shape, BF), ((1, HALO, LANES), lambda i: (i, 0, 0), (tiles, HALO, LANES), F32)],
        [line_rows, pltpu.VMEM((seqs, row_count, LANES), F32), line_rows, bands],
        (cotangent, front, rows, short_w, lines_ahead, mixed, mix, later),
        tiles,
    )

    pieces = ALONG_Z
    packed = jnp.concatenate([filter_part, short_part.reshape(tiles * HALO, LANES)], axis=0)
    depth = packed.shape[0] // pieces
    piece = (depth, LANES)
    peers = 2 * (lax.axis_size("ctx") // pieces)
    sums = pl.pallas_call(
        reduce_kernel,
        out_shape=jax.ShapeDtypeStruct((pieces, *piece), F32),
        in_specs=[pl.BlockSpec(memory_space=pltpu.VMEM)],
        out_specs=pl.BlockSpec(memory_space=pltpu.VMEM),
        scratch_shapes=[
            pltpu.VMEM((pieces, *piece), F32), pltpu.VMEM(piece, F32),
            pltpu.VMEM((peers, *piece), F32), pltpu.VMEM(piece, F32),
        ]
        + [pltpu.SemaphoreType.DMA((8,))] * 6,
        compiler_params=pltpu.CompilerParams(collective_id=1, has_side_effects=True),
    )(packed.reshape(pieces, *piece)).reshape(packed.shape)

    seq_total = seqs * lax.axis_size("dp")
    length_total = row_count * lax.axis_size("ctx")
    filter_grad = sums[:groups_here, ::-1] / math.sqrt(seq_total * length_total * (LANES // groups))
    streams = sums[groups_here:].reshape(tiles, HALO, LANES)[:, : 3 * short_w.shape[1]]
    short_sum = jnp.swapaxes(streams, 0, 1).reshape(3, short_w.shape[1], chans)
    short_grad = short_sum / math.sqrt(seq_total * length_total)
    return (block_out, jnp.swapaxes(grad, 1, 2), filter_grad, short_grad)


def solution(mesh):
    in_specs = (
        P("dp", "ctx", None, "grp"),
        P(None, None, "grp"),
        P("grp", None),
        P("ctx", "grp"),
        P("dp", "ctx", "grp"),
    )
    out_specs = (
        P("dp", "ctx", "grp"),
        P("dp", "ctx", None, "grp"),
        P("grp", None),
        P(None, None, "grp"),
    )
    return jax.shard_map(shards, mesh=mesh, in_specs=in_specs, out_specs=out_specs, check_vma=False)
```

```python
import functools
import math

import jax
import jax.numpy as jnp
from jax import lax
from jax.experimental import pallas as pl
from jax.experimental.pallas import tpu as pltpu
from jax.sharding import PartitionSpec as P

BF = jnp.bfloat16
F32 = jnp.float32
LANES = 128
BLOCK = 128
HALO = 16
MESH = pl.DeviceIdType.MESH
ALONG_Z = 8


def fill(scratch, front, rows):
    scratch[0:HALO, :] = front.astype(F32)
    scratch[HALO : HALO + rows.shape[0], :] = rows.astype(F32)


def feature(scratch, taps, stream, count):
    total = None
    for offset in range(taps.shape[1]):
        start = HALO - offset
        term = taps[stream, offset : offset + 1, :] * scratch[start : start + count, :]
        total = term if total is None else total + term
    return total


def ahead_lines(filters):
    return jnp.concatenate([filters.astype(F32), jnp.zeros(filters.shape, F32)], axis=1)


def behind_lines(filters):
    taps = filters.shape[1]
    row = lax.broadcasted_iota(jnp.int32, (taps, 2 * BLOCK), 0)
    column = lax.broadcasted_iota(jnp.int32, (taps, 2 * BLOCK), 1)
    return jnp.dot(filters, (row + column == BLOCK).astype(BF), preferred_element_type=F32)


def band_rows(lines, band, count=BLOCK):
    groups = lines.shape[0]
    for g in range(groups):
        line = jnp.broadcast_to(lines[g : g + 1, :], (count, lines.shape[1]))
        turned = pltpu.roll(line, 0, 1, stride=1, stride_axis=0)
        band[g * count : (g + 1) * count, :] = turned.astype(BF)


def group_of_lane(shape, groups):
    lane = lax.broadcasted_iota(jnp.int32, shape, len(shape) - 1)
    return (lane % LANES) // (LANES // groups)


def own_group(wide, groups, count=BLOCK):
    owner = group_of_lane((count, wide.shape[1]), groups)
    kept = wide[0:count]
    for g in range(1, groups):
        kept = jnp.where(owner == g, wide[g * count : (g + 1) * count], kept)
    return kept


def window_pair(padded, start, lanes=slice(None)):
    return jnp.concatenate(
        [padded[s, start : start + 2 * BLOCK, lanes] for s in range(padded.shape[0])], axis=1
    )


def filter_sums(mix_ref, product_ref, sums_ref):
    seqs, row_count = product_ref.shape[0], product_ref.shape[1] - BLOCK
    groups = sums_ref.shape[0]
    rows = lax.broadcasted_iota(jnp.int32, (2 * BLOCK, 2 * BLOCK), 0)
    columns = lax.broadcasted_iota(jnp.int32, (2 * BLOCK, 2 * BLOCK), 1)
    upturn = (rows + columns == 2 * BLOCK - 1).astype(BF)
    parts, wins = [], []
    for s in range(seqs):
        for b in range(row_count // BLOCK):
            parts.append(mix_ref[s, b * BLOCK : (b + 1) * BLOCK, :])
            wins.append(product_ref[s, b * BLOCK : (b + 2) * BLOCK, :])
    grads = jnp.concatenate(parts, axis=1)
    windows = jnp.dot(upturn, jnp.concatenate(wins, axis=1), preferred_element_type=F32).astype(BF)
    owner = group_of_lane(grads.shape, groups)
    stacked = jnp.concatenate(
        [jnp.where(owner == g, grads.astype(F32), 0.0).astype(BF) for g in range(groups)], axis=0
    )
    lags = lax.dot_general(
        stacked, windows, (((1,), (1,)), ((), ())), preferred_element_type=F32
    )
    found = []
    for g in range(groups):
        turned = pltpu.roll(lags[g * BLOCK : (g + 1) * BLOCK], 0, 1, stride=1, stride_axis=0)
        found.append(jnp.sum(turned, axis=0, keepdims=True))
    sums_ref[...] = pltpu.roll(jnp.concatenate(found, axis=0), BLOCK + 1, 1)[:, :BLOCK]


def backward_kernel(
    cotangent_ref, front_ref, rows_ref, taps_ref, filters_ref, mixed_ref,
    padded_ref, product_ref, next_ref, grad_ref, short_ref, sums_ref, scratch, pulled, later, band,
):
    seqs, row_count = rows_ref.shape[0], rows_ref.shape[2]
    groups = sums_ref.shape[0]
    taps = taps_ref.shape[1]
    filter_sums(padded_ref, product_ref, sums_ref)
    first = pl.multiple_of(pl.program_id(0) * groups, groups)
    band_rows(ahead_lines(filters_ref[pl.ds(first, groups), :]), band)
    for b in range(row_count // BLOCK):
        wide = jnp.dot(
            band[...], window_pair(padded_ref, b * BLOCK), preferred_element_type=F32
        )
        kept = own_group(wide, groups)
        for s in range(seqs):
            pulled[s, b * BLOCK : (b + 1) * BLOCK, :] = kept[:, s * LANES : (s + 1) * LANES]
    sums = [None] * (3 * taps)
    for s in range(seqs):
        for stream in range(3):
            if stream == 0:
                grad = cotangent_ref[s].astype(F32) * mixed_ref[s]
            else:
                other = 3 - stream
                fill(scratch, front_ref[s, other], rows_ref[s, other])
                grad = pulled[s] * feature(scratch, taps_ref, other, row_count)
            grad = grad.astype(BF).astype(F32)
            fill(scratch, front_ref[s, stream], rows_ref[s, stream])
            later[0:row_count, :] = grad
            later[row_count : row_count + HALO, :] = next_ref[s, stream].astype(F32)
            total = None
            for offset in range(taps):
                term = taps_ref[stream, offset : offset + 1, :] * later[offset : offset + row_count, :]
                total = term if total is None else total + term
                at = HALO - offset
                found = jnp.sum(grad * scratch[at : at + row_count, :], axis=0, keepdims=True)
                row = stream * taps + offset
                sums[row] = found if sums[row] is None else sums[row] + found
            grad_ref[s, stream] = total.astype(BF)
    short_ref[...] = jnp.zeros_like(short_ref)
    for row in range(3 * taps):
        short_ref[0, row : row + 1, :] = sums[row]


def reduce_kernel(
    along_z, scales, filter_ref, short_ref, filter_out, short_out,
    packed, mine_of, part, gathered, whole, result, zs, zr, ys, yr, os, orr,
):
    me, core = lax.axis_index("ctx"), lax.axis_index("dp")
    line, place = me // along_z, me % along_z
    lines = lax.axis_size("ctx") // along_z
    peers = lines * 2
    mine = line * 2 + core
    depth = packed.shape[0] // peers
    tiles, width = short_ref.shape[0], packed.shape[0] // short_ref.shape[0]
    groups = width - short_ref.shape[1]

    def along(step):
        return {"ctx": line * along_z + (place + step) % along_z}

    def across(step):
        other = (mine + step) % peers
        return {"ctx": (other // 2) * along_z + place, "dp": other % 2}

    barrier = pltpu.get_barrier_semaphore()
    for step in range(1, along_z):
        pl.semaphore_signal(barrier, inc=1, device_id=along(step), device_id_type=MESH)
    for step in range(1, peers):
        pl.semaphore_signal(barrier, inc=1, device_id=across(step), device_id_type=MESH)
    for k in range(tiles):
        packed[k * width : k * width + groups, :] = filter_ref[k * groups : (k + 1) * groups, :]
        packed[k * width + groups : (k + 1) * width, :] = short_ref[k]
    pl.semaphore_wait(barrier, along_z + peers - 2)

    def rows_of(piece):
        return pl.ds(pl.multiple_of(piece * depth, depth), depth)

    def first(step):
        return pltpu.make_async_remote_copy(
            src_ref=packed.at[rows_of((mine + step) % peers), :], dst_ref=mine_of.at[mine],
            send_sem=zs.at[step], recv_sem=zr.at[step],
            device_id=across(step), device_id_type=MESH,
        )

    def second(step):
        return pltpu.make_async_remote_copy(
            src_ref=part, dst_ref=gathered.at[place], send_sem=ys.at[step], recv_sem=yr.at[step],
            device_id=along(step), device_id_type=MESH,
        )

    def third(step):
        return pltpu.make_async_remote_copy(
            src_ref=whole, dst_ref=result.at[rows_of(mine), :], send_sem=os.at[step], recv_sem=orr.at[step],
            device_id=across(step), device_id_type=MESH,
        )

    for step in range(1, peers):
        first(step).start()
    mine_of[mine] = packed[rows_of(mine), :]
    for step in range(1, peers):
        first(step).wait_recv()
    total = mine_of[0]
    for k in range(1, peers):
        total = total + mine_of[k]
    part[...] = total
    for step in range(1, along_z):
        second(step).start()
    gathered[place] = total
    for step in range(1, along_z):
        second(step).wait_recv()
    total = gathered[0]
    for k in range(1, along_z):
        total = total + gathered[k]
    whole[...] = total
    for step in range(1, peers):
        third(step).start()
    result[rows_of(mine), :] = total
    for step in range(1, peers):
        third(step).wait_recv()
    taps = short_out.shape[1]
    for k in range(tiles):
        at = k * width
        filter_out[k * groups : (k + 1) * groups, :] = result[at : at + groups, :] * scales[0]
        at += groups
        for stream in range(3):
            rows = result[at + stream * taps : at + (stream + 1) * taps, :]
            short_out[stream, :, k * LANES : (k + 1) * LANES] = rows * scales[1]
    for step in range(1, peers):
        first(step).wait_send()
        third(step).wait_send()
    for step in range(1, along_z):
        second(step).wait_send()


def exchange_kernel(
    along_z, w_ref, rows_ref, taps_ref, filters_ref, cotangent_ref,
    out_ref, grad_ref, mixed_ref, product_ref, mix_ref, front_ref, later_ref,
    whole, gated, gathered, turned, queries, to_a, to_b, from_a, from_b,
    to_right, to_left, from_left, from_right, kept_right, kept_left, own, head,
    scratch, band, low_band,
    z_send, z_recv, up_send, up_recv, down_send, down_recv, far_send, far_recv,
    pair_send, pair_recv, x_send, x_recv, sum_send, sum_recv, halo_send, halo_recv,
):
    ctx, core, x = lax.axis_index("ctx"), lax.axis_index("dp"), lax.axis_index("grp")
    size, ring = lax.axis_size("ctx"), lax.axis_size("grp")
    lines = size // along_z
    y, z = ctx // along_z, ctx % along_z
    part = w_ref.shape[0] // 2
    total, chans = gated.shape
    half = total // 2
    seqs, row_count = rows_ref.shape[0], rows_ref.shape[2]
    tiles = chans // LANES
    groups = filters_ref.shape[0] // tiles

    def at_z(step):
        return {"ctx": y * along_z + (z + along_z + step) % along_z}

    def at_y(step):
        return {"ctx": (y + lines + step) % lines * along_z + z}

    def at_x(step):
        return {"grp": (x + ring + step) % ring}

    def at_ctx(step):
        return {"ctx": (ctx + size + step) % size}

    partner = {"dp": 1 - core}
    barrier = pltpu.get_barrier_semaphore()
    greeted = (at_z(1), at_z(-1), at_y(1), at_y(-1), at_x(1), at_x(-1), at_ctx(1), at_ctx(-1), partner)
    for device in greeted:
        pl.semaphore_signal(barrier, inc=1, device_id=device, device_id_type=MESH)
    pl.semaphore_wait(barrier, len(greeted))

    def copy(src, dst, send, recv, device):
        return pltpu.make_async_remote_copy(
            src_ref=src, dst_ref=dst, send_sem=send, recv_sem=recv, device_id=device, device_id_type=MESH
        )

    started = []

    def go(*what):
        started.append(copy(*what))
        started[-1].start()

    def arrive(here, send, recv, device):
        copy(here, here, send, recv, device).wait_recv()

    def halo(n, src, dst, device):
        go(src, dst, halo_send.at[n], halo_recv.at[n], device)

    def halo_wait(n, here, device, edge):
        arrive(here, halo_send.at[n], halo_recv.at[n], device)

        @pl.when(ctx == edge)
        def _():
            here[...] = jnp.zeros(here.shape, here.dtype)

    def lanes_of(i):
        return pl.ds(pl.multiple_of(i * LANES, LANES), LANES)

    def lines_of(ref, i):
        return ref[pl.ds(pl.multiple_of(i * groups, groups), groups), :]

    def block(step_y, step_z, carrier):
        row = ((y + lines + step_y) % lines * along_z + (z + along_z + step_z) % along_z) * 2 + carrier
        return whole.at[pl.ds(pl.multiple_of(row * part, part), part), :]

    steps = [0]
    for k in range(1, along_z // 2):
        steps.append(k)
    for k in range(1, along_z // 2 + 1):
        steps.insert(2 if k == 1 else len(steps), -k)

    def hand_over(kind, step_y, u):
        place = kind * along_z + u
        mine = block(step_y, steps[u], core)
        go(mine, mine, pair_send.at[place], pair_recv.at[place], partner)

    def z_turn(u):
        mine = w_ref.at[pl.ds(pl.multiple_of(core * part, part), part), :]
        if u > 0:
            mine = block(0, steps[u], core)
            arrive(mine, z_send.at[u], z_recv.at[u], at_z(1))
        for direction in (-1, 1):
            onward = steps[u] + direction
            if onward in steps and (u == 0 or steps[u] * direction > 0):
                v = steps.index(onward)
                go(mine, block(0, steps[u], core), z_send.at[v], z_recv.at[v], at_z(-direction))
        go(mine, block(0, steps[u], core), up_send.at[u], up_recv.at[u], at_y(1))
        go(mine, block(0, steps[u], core), down_send.at[u], down_recv.at[u], at_y(-1))
        if u > 0:
            hand_over(0, 0, u)

    def y_turn(u):
        behind, ahead = block(-1, steps[u], core), block(1, steps[u], core)
        arrive(behind, up_send.at[u], up_recv.at[u], at_y(1))
        if u % 2 == 0:
            go(behind, behind, far_send.at[u], far_recv.at[u], at_y(1))
        hand_over(1, -1, u)
        arrive(ahead, down_send.at[u], down_recv.at[u], at_y(-1))
        if u % 2 == 1:
            go(ahead, ahead, far_send.at[u], far_recv.at[u], at_y(-1))
        hand_over(2, 1, u)

    def far_turn(u):
        arrive(block(2, steps[u], core), far_send.at[u], far_recv.at[u], at_y(1))
        hand_over(3, 2, u)

    pieces = [(b, s) for b in (1, 0) for s in range(seqs)]

    def flat_rows(b, s):
        return pl.ds((b * seqs + s) * BLOCK, BLOCK)

    def x_start(c):
        here = flat_rows(*pieces[c])
        src = gated.at[here, :]
        go(src, gathered.at[0, here, :], x_send.at[0, c], x_recv.at[0, c], at_x(1))
        go(src, gathered.at[1, here, :], x_send.at[1, c], x_recv.at[1, c], at_x(-1))

    def x_wait(slot, c):
        arrive(gathered.at[slot, flat_rows(*pieces[c]), :], x_send.at[slot, c], x_recv.at[slot, c], at_x(1))

    def x_turn(c):
        x_wait(0, c)
        x_wait(1, c)
        here = flat_rows(*pieces[c])
        slot, to = (0, at_x(1)) if c < len(pieces) // 2 else (1, at_x(-1))
        go(gathered.at[slot, here, :], gathered.at[2, here, :], x_send.at[2, c], x_recv.at[2, c], to)

    def mix_block(i, b):
        wide = jnp.dot(band[i], window_pair(product_ref, b * BLOCK, lanes_of(i)), preferred_element_type=F32)
        kept = own_group(wide, groups)
        for s in range(seqs):
            mixed = kept[:, s * LANES : (s + 1) * LANES]
            here = slice(b * BLOCK, (b + 1) * BLOCK)
            mixed_ref[s, here, lanes_of(i)] = mixed
            gated[flat_rows(b, s), lanes_of(i)] = (queries[s, here, lanes_of(i)] * mixed).astype(BF)

    def taps_of(i):
        return taps_ref[:, :, lanes_of(i)]

    def features_of(i, s, streams, count, at=0):
        found = []
        for stream in streams:
            if at == 0:
                before = front_ref[s, stream, :, lanes_of(i)]
            else:
                before = rows_ref[s, stream, at - HALO : at, lanes_of(i)]
            fill(scratch, before, rows_ref[s, stream, at : at + count, lanes_of(i)])
            taps, sum_ = taps_of(i), None
            for offset in range(taps.shape[1]):
                start = HALO - offset
                term = taps[stream, offset : offset + 1, :] * scratch[start : start + count, :]
                sum_ = term if sum_ is None else sum_ + term
            found.append(sum_)
        return found

    def features(i, at, count):
        for s in range(seqs):
            query, key, value = features_of(i, s, range(3), count, at)
            queries[s, at : at + count, lanes_of(i)] = query
            product_ref[s, BLOCK + at : BLOCK + at + count, lanes_of(i)] = (key * value).astype(BF)

    last = row_count - BLOCK

    def tails(i, carry):
        features(i, last, BLOCK)
        return carry

    def bands(i, carry):
        band_rows(behind_lines(lines_of(filters_ref, i)), band.at[i])
        return carry

    def forward(i, carry):
        features(i, 0, last)
        mix_block(i, 1)
        return carry

    def forward_first(i, carry):
        mix_block(i, 0)
        return carry

    halo(0, rows_ref.at[:, :, row_count - HALO :, :], front_ref, at_ctx(1))
    z_turn(0)
    lax.fori_loop(0, tiles, tails, 0)
    halo(1, product_ref.at[:, row_count:, :], product_ref.at[:, 0:BLOCK, :], at_ctx(1))
    lax.fori_loop(0, tiles, bands, 0)
    for b in range(row_count // BLOCK):
        for s in range(seqs):
            turned[flat_rows(b, s), :] = cotangent_ref[s, b * BLOCK : (b + 1) * BLOCK, :]
    for u in range(1, min(3, along_z)):
        z_turn(u)
    halo_wait(0, front_ref, at_ctx(1), 0)
    lax.fori_loop(0, tiles, forward, 0)
    x_start(0)
    x_start(1)
    whole[pl.ds(pl.multiple_of(ctx * 2 * part, 2 * part), 2 * part), :] = w_ref[...]

    def second_half():
        halo_wait(1, product_ref.at[:, 0:BLOCK, :], at_ctx(1), 0)
        lax.fori_loop(0, tiles, forward_first, 0)
        x_start(2)
        x_start(3)

    plan = []
    for u in range(along_z + 2):
        if 3 <= u < along_z:
            plan.append((z_turn, u))
        if 0 <= u - 1 < along_z and u > 0:
            plan.append((y_turn, u - 1))
        if 0 <= u - 2 < along_z and u > 1:
            plan.append((far_turn, u - 2))
        if u == min(3, along_z):
            plan.append((second_half,))
        if u == min(5, along_z + 1):
            plan.append((x_turn, 0))
        if u == min(6, along_z + 1):
            plan.append((x_turn, 1))
        if u == along_z:
            plan.append((x_turn, 2))
    if along_z < 8:
        plan = [p for p in plan if p[0] is not x_turn] + [(x_turn, c) for c in range(3)]
    for what, *which in plan:
        what(*which)
    for kind, step_y in enumerate((0, -1, 1, 2)):
        for u in range(1 if kind == 0 else 0, along_z):
            place = kind * along_z + u
            arrive(block(step_y, steps[u], 1 - core), pair_send.at[place], pair_recv.at[place], partner)

    wide = min(chans, 256)
    right, left, across = (x + 1) % ring, (x + ring - 1) % ring, (x + 2) % ring
    count = chans // wide

    def columns(j):
        return pl.ds(pl.multiple_of(j * wide, wide), wide)

    def partial(owner, j):
        rows = whole[pl.ds(pl.multiple_of(owner * chans + j * wide, wide), wide), :]
        return lax.dot_general(turned[...], rows, (((1,), (1,)), ((), ())), preferred_element_type=F32)

    def far_sums(j, carry):
        found = partial(across, j)
        to_a[:, columns(j)] = found[:half].astype(BF)
        to_b[:, columns(j)] = found[half:].astype(BF)
        return carry

    def near_sums(j, carry):
        found = partial(left, j)
        to_left[:half, columns(j)] = found[:half].astype(BF)
        kept_left[:, columns(j)] = found[half:]
        found = partial(right, j)
        kept_right[:, columns(j)] = found[:half]
        to_right[half:, columns(j)] = found[half:].astype(BF)
        return carry

    def own_sums(j, carry):
        own[:, columns(j)] = partial(x, j)
        return carry

    def outputs(j, carry):
        found = None
        for slot, owner in ((None, x), (0, left), (1, right), (2, across)):
            rows = whole[pl.ds(pl.multiple_of(owner * chans, chans), chans), columns(j)]
            source = gated[...] if slot is None else gathered[slot]
            term = jnp.dot(source, rows, preferred_element_type=F32)
            found = term if found is None else found + term
        for b in range(row_count // BLOCK):
            for s in range(seqs):
                at = (b * seqs + s) * BLOCK
                out_ref[s, b * BLOCK : (b + 1) * BLOCK, columns(j)] = found[at : at + BLOCK].astype(BF)
        return carry

    def piece(ref, at, n):
        return ref.at[pl.ds(at + n * BLOCK, BLOCK), :]

    def send_sum(n, src, dst, device):
        go(src, dst, sum_send.at[n], sum_recv.at[n], device)

    def wait_sum(n, here):
        arrive(here, sum_send.at[n], sum_recv.at[n], at_x(1))

    def relay_a(n):
        wait_sum(n, piece(from_a, 0, n))
        rows = slice(n * BLOCK, (n + 1) * BLOCK)
        to_right[rows, :] = (kept_right[rows, :] + from_a[rows, :].astype(F32)).astype(BF)
        send_sum(4 + n, piece(to_right, 0, n), piece(from_left, 0, n), at_x(1))

    def relay_b(n):
        wait_sum(2 + n, piece(from_b, 0, n))
        rows, there = slice(n * BLOCK, (n + 1) * BLOCK), slice(half + n * BLOCK, half + (n + 1) * BLOCK)
        to_left[there, :] = (kept_left[rows, :] + from_b[rows, :].astype(F32)).astype(BF)
        send_sum(6 + n, piece(to_left, half, n), piece(from_right, half, n), at_x(-1))

    first, second = pl.ds(0, half), pl.ds(half, half)
    lax.fori_loop(0, count, far_sums, 0)
    x_turn(3)
    for n in range(2):
        send_sum(n, piece(to_a, 0, n), piece(from_a, 0, n), at_x(1))
        send_sum(2 + n, piece(to_b, 0, n), piece(from_b, 0, n), at_x(-1))
    lax.fori_loop(0, count, near_sums, 0)
    send_sum(8, to_left.at[first, :], from_right.at[first, :], at_x(-1))
    relay_a(0)
    lax.fori_loop(0, count, own_sums, 0)
    relay_a(1)
    send_sum(9, to_right.at[second, :], from_left.at[second, :], at_x(1))
    relay_b(0)
    relay_b(1)
    for c in range(len(pieces)):
        x_wait(2, c)
    lax.fori_loop(0, count, outputs, 0)

    def finish(b):
        for s in range(seqs):
            at = slice((b * seqs + s) * BLOCK, (b * seqs + s + 1) * BLOCK)
            here = slice(b * BLOCK, (b + 1) * BLOCK)
            found = own[at, :] + (from_left[at, :].astype(F32) + from_right[at, :].astype(F32))
            found = found.astype(BF)
            grad_ref[s, here, :] = found
            mix_ref[s, here, :] = (found.astype(F32) * queries[s, here, :]).astype(BF)

    wait_sum(8, from_right.at[first, :])
    for n in range(2):
        wait_sum(4 + n, piece(from_left, 0, n))
    finish(0)
    halo(2, mix_ref.at[:, 0:BLOCK, :], mix_ref.at[:, row_count:, :], at_ctx(-1))
    wait_sum(9, from_left.at[second, :])
    for n in range(2):
        wait_sum(6 + n, piece(from_right, half, n))
    finish(1)

    def heads(i, carry):
        band_rows(ahead_lines(lines_of(filters_ref, i)), low_band, HALO)
        low = jnp.dot(low_band[...], window_pair(mix_ref, 0, lanes_of(i)), preferred_element_type=F32)
        pulled = own_group(low, groups, HALO)
        for s in range(seqs):
            here = pulled[:, s * LANES : (s + 1) * LANES]
            key, value = features_of(i, s, (1, 2), HALO)
            grad = grad_ref[s, 0:HALO, lanes_of(i)].astype(F32)
            head[s, 0, :, lanes_of(i)] = (grad * mixed_ref[s, 0:HALO, lanes_of(i)]).astype(BF)
            head[s, 1, :, lanes_of(i)] = (here * value).astype(BF)
            head[s, 2, :, lanes_of(i)] = (here * key).astype(BF)
        return carry

    lax.fori_loop(0, tiles, heads, 0)
    halo(3, head, later_ref, at_ctx(-1))
    halo_wait(2, mix_ref.at[:, row_count:, :], at_ctx(-1), size - 1)
    halo_wait(3, later_ref, at_ctx(-1), size - 1)
    for sent in started:
        sent.wait_send()


def exchange(out_w, rows, short_w, medium_h, grad_out):
    seqs, row_count, chans = grad_out.shape
    total = seqs * row_count
    depth = out_w.shape[0] * lax.axis_size("ctx")
    tiles = chans // LANES
    groups = medium_h.shape[0] // tiles
    half = (total // 2, chans)
    dma = pltpu.SemaphoreType.DMA
    flops = 4 * total * depth * chans
    padded = (seqs, row_count + BLOCK, chans)
    edge = (seqs, 3, HALO, chans)
    shape = jax.ShapeDtypeStruct
    return pl.pallas_call(
        functools.partial(exchange_kernel, ALONG_Z),
        out_shape=[
            shape(grad_out.shape, BF), shape(grad_out.shape, BF), shape(grad_out.shape, F32),
            shape(padded, BF), shape(padded, BF), shape(edge, BF), shape(edge, BF),
        ],
        in_specs=[pl.BlockSpec(memory_space=pltpu.VMEM)] * 5,
        out_specs=[pl.BlockSpec(memory_space=pltpu.VMEM)] * 7,
        scratch_shapes=[
            pltpu.VMEM((depth, chans), BF),
            pltpu.VMEM((total, chans), BF),
            pltpu.VMEM((3, total, chans), BF),
            pltpu.VMEM((total, chans), BF),
            pltpu.VMEM((seqs, row_count, chans), F32),
        ]
        + [pltpu.VMEM(half, BF)] * 4
        + [pltpu.VMEM((total, chans), BF)] * 4
        + [pltpu.VMEM(half, F32)] * 2
        + [
            pltpu.VMEM((total, chans), F32),
            pltpu.VMEM(edge, BF),
            pltpu.VMEM((row_count + HALO, LANES), F32),
            pltpu.VMEM((tiles, groups * BLOCK, 2 * BLOCK), BF),
            pltpu.VMEM((groups * HALO, 2 * BLOCK), BF),
        ]
        + [dma((ALONG_Z,))] * 8
        + [dma((4 * ALONG_Z,))] * 2
        + [dma((3, 4))] * 2
        + [dma((10,))] * 2
        + [dma((4,))] * 2,
        cost_estimate=pl.CostEstimate(flops=flops, bytes_accessed=8 * total * chans, transcendentals=0),
        compiler_params=pltpu.CompilerParams(
            collective_id=2, has_side_effects=True, vmem_limit_bytes=58 << 20
        ),
    )(out_w, rows, short_w, medium_h, grad_out)


def tiled(kernel, ins, outs, scratch, arrays, tiles, flops=0):
    read = sum(math.prod(a.shape) * a.dtype.itemsize for a in arrays)
    return pl.pallas_call(
        kernel,
        grid=(tiles,),
        in_specs=[pl.BlockSpec(block, index) for block, index in ins],
        out_specs=[pl.BlockSpec(block, index) for block, index, _, _ in outs],
        out_shape=[jax.ShapeDtypeStruct(shape, kind) for _, _, shape, kind in outs],
        scratch_shapes=scratch,
        cost_estimate=pl.CostEstimate(flops=flops, bytes_accessed=read, transcendentals=0),
        compiler_params=pltpu.CompilerParams(vmem_limit_bytes=48 << 20),
    )(*arrays)


def shards(projected, short_w, medium_h, out_w, grad_out):
    seqs, row_count, _, chans = projected.shape
    taps = medium_h.shape[1]
    groups_here = medium_h.shape[0]
    tiles = chans // LANES
    groups = groups_here // tiles
    rows = jnp.swapaxes(projected, 1, 2)

    lane3 = lambda i: (0, 0, i)
    lane4 = lambda i: (0, 0, 0, i)
    front_spec = ((seqs, 3, HALO, LANES), lane4)
    rows_spec = ((seqs, 3, row_count, LANES), lane4)
    taps_spec = ((3, short_w.shape[1], LANES), lane3)
    filters_spec = ((groups_here, taps), lambda i: (0, 0))
    full_spec = ((seqs, row_count, LANES), lane3)
    line_rows = pltpu.VMEM((row_count + HALO, LANES), F32)
    padded_spec = ((seqs, row_count + BLOCK, LANES), lane3)
    bands = pltpu.VMEM((groups * BLOCK, 2 * BLOCK), BF)

    block_out, cotangent, mixed, product, mix, front, later = exchange(
        out_w, rows, short_w, medium_h, grad_out
    )
    grad, short_part, filter_part = tiled(
        backward_kernel,
        [full_spec, front_spec, rows_spec, taps_spec, filters_spec, full_spec, padded_spec, padded_spec, front_spec],
        [
            (*rows_spec, rows.shape, BF),
            ((1, HALO, LANES), lambda i: (i, 0, 0), (tiles, HALO, LANES), F32),
            ((groups, LANES), lambda i: (i, 0), (groups_here, taps), F32),
        ],
        [line_rows, pltpu.VMEM((seqs, row_count, LANES), F32), line_rows, bands],
        (cotangent, front, rows, short_w, medium_h, mixed, mix, product, later),
        tiles,
    )

    seq_total = seqs * lax.axis_size("dp")
    length_total = row_count * lax.axis_size("ctx")
    scales = (
        1.0 / math.sqrt(seq_total * length_total * (LANES // groups)),
        1.0 / math.sqrt(seq_total * length_total),
    )
    sum_rows = groups_here + tiles * HALO
    peers = 2 * (lax.axis_size("ctx") // ALONG_Z)
    piece = (sum_rows // peers, LANES)
    filter_grad, short_grad = pl.pallas_call(
        functools.partial(reduce_kernel, ALONG_Z, scales),
        out_shape=[jax.ShapeDtypeStruct((groups_here, taps), F32), jax.ShapeDtypeStruct(short_w.shape, F32)],
        in_specs=[pl.BlockSpec(memory_space=pltpu.VMEM)] * 2,
        out_specs=[pl.BlockSpec(memory_space=pltpu.VMEM)] * 2,
        scratch_shapes=[
            pltpu.VMEM((sum_rows, LANES), F32),
            pltpu.VMEM((peers, *piece), F32),
            pltpu.VMEM(piece, F32),
            pltpu.VMEM((ALONG_Z, *piece), F32),
            pltpu.VMEM(piece, F32),
            pltpu.VMEM((sum_rows, LANES), F32),
        ]
        + [pltpu.SemaphoreType.DMA((8,))] * 6,
        compiler_params=pltpu.CompilerParams(collective_id=1, has_side_effects=True),
    )(filter_part, short_part)
    return (block_out, jnp.swapaxes(grad, 1, 2), filter_grad, short_grad)


def solution(mesh):
    in_specs = (
        P("dp", "ctx", None, "grp"),
        P(None, None, "grp"),
        P("grp", None),
        P("ctx", "grp"),
        P("dp", "ctx", "grp"),
    )
    out_specs = (
        P("dp", "ctx", "grp"),
        P("dp", "ctx", None, "grp"),
        P("grp", None),
        P(None, None, "grp"),
    )
    return jax.shard_map(shards, mesh=mesh, in_specs=in_specs, out_specs=out_specs, check_vma=False)
```

```python
import functools
import math

import jax
import jax.numpy as jnp
from jax import lax
from jax.experimental import pallas as pl
from jax.experimental.pallas import tpu as pltpu
from jax.sharding import PartitionSpec as P

BF = jnp.bfloat16
F32 = jnp.float32
LANES = 128
BLOCK = 128
HALO = 8
SUM_ROWS = 16
MESH = pl.DeviceIdType.MESH
ALONG_Z = 8


def fill(scratch, front, rows):
    scratch[0:HALO, :] = front.astype(F32)
    scratch[HALO : HALO + rows.shape[0], :] = rows.astype(F32)


def feature(scratch, taps, stream, count):
    total = None
    for offset in range(taps.shape[1]):
        start = HALO - offset
        term = taps[stream, offset : offset + 1, :] * scratch[start : start + count, :]
        total = term if total is None else total + term
    return total


def ahead_lines(filters):
    return jnp.concatenate([filters.astype(F32), jnp.zeros(filters.shape, F32)], axis=1)


def behind_lines(filters):
    taps = filters.shape[1]
    row = lax.broadcasted_iota(jnp.int32, (taps, 2 * BLOCK), 0)
    column = lax.broadcasted_iota(jnp.int32, (taps, 2 * BLOCK), 1)
    return jnp.dot(filters, (row + column == BLOCK).astype(BF), preferred_element_type=F32)


def band_rows(lines, band, count=BLOCK):
    groups = lines.shape[0]
    for g in range(groups):
        line = jnp.broadcast_to(lines[g : g + 1, :], (count, lines.shape[1]))
        turned = pltpu.roll(line, 0, 1, stride=1, stride_axis=0)
        band[g * count : (g + 1) * count, :] = turned.astype(BF)


def group_of_lane(shape, groups):
    lane = lax.broadcasted_iota(jnp.int32, shape, len(shape) - 1)
    return (lane % LANES) // (LANES // groups)


def own_group(wide, groups, count=BLOCK):
    owner = group_of_lane((count, wide.shape[1]), groups)
    kept = wide[0:count]
    for g in range(1, groups):
        kept = jnp.where(owner == g, wide[g * count : (g + 1) * count], kept)
    return kept


def window_pair(padded, start, lanes=slice(None)):
    return jnp.concatenate(
        [padded[s, start : start + 2 * BLOCK, lanes] for s in range(padded.shape[0])], axis=1
    )


def filter_sums(mix_ref, product_ref, sums_ref):
    seqs, row_count = product_ref.shape[0], product_ref.shape[1] - BLOCK
    groups = sums_ref.shape[0]
    rows = lax.broadcasted_iota(jnp.int32, (2 * BLOCK, 2 * BLOCK), 0)
    columns = lax.broadcasted_iota(jnp.int32, (2 * BLOCK, 2 * BLOCK), 1)
    upturn = (rows + columns == 2 * BLOCK - 1).astype(BF)
    parts, wins = [], []
    for s in range(seqs):
        for b in range(row_count // BLOCK):
            parts.append(mix_ref[s, b * BLOCK : (b + 1) * BLOCK, :])
            wins.append(product_ref[s, b * BLOCK : (b + 2) * BLOCK, :])
    grads = jnp.concatenate(parts, axis=1)
    windows = jnp.dot(upturn, jnp.concatenate(wins, axis=1), preferred_element_type=F32).astype(BF)
    owner = group_of_lane(grads.shape, groups)
    stacked = jnp.concatenate(
        [jnp.where(owner == g, grads.astype(F32), 0.0).astype(BF) for g in range(groups)], axis=0
    )
    lags = lax.dot_general(
        stacked, windows, (((1,), (1,)), ((), ())), preferred_element_type=F32
    )
    found = []
    for g in range(groups):
        turned = pltpu.roll(lags[g * BLOCK : (g + 1) * BLOCK], 0, 1, stride=1, stride_axis=0)
        found.append(jnp.sum(turned, axis=0, keepdims=True))
    sums_ref[...] = pltpu.roll(jnp.concatenate(found, axis=0), BLOCK + 1, 1)[:, :BLOCK]


def backward_kernel(
    cotangent_ref, front_ref, rows_ref, taps_ref, filters_ref, mixed_ref,
    padded_ref, product_ref, next_ref, grad_ref, short_ref, sums_ref, scratch, pulled, later, band,
):
    seqs, row_count = rows_ref.shape[0], rows_ref.shape[2]
    groups = sums_ref.shape[0]
    taps = taps_ref.shape[1]
    filter_sums(padded_ref, product_ref, sums_ref)
    first = pl.multiple_of(pl.program_id(0) * groups, groups)
    band_rows(ahead_lines(filters_ref[pl.ds(first, groups), :]), band)
    for b in range(row_count // BLOCK):
        wide = jnp.dot(
            band[...], window_pair(padded_ref, b * BLOCK), preferred_element_type=F32
        )
        kept = own_group(wide, groups)
        for s in range(seqs):
            pulled[s, b * BLOCK : (b + 1) * BLOCK, :] = kept[:, s * LANES : (s + 1) * LANES]
    sums = [None] * (3 * taps)
    for s in range(seqs):
        for stream in range(3):
            if stream == 0:
                grad = cotangent_ref[s].astype(F32) * mixed_ref[s]
            else:
                other = 3 - stream
                fill(scratch, front_ref[s, other], rows_ref[s, other])
                grad = pulled[s] * feature(scratch, taps_ref, other, row_count)
            grad = grad.astype(BF).astype(F32)
            fill(scratch, front_ref[s, stream], rows_ref[s, stream])
            later[0:row_count, :] = grad
            later[row_count : row_count + HALO, :] = next_ref[s, stream].astype(F32)
            total = None
            for offset in range(taps):
                term = taps_ref[stream, offset : offset + 1, :] * later[offset : offset + row_count, :]
                total = term if total is None else total + term
                at = HALO - offset
                found = jnp.sum(grad * scratch[at : at + row_count, :], axis=0, keepdims=True)
                row = stream * taps + offset
                sums[row] = found if sums[row] is None else sums[row] + found
            grad_ref[s, stream] = total.astype(BF)
    short_ref[...] = jnp.zeros_like(short_ref)
    for row in range(3 * taps):
        short_ref[0, row : row + 1, :] = sums[row]


def reduce_kernel(
    along_z, scales, filter_ref, short_ref, filter_out, short_out,
    packed, mine_of, part, gathered, whole, result, zs, zr, ys, yr, os, orr,
):
    me, core = lax.axis_index("ctx"), lax.axis_index("dp")
    line, place = me // along_z, me % along_z
    lines = lax.axis_size("ctx") // along_z
    peers = lines * 2
    mine = line * 2 + core
    depth = packed.shape[0] // peers
    tiles, width = short_ref.shape[0], packed.shape[0] // short_ref.shape[0]
    groups = width - short_ref.shape[1]

    def along(step):
        return {"ctx": line * along_z + (place + step) % along_z}

    def across(step):
        other = (mine + step) % peers
        return {"ctx": (other // 2) * along_z + place, "dp": other % 2}

    barrier = pltpu.get_barrier_semaphore()
    for step in range(1, along_z):
        pl.semaphore_signal(barrier, inc=1, device_id=along(step), device_id_type=MESH)
    for step in range(1, peers):
        pl.semaphore_signal(barrier, inc=1, device_id=across(step), device_id_type=MESH)
    for k in range(tiles):
        packed[k * width : k * width + groups, :] = filter_ref[k * groups : (k + 1) * groups, :]
        packed[k * width + groups : (k + 1) * width, :] = short_ref[k]
    pl.semaphore_wait(barrier, along_z + peers - 2)

    def rows_of(piece):
        return pl.ds(pl.multiple_of(piece * depth, depth), depth)

    def first(step):
        return pltpu.make_async_remote_copy(
            src_ref=packed.at[rows_of((mine + step) % peers), :], dst_ref=mine_of.at[mine],
            send_sem=zs.at[step], recv_sem=zr.at[step],
            device_id=across(step), device_id_type=MESH,
        )

    def second(step):
        return pltpu.make_async_remote_copy(
            src_ref=part, dst_ref=gathered.at[place], send_sem=ys.at[step], recv_sem=yr.at[step],
            device_id=along(step), device_id_type=MESH,
        )

    def third(step):
        return pltpu.make_async_remote_copy(
            src_ref=whole, dst_ref=result.at[rows_of(mine), :], send_sem=os.at[step], recv_sem=orr.at[step],
            device_id=across(step), device_id_type=MESH,
        )

    for step in range(1, peers):
        first(step).start()
    mine_of[mine] = packed[rows_of(mine), :]
    for step in range(1, peers):
        first(step).wait_recv()
    total = mine_of[0]
    for k in range(1, peers):
        total = total + mine_of[k]
    part[...] = total
    for step in range(1, along_z):
        second(step).start()
    gathered[place] = total
    for step in range(1, along_z):
        second(step).wait_recv()
    total = gathered[0]
    for k in range(1, along_z):
        total = total + gathered[k]
    whole[...] = total
    for step in range(1, peers):
        third(step).start()
    result[rows_of(mine), :] = total
    for step in range(1, peers):
        third(step).wait_recv()
    taps = short_out.shape[1]
    for k in range(tiles):
        at = k * width
        filter_out[k * groups : (k + 1) * groups, :] = result[at : at + groups, :] * scales[0]
        at += groups
        for stream in range(3):
            rows = result[at + stream * taps : at + (stream + 1) * taps, :]
            short_out[stream, :, k * LANES : (k + 1) * LANES] = rows * scales[1]
    for step in range(1, peers):
        first(step).wait_send()
        third(step).wait_send()
    for step in range(1, along_z):
        second(step).wait_send()


def exchange_kernel(
    along_z, w_ref, rows_ref, taps_ref, filters_ref, cotangent_ref,
    out_ref, grad_ref, mixed_ref, product_ref, mix_ref, front_ref, later_ref,
    whole, gated, gathered, turned, queries, to_a, to_b, from_a, from_b,
    to_right, to_left, from_left, from_right, kept_right, kept_left, own, head,
    scratch, band, low_band,
    z_send, z_recv, up_send, up_recv, down_send, down_recv, far_send, far_recv,
    pair_send, pair_recv, x_send, x_recv, sum_send, sum_recv, halo_send, halo_recv,
):
    ctx, core, x = lax.axis_index("ctx"), lax.axis_index("dp"), lax.axis_index("grp")
    size, ring = lax.axis_size("ctx"), lax.axis_size("grp")
    lines = size // along_z
    y, z = ctx // along_z, ctx % along_z
    part = w_ref.shape[0] // 2
    total, chans = gated.shape
    half = total // 2
    seqs, row_count = rows_ref.shape[0], rows_ref.shape[2]
    tiles = chans // LANES
    groups = filters_ref.shape[0] // tiles

    def at_z(step):
        return {"ctx": y * along_z + (z + along_z + step) % along_z}

    def at_y(step):
        return {"ctx": (y + lines + step) % lines * along_z + z}

    def at_x(step):
        return {"grp": (x + ring + step) % ring}

    def at_ctx(step):
        return {"ctx": (ctx + size + step) % size}

    partner = {"dp": 1 - core}
    barrier = pltpu.get_barrier_semaphore()
    greeted = (at_z(1), at_z(-1), at_y(1), at_y(-1), at_x(1), at_x(-1), at_ctx(1), at_ctx(-1), partner)
    for device in greeted:
        pl.semaphore_signal(barrier, inc=1, device_id=device, device_id_type=MESH)
    pl.semaphore_wait(barrier, len(greeted))

    def copy(src, dst, send, recv, device):
        return pltpu.make_async_remote_copy(
            src_ref=src, dst_ref=dst, send_sem=send, recv_sem=recv, device_id=device, device_id_type=MESH
        )

    started = []

    def go(*what):
        started.append(copy(*what))
        started[-1].start()

    def arrive(here, send, recv, device):
        copy(here, here, send, recv, device).wait_recv()

    def halo(n, src, dst, device):
        go(src, dst, halo_send.at[n], halo_recv.at[n], device)

    def halo_wait(n, here, device, edge):
        arrive(here, halo_send.at[n], halo_recv.at[n], device)

        @pl.when(ctx == edge)
        def _():
            here[...] = jnp.zeros(here.shape, here.dtype)

    def lanes_of(i):
        return pl.ds(pl.multiple_of(i * LANES, LANES), LANES)

    def lines_of(ref, i):
        return ref[pl.ds(pl.multiple_of(i * groups, groups), groups), :]

    def block(step_y, step_z, carrier):
        row = ((y + lines + step_y) % lines * along_z + (z + along_z + step_z) % along_z) * 2 + carrier
        return whole.at[pl.ds(pl.multiple_of(row * part, part), part), :]

    steps = [0]
    for k in range(1, along_z // 2):
        steps.append(k)
    for k in range(1, along_z // 2 + 1):
        steps.insert(2 if k == 1 else len(steps), -k)

    def hand_over(kind, step_y, u):
        place = kind * along_z + u
        mine = block(step_y, steps[u], core)
        go(mine, mine, pair_send.at[place], pair_recv.at[place], partner)

    def z_turn(u):
        mine = w_ref.at[pl.ds(pl.multiple_of(core * part, part), part), :]
        if u > 0:
            mine = block(0, steps[u], core)
            arrive(mine, z_send.at[u], z_recv.at[u], at_z(1))
        for direction in (-1, 1):
            onward = steps[u] + direction
            if onward in steps and (u == 0 or steps[u] * direction > 0):
                v = steps.index(onward)
                go(mine, block(0, steps[u], core), z_send.at[v], z_recv.at[v], at_z(-direction))
        go(mine, block(0, steps[u], core), up_send.at[u], up_recv.at[u], at_y(1))
        go(mine, block(0, steps[u], core), down_send.at[u], down_recv.at[u], at_y(-1))
        if u > 0:
            hand_over(0, 0, u)

    def y_turn(u):
        behind, ahead = block(-1, steps[u], core), block(1, steps[u], core)
        arrive(behind, up_send.at[u], up_recv.at[u], at_y(1))
        if u % 2 == 0:
            go(behind, behind, far_send.at[u], far_recv.at[u], at_y(1))
        hand_over(1, -1, u)
        arrive(ahead, down_send.at[u], down_recv.at[u], at_y(-1))
        if u % 2 == 1:
            go(ahead, ahead, far_send.at[u], far_recv.at[u], at_y(-1))
        hand_over(2, 1, u)

    def far_turn(u):
        arrive(block(2, steps[u], core), far_send.at[u], far_recv.at[u], at_y(1))
        hand_over(3, 2, u)

    pieces = [(b, s) for b in (1, 0) for s in range(seqs)]

    def flat_rows(b, s):
        return pl.ds((b * seqs + s) * BLOCK, BLOCK)

    def x_start(c):
        here = flat_rows(*pieces[c])
        src = gated.at[here, :]
        go(src, gathered.at[0, here, :], x_send.at[0, c], x_recv.at[0, c], at_x(1))
        go(src, gathered.at[1, here, :], x_send.at[1, c], x_recv.at[1, c], at_x(-1))

    def x_wait(slot, c):
        arrive(gathered.at[slot, flat_rows(*pieces[c]), :], x_send.at[slot, c], x_recv.at[slot, c], at_x(1))

    def x_turn(c):
        x_wait(0, c)
        x_wait(1, c)
        here = flat_rows(*pieces[c])
        slot, to = (0, at_x(1)) if c < len(pieces) // 2 else (1, at_x(-1))
        go(gathered.at[slot, here, :], gathered.at[2, here, :], x_send.at[2, c], x_recv.at[2, c], to)

    def mix_block(i, b):
        wide = jnp.dot(band[i], window_pair(product_ref, b * BLOCK, lanes_of(i)), preferred_element_type=F32)
        kept = own_group(wide, groups)
        for s in range(seqs):
            mixed = kept[:, s * LANES : (s + 1) * LANES]
            here = slice(b * BLOCK, (b + 1) * BLOCK)
            mixed_ref[s, here, lanes_of(i)] = mixed
            gated[flat_rows(b, s), lanes_of(i)] = (queries[s, here, lanes_of(i)] * mixed).astype(BF)

    def taps_of(i):
        return taps_ref[:, :, lanes_of(i)]

    def features_of(i, s, streams, count, at=0):
        found = []
        for stream in streams:
            if at == 0:
                before = front_ref[s, stream, :, lanes_of(i)]
            else:
                before = rows_ref[s, stream, at - HALO : at, lanes_of(i)]
            fill(scratch, before, rows_ref[s, stream, at : at + count, lanes_of(i)])
            taps, sum_ = taps_of(i), None
            for offset in range(taps.shape[1]):
                start = HALO - offset
                term = taps[stream, offset : offset + 1, :] * scratch[start : start + count, :]
                sum_ = term if sum_ is None else sum_ + term
            found.append(sum_)
        return found

    def features(i, at, count):
        for s in range(seqs):
            query, key, value = features_of(i, s, range(3), count, at)
            queries[s, at : at + count, lanes_of(i)] = query
            product_ref[s, BLOCK + at : BLOCK + at + count, lanes_of(i)] = (key * value).astype(BF)

    last = row_count - BLOCK

    def tails(i, carry):
        features(i, last, BLOCK)
        return carry

    def bands(i, carry):
        band_rows(behind_lines(lines_of(filters_ref, i)), band.at[i])
        return carry

    def forward(i, carry):
        features(i, 0, last)
        mix_block(i, 1)
        return carry

    def forward_first(i, carry):
        mix_block(i, 0)
        return carry

    halo(0, rows_ref.at[:, :, row_count - HALO :, :], front_ref, at_ctx(1))
    z_turn(0)
    lax.fori_loop(0, tiles, tails, 0)
    halo(1, product_ref.at[:, row_count:, :], product_ref.at[:, 0:BLOCK, :], at_ctx(1))
    lax.fori_loop(0, tiles, bands, 0)
    for b in range(row_count // BLOCK):
        for s in range(seqs):
            turned[flat_rows(b, s), :] = cotangent_ref[s, b * BLOCK : (b + 1) * BLOCK, :]
    for u in range(1, min(3, along_z)):
        z_turn(u)
    halo_wait(0, front_ref, at_ctx(1), 0)
    lax.fori_loop(0, tiles, forward, 0)
    x_start(0)
    x_start(1)
    whole[pl.ds(pl.multiple_of(ctx * 2 * part, 2 * part), 2 * part), :] = w_ref[...]

    def second_half():
        halo_wait(1, product_ref.at[:, 0:BLOCK, :], at_ctx(1), 0)
        lax.fori_loop(0, tiles, forward_first, 0)
        x_start(2)
        x_start(3)

    plan = []
    for u in range(along_z):
        plan += [(z_turn, u)] if u >= 3 else []
        plan += [(y_turn, u - 3)] if u >= 3 else []
        plan += [(far_turn, u - 4)] if u >= 4 else []
    plan.insert(min(len(plan), 9), (x_turn, 0))
    plan.insert(min(len(plan), 13), (second_half,))
    for u in range(max(along_z - 3, 0), along_z):
        plan += [(y_turn, u), (far_turn, u - 1)] if u > 0 else [(y_turn, u)]
        if u == along_z - 3:
            plan.append((x_turn, 1))
    plan += [(far_turn, along_z - 1), (x_turn, 2)]
    if along_z < 8:
        plan = [(second_half,)] + [(x_turn, c) for c in range(3)]
        plan += [(y_turn, u) for u in range(along_z)] + [(far_turn, u) for u in range(along_z)]
    for what, *which in plan:
        what(*which)
    for kind, step_y in enumerate((0, -1, 1, 2)):
        for u in range(1 if kind == 0 else 0, along_z):
            place = kind * along_z + u
            arrive(block(step_y, steps[u], 1 - core), pair_send.at[place], pair_recv.at[place], partner)

    wide = min(chans, 256)
    right, left, across = (x + 1) % ring, (x + ring - 1) % ring, (x + 2) % ring
    count = chans // wide

    def columns(j):
        return pl.ds(pl.multiple_of(j * wide, wide), wide)

    def partial(owner, j):
        rows = whole[pl.ds(pl.multiple_of(owner * chans + j * wide, wide), wide), :]
        return lax.dot_general(turned[...], rows, (((1,), (1,)), ((), ())), preferred_element_type=F32)

    def far_sums(j, carry):
        found = partial(across, j)
        to_a[:, columns(j)] = found[:half].astype(BF)
        to_b[:, columns(j)] = found[half:].astype(BF)
        return carry

    def near_sums(j, carry):
        found = partial(left, j)
        to_left[:half, columns(j)] = found[:half].astype(BF)
        kept_left[:, columns(j)] = found[half:]
        found = partial(right, j)
        kept_right[:, columns(j)] = found[:half]
        to_right[half:, columns(j)] = found[half:].astype(BF)
        return carry

    def own_sums(j, carry):
        own[:, columns(j)] = partial(x, j)
        return carry

    def outputs(j, carry):
        found = None
        for slot, owner in ((None, x), (0, left), (1, right), (2, across)):
            rows = whole[pl.ds(pl.multiple_of(owner * chans, chans), chans), columns(j)]
            source = gated[...] if slot is None else gathered[slot]
            term = jnp.dot(source, rows, preferred_element_type=F32)
            found = term if found is None else found + term
        for b in range(row_count // BLOCK):
            for s in range(seqs):
                at = (b * seqs + s) * BLOCK
                out_ref[s, b * BLOCK : (b + 1) * BLOCK, columns(j)] = found[at : at + BLOCK].astype(BF)
        return carry

    def piece(ref, at, n):
        return ref.at[pl.ds(at + n * BLOCK, BLOCK), :]

    def send_sum(n, src, dst, device):
        go(src, dst, sum_send.at[n], sum_recv.at[n], device)

    def wait_sum(n, here):
        arrive(here, sum_send.at[n], sum_recv.at[n], at_x(1))

    def relay_a(n):
        wait_sum(n, piece(from_a, 0, n))
        rows = slice(n * BLOCK, (n + 1) * BLOCK)
        to_right[rows, :] = (kept_right[rows, :] + from_a[rows, :].astype(F32)).astype(BF)
        send_sum(4 + n, piece(to_right, 0, n), piece(from_left, 0, n), at_x(1))

    def relay_b(n):
        wait_sum(2 + n, piece(from_b, 0, n))
        rows, there = slice(n * BLOCK, (n + 1) * BLOCK), slice(half + n * BLOCK, half + (n + 1) * BLOCK)
        to_left[there, :] = (kept_left[rows, :] + from_b[rows, :].astype(F32)).astype(BF)
        send_sum(6 + n, piece(to_left, half, n), piece(from_right, half, n), at_x(-1))

    first, second = pl.ds(0, half), pl.ds(half, half)
    lax.fori_loop(0, count, far_sums, 0)
    x_turn(3)
    for n in range(2):
        send_sum(n, piece(to_a, 0, n), piece(from_a, 0, n), at_x(1))
        send_sum(2 + n, piece(to_b, 0, n), piece(from_b, 0, n), at_x(-1))
    lax.fori_loop(0, count, near_sums, 0)
    send_sum(8, to_left.at[first, :], from_right.at[first, :], at_x(-1))
    relay_a(0)
    lax.fori_loop(0, count, own_sums, 0)
    relay_a(1)
    send_sum(9, to_right.at[second, :], from_left.at[second, :], at_x(1))
    relay_b(0)
    relay_b(1)
    for c in range(len(pieces)):
        x_wait(2, c)
    lax.fori_loop(0, count, outputs, 0)

    def finish(b):
        for s in range(seqs):
            at = slice((b * seqs + s) * BLOCK, (b * seqs + s + 1) * BLOCK)
            here = slice(b * BLOCK, (b + 1) * BLOCK)
            found = own[at, :] + (from_left[at, :].astype(F32) + from_right[at, :].astype(F32))
            found = found.astype(BF)
            grad_ref[s, here, :] = found
            mix_ref[s, here, :] = (found.astype(F32) * queries[s, here, :]).astype(BF)

    def low_bands(i, carry):
        band_rows(ahead_lines(lines_of(filters_ref, i)), low_band.at[i], HALO)
        return carry

    lax.fori_loop(0, tiles, low_bands, 0)
    wait_sum(8, from_right.at[first, :])
    for n in range(2):
        wait_sum(4 + n, piece(from_left, 0, n))
    finish(0)
    halo(2, mix_ref.at[:, 0:BLOCK, :], mix_ref.at[:, row_count:, :], at_ctx(-1))
    wait_sum(9, from_left.at[second, :])
    for n in range(2):
        wait_sum(6 + n, piece(from_right, half, n))
    finish(1)

    def heads(i, carry):
        low = jnp.dot(low_band[i], window_pair(mix_ref, 0, lanes_of(i)), preferred_element_type=F32)
        pulled = own_group(low, groups, HALO)
        for s in range(seqs):
            here = pulled[:, s * LANES : (s + 1) * LANES]
            key, value = features_of(i, s, (1, 2), HALO)
            grad = grad_ref[s, 0:HALO, lanes_of(i)].astype(F32)
            head[s, 0, :, lanes_of(i)] = (grad * mixed_ref[s, 0:HALO, lanes_of(i)]).astype(BF)
            head[s, 1, :, lanes_of(i)] = (here * value).astype(BF)
            head[s, 2, :, lanes_of(i)] = (here * key).astype(BF)
        return carry

    lax.fori_loop(0, tiles, heads, 0)
    halo(3, head, later_ref, at_ctx(-1))
    halo_wait(2, mix_ref.at[:, row_count:, :], at_ctx(-1), size - 1)
    halo_wait(3, later_ref, at_ctx(-1), size - 1)
    for sent in started:
        sent.wait_send()


def exchange(out_w, rows, short_w, medium_h, grad_out):
    seqs, row_count, chans = grad_out.shape
    total = seqs * row_count
    depth = out_w.shape[0] * lax.axis_size("ctx")
    tiles = chans // LANES
    groups = medium_h.shape[0] // tiles
    half = (total // 2, chans)
    dma = pltpu.SemaphoreType.DMA
    flops = 4 * total * depth * chans
    padded = (seqs, row_count + BLOCK, chans)
    edge = (seqs, 3, HALO, chans)
    shape = jax.ShapeDtypeStruct
    return pl.pallas_call(
        functools.partial(exchange_kernel, ALONG_Z),
        out_shape=[
            shape(grad_out.shape, BF), shape(grad_out.shape, BF), shape(grad_out.shape, F32),
            shape(padded, BF), shape(padded, BF), shape(edge, BF), shape(edge, BF),
        ],
        in_specs=[pl.BlockSpec(memory_space=pltpu.VMEM)] * 5,
        out_specs=[pl.BlockSpec(memory_space=pltpu.VMEM)] * 7,
        scratch_shapes=[
            pltpu.VMEM((depth, chans), BF),
            pltpu.VMEM((total, chans), BF),
            pltpu.VMEM((3, total, chans), BF),
            pltpu.VMEM((total, chans), BF),
            pltpu.VMEM((seqs, row_count, chans), F32),
        ]
        + [pltpu.VMEM(half, BF)] * 4
        + [pltpu.VMEM((total, chans), BF)] * 4
        + [pltpu.VMEM(half, F32)] * 2
        + [
            pltpu.VMEM((total, chans), F32),
            pltpu.VMEM(edge, BF),
            pltpu.VMEM((row_count + HALO, LANES), F32),
            pltpu.VMEM((tiles, groups * BLOCK, 2 * BLOCK), BF),
            pltpu.VMEM((tiles, groups * HALO, 2 * BLOCK), BF),
        ]
        + [dma((ALONG_Z,))] * 8
        + [dma((4 * ALONG_Z,))] * 2
        + [dma((3, 4))] * 2
        + [dma((10,))] * 2
        + [dma((4,))] * 2,
        cost_estimate=pl.CostEstimate(flops=flops, bytes_accessed=8 * total * chans, transcendentals=0),
        compiler_params=pltpu.CompilerParams(
            collective_id=2, has_side_effects=True, vmem_limit_bytes=58 << 20
        ),
    )(out_w, rows, short_w, medium_h, grad_out)


def tiled(kernel, ins, outs, scratch, arrays, tiles, flops=0):
    read = sum(math.prod(a.shape) * a.dtype.itemsize for a in arrays)
    return pl.pallas_call(
        kernel,
        grid=(tiles,),
        in_specs=[pl.BlockSpec(block, index) for block, index in ins],
        out_specs=[pl.BlockSpec(block, index) for block, index, _, _ in outs],
        out_shape=[jax.ShapeDtypeStruct(shape, kind) for _, _, shape, kind in outs],
        scratch_shapes=scratch,
        cost_estimate=pl.CostEstimate(flops=flops, bytes_accessed=read, transcendentals=0),
        compiler_params=pltpu.CompilerParams(vmem_limit_bytes=60 << 20),
    )(*arrays)


def shards(projected, short_w, medium_h, out_w, grad_out):
    seqs, row_count, _, chans = projected.shape
    taps = medium_h.shape[1]
    groups_here = medium_h.shape[0]
    tiles = chans // LANES
    groups = groups_here // tiles
    rows = jnp.swapaxes(projected, 1, 2)

    lane3 = lambda i: (0, 0, i)
    lane4 = lambda i: (0, 0, 0, i)
    front_spec = ((seqs, 3, HALO, LANES), lane4)
    rows_spec = ((seqs, 3, row_count, LANES), lane4)
    taps_spec = ((3, short_w.shape[1], LANES), lane3)
    filters_spec = ((groups_here, taps), lambda i: (0, 0))
    full_spec = ((seqs, row_count, LANES), lane3)
    line_rows = pltpu.VMEM((row_count + HALO, LANES), F32)
    padded_spec = ((seqs, row_count + BLOCK, LANES), lane3)
    bands = pltpu.VMEM((groups * BLOCK, 2 * BLOCK), BF)

    block_out, cotangent, mixed, product, mix, front, later = exchange(
        out_w, rows, short_w, medium_h, grad_out
    )
    grad, short_part, filter_part = tiled(
        backward_kernel,
        [full_spec, front_spec, rows_spec, taps_spec, filters_spec, full_spec, padded_spec, padded_spec, front_spec],
        [
            (*rows_spec, rows.shape, BF),
            ((1, SUM_ROWS, LANES), lambda i: (i, 0, 0), (tiles, SUM_ROWS, LANES), F32),
            ((groups, LANES), lambda i: (i, 0), (groups_here, taps), F32),
        ],
        [line_rows, pltpu.VMEM((seqs, row_count, LANES), F32), line_rows, bands],
        (cotangent, front, rows, short_w, medium_h, mixed, mix, product, later),
        tiles,
    )

    seq_total = seqs * lax.axis_size("dp")
    length_total = row_count * lax.axis_size("ctx")
    scales = (
        1.0 / math.sqrt(seq_total * length_total * (LANES // groups)),
        1.0 / math.sqrt(seq_total * length_total),
    )
    sum_rows = groups_here + tiles * SUM_ROWS
    peers = 2 * (lax.axis_size("ctx") // ALONG_Z)
    piece = (sum_rows // peers, LANES)
    filter_grad, short_grad = pl.pallas_call(
        functools.partial(reduce_kernel, ALONG_Z, scales),
        out_shape=[jax.ShapeDtypeStruct((groups_here, taps), F32), jax.ShapeDtypeStruct(short_w.shape, F32)],
        in_specs=[pl.BlockSpec(memory_space=pltpu.VMEM)] * 2,
        out_specs=[pl.BlockSpec(memory_space=pltpu.VMEM)] * 2,
        scratch_shapes=[
            pltpu.VMEM((sum_rows, LANES), F32),
            pltpu.VMEM((peers, *piece), F32),
            pltpu.VMEM(piece, F32),
            pltpu.VMEM((ALONG_Z, *piece), F32),
            pltpu.VMEM(piece, F32),
            pltpu.VMEM((sum_rows, LANES), F32),
        ]
        + [pltpu.SemaphoreType.DMA((8,))] * 6,
        compiler_params=pltpu.CompilerParams(collective_id=1, has_side_effects=True),
    )(filter_part, short_part)
    return (block_out, jnp.swapaxes(grad, 1, 2), filter_grad, short_grad)


def solution(mesh):
    in_specs = (
        P("dp", "ctx", None, "grp"),
        P(None, None, "grp"),
        P("grp", None),
        P("ctx", "grp"),
        P("dp", "ctx", "grp"),
    )
    out_specs = (
        P("dp", "ctx", "grp"),
        P("dp", "ctx", None, "grp"),
        P("grp", None),
        P(None, None, "grp"),
    )
    return jax.shard_map(shards, mesh=mesh, in_specs=in_specs, out_specs=out_specs, check_vma=False)
```

```python
import functools
import math

import jax
import jax.numpy as jnp
from jax import lax
from jax.experimental import pallas as pl
from jax.experimental.pallas import tpu as pltpu
from jax.sharding import PartitionSpec as P

BF = jnp.bfloat16
F32 = jnp.float32
LANES = 128
BLOCK = 128
HALO = 8
SUM_ROWS = 16
MESH = pl.DeviceIdType.MESH
ALONG_Z = 8


def fill(scratch, front, rows):
    scratch[0:HALO, :] = front.astype(F32)
    scratch[HALO : HALO + rows.shape[0], :] = rows.astype(F32)


def feature(scratch, taps, stream, count):
    total = None
    for offset in range(taps.shape[1]):
        start = HALO - offset
        term = taps[stream, offset : offset + 1, :] * scratch[start : start + count, :]
        total = term if total is None else total + term
    return total


def ahead_lines(filters):
    return jnp.concatenate([filters.astype(F32), jnp.zeros(filters.shape, F32)], axis=1)


def behind_lines(filters):
    taps = filters.shape[1]
    row = lax.broadcasted_iota(jnp.int32, (taps, 2 * BLOCK), 0)
    column = lax.broadcasted_iota(jnp.int32, (taps, 2 * BLOCK), 1)
    return jnp.dot(filters, (row + column == BLOCK).astype(BF), preferred_element_type=F32)


def band_rows(lines, band, count=BLOCK):
    groups = lines.shape[0]
    for g in range(groups):
        line = jnp.broadcast_to(lines[g : g + 1, :], (count, lines.shape[1]))
        turned = pltpu.roll(line, 0, 1, stride=1, stride_axis=0)
        band[g * count : (g + 1) * count, :] = turned.astype(BF)


def group_of_lane(shape, groups):
    lane = lax.broadcasted_iota(jnp.int32, shape, len(shape) - 1)
    return (lane % LANES) // (LANES // groups)


def own_group(wide, groups, count=BLOCK):
    owner = group_of_lane((count, wide.shape[1]), groups)
    kept = wide[0:count]
    for g in range(1, groups):
        kept = jnp.where(owner == g, wide[g * count : (g + 1) * count], kept)
    return kept


def window_pair(padded, start, lanes=slice(None)):
    return jnp.concatenate(
        [padded[s, start : start + 2 * BLOCK, lanes] for s in range(padded.shape[0])], axis=1
    )


def filter_sums(grads, windows, groups):
    rows = lax.broadcasted_iota(jnp.int32, (2 * BLOCK, 2 * BLOCK), 0)
    columns = lax.broadcasted_iota(jnp.int32, (2 * BLOCK, 2 * BLOCK), 1)
    upturn = (rows + columns == 2 * BLOCK - 1).astype(BF)
    windows = jnp.dot(upturn, windows, preferred_element_type=F32).astype(BF)
    owner = group_of_lane(grads.shape, groups)
    wide = grads.astype(F32)
    stacked = jnp.concatenate(
        [jnp.where(owner == g, wide, 0.0).astype(BF) for g in range(groups)], axis=0
    )
    lags = lax.dot_general(
        stacked, windows, (((1,), (1,)), ((), ())), preferred_element_type=F32
    )
    found = []
    for g in range(groups):
        turned = pltpu.roll(lags[g * BLOCK : (g + 1) * BLOCK], 0, 1, stride=1, stride_axis=0)
        found.append(jnp.sum(turned, axis=0, keepdims=True))
    return pltpu.roll(jnp.concatenate(found, axis=0), BLOCK + 1, 1)[:, :BLOCK]


def backward_kernel(
    cotangent_ref, front_ref, rows_ref, taps_ref, filters_ref, mixed_ref,
    padded_ref, next_ref, grad_ref, short_ref, scratch, pulled, later, band,
):
    seqs, row_count = rows_ref.shape[0], rows_ref.shape[2]
    groups = band.shape[0] // BLOCK
    taps = taps_ref.shape[1]
    first = pl.multiple_of(pl.program_id(0) * groups, groups)
    band_rows(ahead_lines(filters_ref[pl.ds(first, groups), :]), band)
    for b in range(row_count // BLOCK):
        wide = jnp.dot(
            band[...], window_pair(padded_ref, b * BLOCK), preferred_element_type=F32
        )
        kept = own_group(wide, groups)
        for s in range(seqs):
            pulled[s, b * BLOCK : (b + 1) * BLOCK, :] = kept[:, s * LANES : (s + 1) * LANES]
    sums = [None] * (3 * taps)
    for s in range(seqs):
        for stream in range(3):
            if stream == 0:
                grad = cotangent_ref[s].astype(F32) * mixed_ref[s]
            else:
                other = 3 - stream
                fill(scratch, front_ref[s, other], rows_ref[s, other])
                grad = pulled[s] * feature(scratch, taps_ref, other, row_count)
            grad = grad.astype(BF).astype(F32)
            fill(scratch, front_ref[s, stream], rows_ref[s, stream])
            later[0:row_count, :] = grad
            later[row_count : row_count + HALO, :] = next_ref[s, stream].astype(F32)
            total = None
            for offset in range(taps):
                term = taps_ref[stream, offset : offset + 1, :] * later[offset : offset + row_count, :]
                total = term if total is None else total + term
                at = HALO - offset
                found = jnp.sum(grad * scratch[at : at + row_count, :], axis=0, keepdims=True)
                row = stream * taps + offset
                sums[row] = found if sums[row] is None else sums[row] + found
            grad_ref[s, stream] = total.astype(BF)
    short_ref[...] = jnp.zeros_like(short_ref)
    for row in range(3 * taps):
        short_ref[0, row : row + 1, :] = sums[row]


def reduce_kernel(
    along_z, scales, filter_ref, short_ref, filter_out, short_out,
    packed, mine_of, part, gathered, whole, result, zs, zr, ys, yr, os, orr,
):
    me, core = lax.axis_index("ctx"), lax.axis_index("dp")
    line, place = me // along_z, me % along_z
    lines = lax.axis_size("ctx") // along_z
    peers = lines * 2
    mine = line * 2 + core
    depth = packed.shape[0] // peers
    tiles, width = short_ref.shape[0], packed.shape[0] // short_ref.shape[0]
    groups = width - short_ref.shape[1]

    def along(step):
        return {"ctx": line * along_z + (place + step) % along_z}

    def across(step):
        other = (mine + step) % peers
        return {"ctx": (other // 2) * along_z + place, "dp": other % 2}

    barrier = pltpu.get_barrier_semaphore()
    for step in range(1, along_z):
        pl.semaphore_signal(barrier, inc=1, device_id=along(step), device_id_type=MESH)
    for step in range(1, peers):
        pl.semaphore_signal(barrier, inc=1, device_id=across(step), device_id_type=MESH)
    for k in range(tiles):
        packed[k * width : k * width + groups, :] = filter_ref[k * groups : (k + 1) * groups, :]
        packed[k * width + groups : (k + 1) * width, :] = short_ref[k]
    pl.semaphore_wait(barrier, along_z + peers - 2)

    def rows_of(piece):
        return pl.ds(pl.multiple_of(piece * depth, depth), depth)

    def first(step):
        return pltpu.make_async_remote_copy(
            src_ref=packed.at[rows_of((mine + step) % peers), :], dst_ref=mine_of.at[mine],
            send_sem=zs.at[step], recv_sem=zr.at[step],
            device_id=across(step), device_id_type=MESH,
        )

    def second(step):
        return pltpu.make_async_remote_copy(
            src_ref=part, dst_ref=gathered.at[place], send_sem=ys.at[step], recv_sem=yr.at[step],
            device_id=along(step), device_id_type=MESH,
        )

    def third(step):
        return pltpu.make_async_remote_copy(
            src_ref=whole, dst_ref=result.at[rows_of(mine), :], send_sem=os.at[step], recv_sem=orr.at[step],
            device_id=across(step), device_id_type=MESH,
        )

    for step in range(1, peers):
        first(step).start()
    mine_of[mine] = packed[rows_of(mine), :]
    for step in range(1, peers):
        first(step).wait_recv()
    total = mine_of[0]
    for k in range(1, peers):
        total = total + mine_of[k]
    part[...] = total
    for step in range(1, along_z):
        second(step).start()
    gathered[place] = total
    for step in range(1, along_z):
        second(step).wait_recv()
    total = gathered[0]
    for k in range(1, along_z):
        total = total + gathered[k]
    whole[...] = total
    for step in range(1, peers):
        third(step).start()
    result[rows_of(mine), :] = total
    for step in range(1, peers):
        third(step).wait_recv()
    taps = short_out.shape[1]
    for k in range(tiles):
        at = k * width
        filter_out[k * groups : (k + 1) * groups, :] = result[at : at + groups, :] * scales[0]
        at += groups
        for stream in range(3):
            rows = result[at + stream * taps : at + (stream + 1) * taps, :]
            short_out[stream, :, k * LANES : (k + 1) * LANES] = rows * scales[1]
    for step in range(1, peers):
        first(step).wait_send()
        third(step).wait_send()
    for step in range(1, along_z):
        second(step).wait_send()


def exchange_kernel(
    along_z, w_ref, rows_ref, taps_ref, filters_ref, cotangent_ref,
    out_ref, grad_ref, mixed_ref, mix_ref, front_ref, later_ref, sums_ref,
    product_ref, whole, gated, gathered, turned, queries, to_a, to_b, from_a, from_b,
    to_right, to_left, from_left, from_right, kept_right, kept_left, own, head,
    scratch, band, low_band,
    z_send, z_recv, up_send, up_recv, down_send, down_recv, far_send, far_recv,
    pair_send, pair_recv, x_send, x_recv, sum_send, sum_recv, halo_send, halo_recv,
):
    ctx, core, x = lax.axis_index("ctx"), lax.axis_index("dp"), lax.axis_index("grp")
    size, ring = lax.axis_size("ctx"), lax.axis_size("grp")
    lines = size // along_z
    y, z = ctx // along_z, ctx % along_z
    edge = jnp.where((z + 1) % along_z < 2, 1, 0)
    part = w_ref.shape[0] // 2
    total, chans = gated.shape
    half = total // 2
    seqs, row_count = rows_ref.shape[0], rows_ref.shape[2]
    tiles = chans // LANES
    groups = filters_ref.shape[0] // tiles

    def at_z(step):
        return {"ctx": y * along_z + (z + along_z + step) % along_z}

    def at_y(step):
        return {"ctx": (y + lines + step) % lines * along_z + z}

    def at_x(step):
        return {"grp": (x + ring + step) % ring}

    def at_ctx(step):
        return {"ctx": (ctx + size + step) % size}

    partner = {"dp": 1 - core}
    barrier = pltpu.get_barrier_semaphore()
    greeted = (at_z(1), at_z(-1), at_y(1), at_y(-1), at_x(1), at_x(-1), at_ctx(1), at_ctx(-1), partner)
    for device in greeted:
        pl.semaphore_signal(barrier, inc=1, device_id=device, device_id_type=MESH)
    pl.semaphore_wait(barrier, len(greeted))

    def copy(src, dst, send, recv, device):
        return pltpu.make_async_remote_copy(
            src_ref=src, dst_ref=dst, send_sem=send, recv_sem=recv, device_id=device, device_id_type=MESH
        )

    started = []

    def go(*what):
        started.append(copy(*what))
        started[-1].start()

    def arrive(here, send, recv, device):
        copy(here, here, send, recv, device).wait_recv()

    def halo(n, src, dst, device):
        go(src, dst, halo_send.at[n], halo_recv.at[n], device)

    def halo_wait(n, here, device, edge):
        arrive(here, halo_send.at[n], halo_recv.at[n], device)

        @pl.when(ctx == edge)
        def _():
            here[...] = jnp.zeros(here.shape, here.dtype)

    def lanes_of(i):
        return pl.ds(pl.multiple_of(i * LANES, LANES), LANES)

    def lines_of(ref, i):
        return ref[pl.ds(pl.multiple_of(i * groups, groups), groups), :]

    def block(step_y, step_z, carrier):
        row = ((y + lines + step_y) % lines * along_z + (z + along_z + step_z) % along_z) * 2 + carrier
        return whole.at[pl.ds(pl.multiple_of(row * part, part), part), :]

    steps = [0]
    for k in range(1, along_z // 2):
        steps.append(k)
    for k in range(1, along_z // 2 + 1):
        steps.insert(2 if k == 1 else len(steps), -k)

    def hand_over(kind, step_y, u):
        place = kind * along_z + u
        mine = block(step_y, steps[u], core)
        go(mine, mine, pair_send.at[place], pair_recv.at[place], partner)

    def z_turn(u):
        mine = w_ref.at[pl.ds(pl.multiple_of(core * part, part), part), :]
        if u > 0:
            mine = block(0, steps[u], core)
            arrive(mine, z_send.at[u], z_recv.at[u], at_z(1))
        for direction in (-1, 1):
            onward = steps[u] + direction
            if onward in steps and (u == 0 or steps[u] * direction > 0):
                v = steps.index(onward)
                go(mine, block(0, steps[u], core), z_send.at[v], z_recv.at[v], at_z(-direction))
        go(mine, block(0, steps[u], core), up_send.at[u], up_recv.at[u], at_y(1))
        go(mine, block(0, steps[u], core), down_send.at[u], down_recv.at[u], at_y(-1))
        if u > 0:
            hand_over(0, 0, u)

    def y_turn(u):
        behind, ahead = block(-1, steps[u], core), block(1, steps[u], core)
        arrive(behind, up_send.at[u], up_recv.at[u], at_y(1))
        hand_over(1, -1, u)
        arrive(ahead, down_send.at[u], down_recv.at[u], at_y(-1))
        hand_over(2, 1, u)
        up = 1 if u % 2 == 0 else -1
        if u % 4 == 0:
            up = 1 - 2 * edge
        onward = block(-up, steps[u], core)
        go(onward, onward, far_send.at[u], far_recv.at[u], at_y(up))

    def far_turn(u):
        arrive(block(2, steps[u], core), far_send.at[u], far_recv.at[u], at_y(1))
        hand_over(3, 2, u)

    pieces = [(b, s) for b in (1, 0) for s in range(seqs)]

    def flat_rows(b, s):
        return pl.ds((b * seqs + s) * BLOCK, BLOCK)

    def x_start(c):
        here = flat_rows(*pieces[c])
        src = gated.at[here, :]
        go(src, gathered.at[0, here, :], x_send.at[0, c], x_recv.at[0, c], at_x(1))
        go(src, gathered.at[1, here, :], x_send.at[1, c], x_recv.at[1, c], at_x(-1))

    def x_wait(slot, c):
        arrive(gathered.at[slot, flat_rows(*pieces[c]), :], x_send.at[slot, c], x_recv.at[slot, c], at_x(1))

    def x_turn(c):
        x_wait(0, c)
        x_wait(1, c)
        here = flat_rows(*pieces[c])
        slot, to = (0, at_x(1)) if c < len(pieces) // 2 else (1, at_x(-1))
        go(gathered.at[slot, here, :], gathered.at[2, here, :], x_send.at[2, c], x_recv.at[2, c], to)

    def mix_block(i, b):
        wide = jnp.dot(band[i], window_pair(product_ref, b * BLOCK, lanes_of(i)), preferred_element_type=F32)
        kept = own_group(wide, groups)
        for s in range(seqs):
            mixed = kept[:, s * LANES : (s + 1) * LANES]
            here = slice(b * BLOCK, (b + 1) * BLOCK)
            mixed_ref[s, here, lanes_of(i)] = mixed
            gated[flat_rows(b, s), lanes_of(i)] = (queries[s, here, lanes_of(i)] * mixed).astype(BF)

    def taps_of(i):
        return taps_ref[:, :, lanes_of(i)]

    def features_of(i, s, streams, count, at=0):
        found = []
        for stream in streams:
            if at == 0:
                before = front_ref[s, stream, :, lanes_of(i)]
            else:
                before = rows_ref[s, stream, at - HALO : at, lanes_of(i)]
            fill(scratch, before, rows_ref[s, stream, at : at + count, lanes_of(i)])
            taps, sum_ = taps_of(i), None
            for offset in range(taps.shape[1]):
                start = HALO - offset
                term = taps[stream, offset : offset + 1, :] * scratch[start : start + count, :]
                sum_ = term if sum_ is None else sum_ + term
            found.append(sum_)
        return found

    def features(i, at, count):
        for s in range(seqs):
            query, key, value = features_of(i, s, range(3), count, at)
            queries[s, at : at + count, lanes_of(i)] = query
            product_ref[s, BLOCK + at : BLOCK + at + count, lanes_of(i)] = (key * value).astype(BF)

    last = row_count - BLOCK

    def tails(i, carry):
        features(i, last, BLOCK)
        return carry

    def bands(i, carry):
        band_rows(behind_lines(lines_of(filters_ref, i)), band.at[i])
        return carry

    def forward(i, carry):
        features(i, 0, last)
        mix_block(i, 1)
        return carry

    def forward_first(i, carry):
        mix_block(i, 0)
        return carry

    halo(0, rows_ref.at[:, :, row_count - HALO :, :], front_ref, at_ctx(1))
    z_turn(0)
    lax.fori_loop(0, tiles, tails, 0)
    halo(1, product_ref.at[:, row_count:, :], product_ref.at[:, 0:BLOCK, :], at_ctx(1))
    lax.fori_loop(0, tiles, bands, 0)
    for b in range(row_count // BLOCK):
        for s in range(seqs):
            turned[flat_rows(b, s), :] = cotangent_ref[s, b * BLOCK : (b + 1) * BLOCK, :]
    for u in range(1, min(3, along_z)):
        z_turn(u)
    halo_wait(0, front_ref, at_ctx(1), 0)
    lax.fori_loop(0, tiles, forward, 0)
    x_start(0)
    x_start(1)
    whole[pl.ds(pl.multiple_of(ctx * 2 * part, 2 * part), 2 * part), :] = w_ref[...]

    def second_half():
        halo_wait(1, product_ref.at[:, 0:BLOCK, :], at_ctx(1), 0)
        lax.fori_loop(0, tiles, forward_first, 0)
        x_start(2)
        x_start(3)

    plan = []
    for u in range(along_z):
        plan += [(z_turn, u)] if u >= 3 else []
        plan += [(y_turn, u - 3)] if u >= 3 else []
        plan += [(far_turn, u - 4)] if u >= 4 else []
    plan.insert(min(len(plan), 9), (x_turn, 0))
    plan.insert(min(len(plan), 13), (second_half,))
    for u in range(max(along_z - 3, 0), along_z):
        plan += [(y_turn, u), (far_turn, u - 1)] if u > 0 else [(y_turn, u)]
        if u == along_z - 3:
            plan.append((x_turn, 1))
    plan += [(far_turn, along_z - 1), (x_turn, 2)]
    if along_z < 8:
        plan = [(second_half,)] + [(x_turn, c) for c in range(3)]
        plan += [(y_turn, u) for u in range(along_z)] + [(far_turn, u) for u in range(along_z)]
    for what, *which in plan:
        what(*which)
    for kind, step_y in enumerate((0, -1, 1, 2)):
        for u in range(1 if kind == 0 else 0, along_z):
            place = kind * along_z + u
            arrive(block(step_y, steps[u], 1 - core), pair_send.at[place], pair_recv.at[place], partner)

    wide = min(chans, 256)
    right, left, across = (x + 1) % ring, (x + ring - 1) % ring, (x + 2) % ring
    count = chans // wide

    def columns(j):
        return pl.ds(pl.multiple_of(j * wide, wide), wide)

    def partial(owner, j):
        rows = whole[pl.ds(pl.multiple_of(owner * chans + j * wide, wide), wide), :]
        return lax.dot_general(turned[...], rows, (((1,), (1,)), ((), ())), preferred_element_type=F32)

    def far_sums(j, carry):
        found = partial(across, j)
        to_a[:, columns(j)] = found[:half].astype(BF)
        to_b[:, columns(j)] = found[half:].astype(BF)
        return carry

    def near_sums(j, carry):
        found = partial(left, j)
        to_left[:half, columns(j)] = found[:half].astype(BF)
        kept_left[:, columns(j)] = found[half:]
        found = partial(right, j)
        kept_right[:, columns(j)] = found[:half]
        to_right[half:, columns(j)] = found[half:].astype(BF)
        return carry

    def own_sums(j, carry):
        own[:, columns(j)] = partial(x, j)
        return carry

    def outputs(j, carry):
        found = None
        for slot, owner in ((None, x), (0, left), (1, right), (2, across)):
            rows = whole[pl.ds(pl.multiple_of(owner * chans, chans), chans), columns(j)]
            source = gated[...] if slot is None else gathered[slot]
            term = jnp.dot(source, rows, preferred_element_type=F32)
            found = term if found is None else found + term
        for b in range(row_count // BLOCK):
            for s in range(seqs):
                at = (b * seqs + s) * BLOCK
                out_ref[s, b * BLOCK : (b + 1) * BLOCK, columns(j)] = found[at : at + BLOCK].astype(BF)
        return carry

    def piece(ref, at, n):
        return ref.at[pl.ds(at + n * BLOCK, BLOCK), :]

    def send_sum(n, src, dst, device):
        go(src, dst, sum_send.at[n], sum_recv.at[n], device)

    def wait_sum(n, here):
        arrive(here, sum_send.at[n], sum_recv.at[n], at_x(1))

    def relay_a(n):
        wait_sum(n, piece(from_a, 0, n))
        rows = slice(n * BLOCK, (n + 1) * BLOCK)
        to_right[rows, :] = (kept_right[rows, :] + from_a[rows, :].astype(F32)).astype(BF)
        send_sum(4 + n, piece(to_right, 0, n), piece(from_left, 0, n), at_x(1))

    def relay_b(n):
        wait_sum(2 + n, piece(from_b, 0, n))
        rows, there = slice(n * BLOCK, (n + 1) * BLOCK), slice(half + n * BLOCK, half + (n + 1) * BLOCK)
        to_left[there, :] = (kept_left[rows, :] + from_b[rows, :].astype(F32)).astype(BF)
        send_sum(6 + n, piece(to_left, half, n), piece(from_right, half, n), at_x(-1))

    first, second = pl.ds(0, half), pl.ds(half, half)
    lax.fori_loop(0, count, far_sums, 0)
    x_turn(3)
    for n in range(2):
        send_sum(n, piece(to_a, 0, n), piece(from_a, 0, n), at_x(1))
        send_sum(2 + n, piece(to_b, 0, n), piece(from_b, 0, n), at_x(-1))
    lax.fori_loop(0, count, near_sums, 0)
    send_sum(8, to_left.at[first, :], from_right.at[first, :], at_x(-1))
    relay_a(0)
    lax.fori_loop(0, count, own_sums, 0)
    relay_a(1)
    send_sum(9, to_right.at[second, :], from_left.at[second, :], at_x(1))
    relay_b(0)
    relay_b(1)
    for c in range(len(pieces)):
        x_wait(2, c)
    lax.fori_loop(0, count, outputs, 0)

    def finish(b):
        for s in range(seqs):
            at = slice((b * seqs + s) * BLOCK, (b * seqs + s + 1) * BLOCK)
            here = slice(b * BLOCK, (b + 1) * BLOCK)
            found = own[at, :] + (from_left[at, :].astype(F32) + from_right[at, :].astype(F32))
            found = found.astype(BF)
            grad_ref[s, here, :] = found
            mix_ref[s, here, :] = (found.astype(F32) * queries[s, here, :]).astype(BF)

    def low_bands(i, carry):
        band_rows(ahead_lines(lines_of(filters_ref, i)), low_band.at[i], HALO)
        return carry

    lax.fori_loop(0, tiles, low_bands, 0)
    wait_sum(8, from_right.at[first, :])
    for n in range(2):
        wait_sum(4 + n, piece(from_left, 0, n))
    finish(0)
    halo(2, mix_ref.at[:, 0:BLOCK, :], mix_ref.at[:, row_count:, :], at_ctx(-1))

    def block_sums(i, b):
        grads = [mix_ref[s, b * BLOCK : (b + 1) * BLOCK, lanes_of(i)] for s in range(seqs)]
        windows = window_pair(product_ref, b * BLOCK, lanes_of(i))
        return filter_sums(jnp.concatenate(grads, axis=1), windows, groups)

    def sums_of(i):
        return pl.ds(pl.multiple_of(i * groups, groups), groups)

    def first_sums(i, carry):
        sums_ref[sums_of(i), :] = block_sums(i, 0)
        return carry

    def second_sums(i, carry):
        sums_ref[sums_of(i), :] += block_sums(i, 1)
        return carry

    lax.fori_loop(0, tiles, first_sums, 0)
    wait_sum(9, from_left.at[second, :])
    for n in range(2):
        wait_sum(6 + n, piece(from_right, half, n))
    finish(1)

    def heads(i, carry):
        low = jnp.dot(low_band[i], window_pair(mix_ref, 0, lanes_of(i)), preferred_element_type=F32)
        pulled = own_group(low, groups, HALO)
        for s in range(seqs):
            here = pulled[:, s * LANES : (s + 1) * LANES]
            key, value = features_of(i, s, (1, 2), HALO)
            grad = grad_ref[s, 0:HALO, lanes_of(i)].astype(F32)
            head[s, 0, :, lanes_of(i)] = (grad * mixed_ref[s, 0:HALO, lanes_of(i)]).astype(BF)
            head[s, 1, :, lanes_of(i)] = (here * value).astype(BF)
            head[s, 2, :, lanes_of(i)] = (here * key).astype(BF)
        return carry

    lax.fori_loop(0, tiles, heads, 0)
    halo(3, head, later_ref, at_ctx(-1))
    lax.fori_loop(0, tiles, second_sums, 0)
    halo_wait(2, mix_ref.at[:, row_count:, :], at_ctx(-1), size - 1)
    halo_wait(3, later_ref, at_ctx(-1), size - 1)
    for sent in started:
        sent.wait_send()


def exchange(out_w, rows, short_w, medium_h, grad_out):
    seqs, row_count, chans = grad_out.shape
    total = seqs * row_count
    depth = out_w.shape[0] * lax.axis_size("ctx")
    tiles = chans // LANES
    groups = medium_h.shape[0] // tiles
    half = (total // 2, chans)
    dma = pltpu.SemaphoreType.DMA
    flops = 4 * total * depth * chans
    padded = (seqs, row_count + BLOCK, chans)
    edge = (seqs, 3, HALO, chans)
    shape = jax.ShapeDtypeStruct
    return pl.pallas_call(
        functools.partial(exchange_kernel, ALONG_Z),
        out_shape=[
            shape(grad_out.shape, BF), shape(grad_out.shape, BF), shape(grad_out.shape, F32),
            shape(padded, BF), shape(edge, BF), shape(edge, BF), shape(medium_h.shape, F32),
        ],
        in_specs=[pl.BlockSpec(memory_space=pltpu.VMEM)] * 5,
        out_specs=[pl.BlockSpec(memory_space=pltpu.VMEM)] * 7,
        scratch_shapes=[
            pltpu.VMEM(padded, BF),
            pltpu.VMEM((depth, chans), BF),
            pltpu.VMEM((total, chans), BF),
            pltpu.VMEM((3, total, chans), BF),
            pltpu.VMEM((total, chans), BF),
            pltpu.VMEM((seqs, row_count, chans), F32),
        ]
        + [pltpu.VMEM(half, BF)] * 4
        + [pltpu.VMEM((total, chans), BF)] * 4
        + [pltpu.VMEM(half, F32)] * 2
        + [
            pltpu.VMEM((total, chans), F32),
            pltpu.VMEM(edge, BF),
            pltpu.VMEM((row_count + HALO, LANES), F32),
            pltpu.VMEM((tiles, groups * BLOCK, 2 * BLOCK), BF),
            pltpu.VMEM((tiles, groups * HALO, 2 * BLOCK), BF),
        ]
        + [dma((ALONG_Z,))] * 8
        + [dma((4 * ALONG_Z,))] * 2
        + [dma((3, 4))] * 2
        + [dma((10,))] * 2
        + [dma((4,))] * 2,
        cost_estimate=pl.CostEstimate(flops=flops, bytes_accessed=8 * total * chans, transcendentals=0),
        compiler_params=pltpu.CompilerParams(
            collective_id=2, has_side_effects=True, vmem_limit_bytes=58 << 20
        ),
    )(out_w, rows, short_w, medium_h, grad_out)


def tiled(kernel, ins, outs, scratch, arrays, tiles, flops=0):
    read = sum(math.prod(a.shape) * a.dtype.itemsize for a in arrays)
    return pl.pallas_call(
        kernel,
        grid=(tiles,),
        in_specs=[pl.BlockSpec(block, index) for block, index in ins],
        out_specs=[pl.BlockSpec(block, index) for block, index, _, _ in outs],
        out_shape=[jax.ShapeDtypeStruct(shape, kind) for _, _, shape, kind in outs],
        scratch_shapes=scratch,
        cost_estimate=pl.CostEstimate(flops=flops, bytes_accessed=read, transcendentals=0),
        compiler_params=pltpu.CompilerParams(vmem_limit_bytes=60 << 20),
    )(*arrays)


def shards(projected, short_w, medium_h, out_w, grad_out):
    seqs, row_count, _, chans = projected.shape
    taps = medium_h.shape[1]
    groups_here = medium_h.shape[0]
    tiles = chans // LANES
    groups = groups_here // tiles
    rows = jnp.swapaxes(projected, 1, 2)

    lane3 = lambda i: (0, 0, i)
    lane4 = lambda i: (0, 0, 0, i)
    front_spec = ((seqs, 3, HALO, LANES), lane4)
    rows_spec = ((seqs, 3, row_count, LANES), lane4)
    taps_spec = ((3, short_w.shape[1], LANES), lane3)
    filters_spec = ((groups_here, taps), lambda i: (0, 0))
    full_spec = ((seqs, row_count, LANES), lane3)
    line_rows = pltpu.VMEM((row_count + HALO, LANES), F32)
    padded_spec = ((seqs, row_count + BLOCK, LANES), lane3)
    bands = pltpu.VMEM((groups * BLOCK, 2 * BLOCK), BF)

    block_out, cotangent, mixed, mix, front, later, filter_part = exchange(
        out_w, rows, short_w, medium_h, grad_out
    )
    grad, short_part = tiled(
        backward_kernel,
        [full_spec, front_spec, rows_spec, taps_spec, filters_spec, full_spec, padded_spec, front_spec],
        [
            (*rows_spec, rows.shape, BF),
            ((1, SUM_ROWS, LANES), lambda i: (i, 0, 0), (tiles, SUM_ROWS, LANES), F32),
        ],
        [line_rows, pltpu.VMEM((seqs, row_count, LANES), F32), line_rows, bands],
        (cotangent, front, rows, short_w, medium_h, mixed, mix, later),
        tiles,
    )

    seq_total = seqs * lax.axis_size("dp")
    length_total = row_count * lax.axis_size("ctx")
    scales = (
        1.0 / math.sqrt(seq_total * length_total * (LANES // groups)),
        1.0 / math.sqrt(seq_total * length_total),
    )
    sum_rows = groups_here + tiles * SUM_ROWS
    peers = 2 * (lax.axis_size("ctx") // ALONG_Z)
    piece = (sum_rows // peers, LANES)
    filter_grad, short_grad = pl.pallas_call(
        functools.partial(reduce_kernel, ALONG_Z, scales),
        out_shape=[jax.ShapeDtypeStruct((groups_here, taps), F32), jax.ShapeDtypeStruct(short_w.shape, F32)],
        in_specs=[pl.BlockSpec(memory_space=pltpu.VMEM)] * 2,
        out_specs=[pl.BlockSpec(memory_space=pltpu.VMEM)] * 2,
        scratch_shapes=[
            pltpu.VMEM((sum_rows, LANES), F32),
            pltpu.VMEM((peers, *piece), F32),
            pltpu.VMEM(piece, F32),
            pltpu.VMEM((ALONG_Z, *piece), F32),
            pltpu.VMEM(piece, F32),
            pltpu.VMEM((sum_rows, LANES), F32),
        ]
        + [pltpu.SemaphoreType.DMA((8,))] * 6,
        compiler_params=pltpu.CompilerParams(collective_id=1, has_side_effects=True),
    )(filter_part, short_part)
    return (block_out, jnp.swapaxes(grad, 1, 2), filter_grad, short_grad)


def solution(mesh):
    in_specs = (
        P("dp", "ctx", None, "grp"),
        P(None, None, "grp"),
        P("grp", None),
        P("ctx", "grp"),
        P("dp", "ctx", "grp"),
    )
    out_specs = (
        P("dp", "ctx", "grp"),
        P("dp", "ctx", None, "grp"),
        P("grp", None),
        P(None, None, "grp"),
    )
    return jax.shard_map(shards, mesh=mesh, in_specs=in_specs, out_specs=out_specs, check_vma=False)
```

```python
import functools
import math

import jax
import jax.numpy as jnp
from jax import lax
from jax.experimental import pallas as pl
from jax.experimental.pallas import tpu as pltpu
from jax.sharding import PartitionSpec as P

BF = jnp.bfloat16
F32 = jnp.float32
LANES = 128
BLOCK = 128
HALO = 8
SUM_ROWS = 16
MESH = pl.DeviceIdType.MESH
ALONG_Z = 8


def fill(scratch, front, rows):
    scratch[0:HALO, :] = front.astype(F32)
    scratch[HALO : HALO + rows.shape[0], :] = rows.astype(F32)


def feature(scratch, taps, stream, count):
    total = None
    for offset in range(taps.shape[1]):
        start = HALO - offset
        term = taps[stream, offset : offset + 1, :] * scratch[start : start + count, :]
        total = term if total is None else total + term
    return total


def ahead_lines(filters):
    return jnp.concatenate([filters.astype(F32), jnp.zeros(filters.shape, F32)], axis=1)


def behind_lines(filters):
    taps = filters.shape[1]
    row = lax.broadcasted_iota(jnp.int32, (taps, 2 * BLOCK), 0)
    column = lax.broadcasted_iota(jnp.int32, (taps, 2 * BLOCK), 1)
    return jnp.dot(filters, (row + column == BLOCK).astype(BF), preferred_element_type=F32)


def band_rows(lines, band, count=BLOCK):
    groups = lines.shape[0]
    for g in range(groups):
        line = jnp.broadcast_to(lines[g : g + 1, :], (count, lines.shape[1]))
        turned = pltpu.roll(line, 0, 1, stride=1, stride_axis=0)
        band[g * count : (g + 1) * count, :] = turned.astype(BF)


def group_of_lane(shape, groups):
    lane = lax.broadcasted_iota(jnp.int32, shape, len(shape) - 1)
    return (lane % LANES) // (LANES // groups)


def own_group(wide, groups, count=BLOCK):
    owner = group_of_lane((count, wide.shape[1]), groups)
    kept = wide[0:count]
    for g in range(1, groups):
        kept = jnp.where(owner == g, wide[g * count : (g + 1) * count], kept)
    return kept


def window_pair(padded, start, lanes=slice(None)):
    return jnp.concatenate(
        [padded[s, start : start + 2 * BLOCK, lanes] for s in range(padded.shape[0])], axis=1
    )


def filter_sums(grads, windows, groups):
    rows = lax.broadcasted_iota(jnp.int32, (2 * BLOCK, 2 * BLOCK), 0)
    columns = lax.broadcasted_iota(jnp.int32, (2 * BLOCK, 2 * BLOCK), 1)
    upturn = (rows + columns == 2 * BLOCK - 1).astype(BF)
    windows = jnp.dot(upturn, windows, preferred_element_type=F32).astype(BF)
    owner = group_of_lane(grads.shape, groups)
    wide = grads.astype(F32)
    stacked = jnp.concatenate(
        [jnp.where(owner == g, wide, 0.0).astype(BF) for g in range(groups)], axis=0
    )
    lags = lax.dot_general(
        stacked, windows, (((1,), (1,)), ((), ())), preferred_element_type=F32
    )
    found = []
    for g in range(groups):
        turned = pltpu.roll(lags[g * BLOCK : (g + 1) * BLOCK], 0, 1, stride=1, stride_axis=0)
        found.append(jnp.sum(turned, axis=0, keepdims=True))
    return pltpu.roll(jnp.concatenate(found, axis=0), BLOCK + 1, 1)[:, :BLOCK]


def backward_kernel(
    cotangent_ref, front_ref, rows_ref, taps_ref, filters_ref, mixed_ref,
    padded_ref, next_ref, grad_ref, short_ref, scratch, pulled, later, band,
):
    seqs, row_count = rows_ref.shape[0], rows_ref.shape[2]
    groups = band.shape[0] // BLOCK
    taps = taps_ref.shape[1]
    first = pl.multiple_of(pl.program_id(0) * groups, groups)
    band_rows(ahead_lines(filters_ref[pl.ds(first, groups), :]), band)
    for b in range(row_count // BLOCK):
        wide = jnp.dot(
            band[...], window_pair(padded_ref, b * BLOCK), preferred_element_type=F32
        )
        kept = own_group(wide, groups)
        for s in range(seqs):
            pulled[s, b * BLOCK : (b + 1) * BLOCK, :] = kept[:, s * LANES : (s + 1) * LANES]
    sums = [None] * (3 * taps)
    for s in range(seqs):
        for stream in range(3):
            fill(scratch.at[stream], front_ref[s, stream], rows_ref[s, stream])
        for stream in range(3):
            if stream == 0:
                grad = cotangent_ref[s].astype(F32) * mixed_ref[s]
            else:
                other = 3 - stream
                grad = pulled[s] * feature(scratch.at[other], taps_ref, other, row_count)
            grad = grad.astype(BF).astype(F32)
            later[0:row_count, :] = grad
            later[row_count : row_count + HALO, :] = next_ref[s, stream].astype(F32)
            total = None
            for offset in range(taps):
                term = taps_ref[stream, offset : offset + 1, :] * later[offset : offset + row_count, :]
                total = term if total is None else total + term
                at = HALO - offset
                found = jnp.sum(grad * scratch[stream, at : at + row_count, :], axis=0, keepdims=True)
                row = stream * taps + offset
                sums[row] = found if sums[row] is None else sums[row] + found
            grad_ref[s, stream] = total.astype(BF)
    short_ref[...] = jnp.zeros_like(short_ref)
    for row in range(3 * taps):
        short_ref[0, row : row + 1, :] = sums[row]


def reduce_kernel(
    along_z, scales, filter_ref, short_ref, filter_out, short_out,
    packed, mine_of, part, gathered, whole, result, zs, zr, ys, yr, os, orr,
):
    me, core = lax.axis_index("ctx"), lax.axis_index("dp")
    line, place = me // along_z, me % along_z
    lines = lax.axis_size("ctx") // along_z
    peers = lines * 2
    mine = line * 2 + core
    depth = packed.shape[0] // peers
    tiles, width = short_ref.shape[0], packed.shape[0] // short_ref.shape[0]
    groups = width - short_ref.shape[1]

    def along(step):
        return {"ctx": line * along_z + (place + step) % along_z}

    def across(step):
        other = (mine + step) % peers
        return {"ctx": (other // 2) * along_z + place, "dp": other % 2}

    barrier = pltpu.get_barrier_semaphore()
    for step in range(1, along_z):
        pl.semaphore_signal(barrier, inc=1, device_id=along(step), device_id_type=MESH)
    for step in range(1, peers):
        pl.semaphore_signal(barrier, inc=1, device_id=across(step), device_id_type=MESH)
    for k in range(tiles):
        packed[k * width : k * width + groups, :] = filter_ref[k * groups : (k + 1) * groups, :]
        packed[k * width + groups : (k + 1) * width, :] = short_ref[k]
    pl.semaphore_wait(barrier, along_z + peers - 2)

    def rows_of(piece):
        return pl.ds(pl.multiple_of(piece * depth, depth), depth)

    def first(step):
        return pltpu.make_async_remote_copy(
            src_ref=packed.at[rows_of((mine + step) % peers), :], dst_ref=mine_of.at[mine],
            send_sem=zs.at[step], recv_sem=zr.at[step],
            device_id=across(step), device_id_type=MESH,
        )

    def second(step):
        return pltpu.make_async_remote_copy(
            src_ref=part, dst_ref=gathered.at[place], send_sem=ys.at[step], recv_sem=yr.at[step],
            device_id=along(step), device_id_type=MESH,
        )

    def third(step):
        return pltpu.make_async_remote_copy(
            src_ref=whole, dst_ref=result.at[rows_of(mine), :], send_sem=os.at[step], recv_sem=orr.at[step],
            device_id=across(step), device_id_type=MESH,
        )

    for step in range(1, peers):
        first(step).start()
    mine_of[mine] = packed[rows_of(mine), :]
    for step in range(1, peers):
        first(step).wait_recv()
    total = mine_of[0]
    for k in range(1, peers):
        total = total + mine_of[k]
    part[...] = total
    for step in range(1, along_z):
        second(step).start()
    gathered[place] = total
    for step in range(1, along_z):
        second(step).wait_recv()
    total = gathered[0]
    for k in range(1, along_z):
        total = total + gathered[k]
    whole[...] = total
    for step in range(1, peers):
        third(step).start()
    result[rows_of(mine), :] = total
    for step in range(1, peers):
        third(step).wait_recv()
    taps = short_out.shape[1]
    for k in range(tiles):
        at = k * width
        filter_out[k * groups : (k + 1) * groups, :] = result[at : at + groups, :] * scales[0]
        at += groups
        for stream in range(3):
            rows = result[at + stream * taps : at + (stream + 1) * taps, :]
            short_out[stream, :, k * LANES : (k + 1) * LANES] = rows * scales[1]
    for step in range(1, peers):
        first(step).wait_send()
        third(step).wait_send()
    for step in range(1, along_z):
        second(step).wait_send()


def exchange_kernel(
    along_z, w_ref, rows_ref, taps_ref, filters_ref, cotangent_ref,
    out_ref, grad_ref, mixed_ref, mix_ref, front_ref, later_ref, sums_ref,
    product_ref, whole, gated, gathered, turned, queries, to_a, to_b, from_a, from_b,
    to_right, to_left, from_left, from_right, kept_right, kept_left, own, head,
    scratch, band, low_band,
    z_send, z_recv, up_send, up_recv, down_send, down_recv, far_send, far_recv,
    pair_send, pair_recv, x_send, x_recv, sum_send, sum_recv, halo_send, halo_recv,
):
    ctx, core, x = lax.axis_index("ctx"), lax.axis_index("dp"), lax.axis_index("grp")
    size, ring = lax.axis_size("ctx"), lax.axis_size("grp")
    lines = size // along_z
    y, z = ctx // along_z, ctx % along_z
    edge = jnp.where((z + 1) % along_z < 2, 1, 0)
    part = w_ref.shape[0] // 2
    total, chans = gated.shape
    half = total // 2
    seqs, row_count = rows_ref.shape[0], rows_ref.shape[2]
    tiles = chans // LANES
    groups = filters_ref.shape[0] // tiles

    def at_z(step):
        return {"ctx": y * along_z + (z + along_z + step) % along_z}

    def at_y(step):
        return {"ctx": (y + lines + step) % lines * along_z + z}

    def at_x(step):
        return {"grp": (x + ring + step) % ring}

    def at_ctx(step):
        return {"ctx": (ctx + size + step) % size}

    partner = {"dp": 1 - core}
    barrier = pltpu.get_barrier_semaphore()
    greeted = (at_z(1), at_z(-1), at_y(1), at_y(-1), at_x(1), at_x(-1), at_ctx(1), at_ctx(-1), partner)
    for device in greeted:
        pl.semaphore_signal(barrier, inc=1, device_id=device, device_id_type=MESH)
    pl.semaphore_wait(barrier, len(greeted))

    def copy(src, dst, send, recv, device):
        return pltpu.make_async_remote_copy(
            src_ref=src, dst_ref=dst, send_sem=send, recv_sem=recv, device_id=device, device_id_type=MESH
        )

    started = []

    def go(*what):
        started.append(copy(*what))
        started[-1].start()

    def arrive(here, send, recv, device):
        copy(here, here, send, recv, device).wait_recv()

    def halo(n, src, dst, device):
        go(src, dst, halo_send.at[n], halo_recv.at[n], device)

    def halo_wait(n, here, device, edge):
        arrive(here, halo_send.at[n], halo_recv.at[n], device)

        @pl.when(ctx == edge)
        def _():
            here[...] = jnp.zeros(here.shape, here.dtype)

    def lanes_of(i):
        return pl.ds(pl.multiple_of(i * LANES, LANES), LANES)

    def lines_of(ref, i):
        return ref[pl.ds(pl.multiple_of(i * groups, groups), groups), :]

    def block(step_y, step_z, carrier):
        row = ((y + lines + step_y) % lines * along_z + (z + along_z + step_z) % along_z) * 2 + carrier
        return whole.at[pl.ds(pl.multiple_of(row * part, part), part), :]

    steps = [0]
    for k in range(1, along_z // 2):
        steps.append(k)
    for k in range(1, along_z // 2 + 1):
        steps.insert(2 if k == 1 else len(steps), -k)

    def hand_over(kind, step_y, u):
        place = kind * along_z + u
        mine = block(step_y, steps[u], core)
        go(mine, mine, pair_send.at[place], pair_recv.at[place], partner)

    def z_turn(u):
        mine = w_ref.at[pl.ds(pl.multiple_of(core * part, part), part), :]
        if u > 0:
            mine = block(0, steps[u], core)
            arrive(mine, z_send.at[u], z_recv.at[u], at_z(1))
        for direction in (-1, 1):
            onward = steps[u] + direction
            if onward in steps and (u == 0 or steps[u] * direction > 0):
                v = steps.index(onward)
                go(mine, block(0, steps[u], core), z_send.at[v], z_recv.at[v], at_z(-direction))
        upward = copy(mine, block(0, steps[u], core), up_send.at[u], up_recv.at[u], at_y(1))
        started.append(upward)
        if along_z >= 8 and 1 <= u <= 4:
            pl.when(z != 0)(upward.start)
            held.append(upward)
        else:
            upward.start()
        go(mine, block(0, steps[u], core), down_send.at[u], down_recv.at[u], at_y(-1))
        if u > 0:
            hand_over(0, 0, u)

    held = []

    def release():
        for upward in held:
            pl.when(z == 0)(upward.start)

    def y_turn(u):
        behind, ahead = block(-1, steps[u], core), block(1, steps[u], core)
        arrive(behind, up_send.at[u], up_recv.at[u], at_y(1))
        hand_over(1, -1, u)
        arrive(ahead, down_send.at[u], down_recv.at[u], at_y(-1))
        hand_over(2, 1, u)
        up = 1 if u % 2 == 0 else -1
        if u % 4 == 0:
            up = 1 - 2 * edge
        onward = block(-up, steps[u], core)
        go(onward, onward, far_send.at[u], far_recv.at[u], at_y(up))

    def far_turn(u):
        arrive(block(2, steps[u], core), far_send.at[u], far_recv.at[u], at_y(1))
        hand_over(3, 2, u)

    pieces = [(b, s) for b in (1, 0) for s in range(seqs)]

    def flat_rows(b, s):
        return pl.ds((b * seqs + s) * BLOCK, BLOCK)

    def x_start(c):
        here = flat_rows(*pieces[c])
        src = gated.at[here, :]
        go(src, gathered.at[0, here, :], x_send.at[0, c], x_recv.at[0, c], at_x(1))
        go(src, gathered.at[1, here, :], x_send.at[1, c], x_recv.at[1, c], at_x(-1))

    def x_wait(slot, c):
        arrive(gathered.at[slot, flat_rows(*pieces[c]), :], x_send.at[slot, c], x_recv.at[slot, c], at_x(1))

    def x_turn(c):
        x_wait(0, c)
        x_wait(1, c)
        here = flat_rows(*pieces[c])
        slot, to = (0, at_x(1)) if c < len(pieces) // 2 else (1, at_x(-1))
        go(gathered.at[slot, here, :], gathered.at[2, here, :], x_send.at[2, c], x_recv.at[2, c], to)

    def mix_block(i, b):
        wide = jnp.dot(band[i], window_pair(product_ref, b * BLOCK, lanes_of(i)), preferred_element_type=F32)
        kept = own_group(wide, groups)
        for s in range(seqs):
            mixed = kept[:, s * LANES : (s + 1) * LANES]
            here = slice(b * BLOCK, (b + 1) * BLOCK)
            mixed_ref[s, here, lanes_of(i)] = mixed
            gated[flat_rows(b, s), lanes_of(i)] = (queries[s, here, lanes_of(i)] * mixed).astype(BF)

    def taps_of(i):
        return taps_ref[:, :, lanes_of(i)]

    def features_of(i, s, streams, count, at=0):
        found = []
        for stream in streams:
            if at == 0:
                before = front_ref[s, stream, :, lanes_of(i)]
            else:
                before = rows_ref[s, stream, at - HALO : at, lanes_of(i)]
            fill(scratch, before, rows_ref[s, stream, at : at + count, lanes_of(i)])
            taps, sum_ = taps_of(i), None
            for offset in range(taps.shape[1]):
                start = HALO - offset
                term = taps[stream, offset : offset + 1, :] * scratch[start : start + count, :]
                sum_ = term if sum_ is None else sum_ + term
            found.append(sum_)
        return found

    def features(i, at, count):
        for s in range(seqs):
            query, key, value = features_of(i, s, range(3), count, at)
            queries[s, at : at + count, lanes_of(i)] = query
            product_ref[s, BLOCK + at : BLOCK + at + count, lanes_of(i)] = (key * value).astype(BF)

    last = row_count - BLOCK

    def tails(i, carry):
        features(i, last, BLOCK)
        return carry

    def bands(i, carry):
        band_rows(behind_lines(lines_of(filters_ref, i)), band.at[i])
        return carry

    def forward(i, carry):
        features(i, 0, last)
        mix_block(i, 1)
        return carry

    def forward_first(i, carry):
        mix_block(i, 0)
        return carry

    halo(0, rows_ref.at[:, :, row_count - HALO :, :], front_ref, at_ctx(1))
    z_turn(0)
    lax.fori_loop(0, tiles, tails, 0)
    halo(1, product_ref.at[:, row_count:, :], product_ref.at[:, 0:BLOCK, :], at_ctx(1))
    lax.fori_loop(0, tiles, bands, 0)
    for b in range(row_count // BLOCK):
        for s in range(seqs):
            turned[flat_rows(b, s), :] = cotangent_ref[s, b * BLOCK : (b + 1) * BLOCK, :]
    for u in range(1, min(3, along_z)):
        z_turn(u)
    halo_wait(0, front_ref, at_ctx(1), 0)
    lax.fori_loop(0, tiles, forward, 0)
    x_start(0)
    x_start(1)
    whole[pl.ds(pl.multiple_of(ctx * 2 * part, 2 * part), 2 * part), :] = w_ref[...]

    def second_half():
        halo_wait(1, product_ref.at[:, 0:BLOCK, :], at_ctx(1), 0)
        lax.fori_loop(0, tiles, forward_first, 0)
        x_start(2)
        x_start(3)

    plan = []
    for u in range(along_z):
        plan += [(z_turn, u)] if u >= 3 else []
        plan += [(y_turn, u - 3)] if u >= 3 else []
        plan += [(far_turn, u - 4)] if u >= 4 else []
    plan.insert(min(len(plan), 9), (x_turn, 0))
    plan.insert(min(len(plan), 13), (second_half,))
    for u in range(max(along_z - 3, 0), along_z):
        plan += [(y_turn, u), (far_turn, u - 1)] if u > 0 else [(y_turn, u)]
        if u == along_z - 3:
            plan.append((x_turn, 1))
    plan += [(far_turn, along_z - 1), (x_turn, 2)]
    if along_z >= 8:
        plan.remove((z_turn, 5))
        at = plan.index((y_turn, 1))
        plan[at:at] = [(z_turn, 5), (release,)]
    if along_z < 8:
        plan = [(second_half,)] + [(x_turn, c) for c in range(3)]
        plan += [(y_turn, u) for u in range(along_z)] + [(far_turn, u) for u in range(along_z)]
    for what, *which in plan:
        what(*which)
    for kind, step_y in enumerate((0, -1, 1, 2)):
        for u in range(1 if kind == 0 else 0, along_z):
            place = kind * along_z + u
            arrive(block(step_y, steps[u], 1 - core), pair_send.at[place], pair_recv.at[place], partner)

    wide = min(chans, 256)
    right, left, across = (x + 1) % ring, (x + ring - 1) % ring, (x + 2) % ring
    count = chans // wide

    def columns(j):
        return pl.ds(pl.multiple_of(j * wide, wide), wide)

    def partial(owner, j):
        rows = whole[pl.ds(pl.multiple_of(owner * chans + j * wide, wide), wide), :]
        return lax.dot_general(turned[...], rows, (((1,), (1,)), ((), ())), preferred_element_type=F32)

    def far_sums(j, carry):
        found = partial(across, j)
        to_a[:, columns(j)] = found[:half].astype(BF)
        to_b[:, columns(j)] = found[half:].astype(BF)
        return carry

    def near_sums(j, carry):
        found = partial(left, j)
        to_left[:half, columns(j)] = found[:half].astype(BF)
        kept_left[:, columns(j)] = found[half:]
        found = partial(right, j)
        kept_right[:, columns(j)] = found[:half]
        to_right[half:, columns(j)] = found[half:].astype(BF)
        return carry

    def own_sums(j, carry):
        own[:, columns(j)] = partial(x, j)
        return carry

    def outputs(j, carry):
        found = None
        for slot, owner in ((None, x), (0, left), (1, right), (2, across)):
            rows = whole[pl.ds(pl.multiple_of(owner * chans, chans), chans), columns(j)]
            source = gated[...] if slot is None else gathered[slot]
            term = jnp.dot(source, rows, preferred_element_type=F32)
            found = term if found is None else found + term
        for b in range(row_count // BLOCK):
            for s in range(seqs):
                at = (b * seqs + s) * BLOCK
                out_ref[s, b * BLOCK : (b + 1) * BLOCK, columns(j)] = found[at : at + BLOCK].astype(BF)
        return carry

    def piece(ref, at, n):
        return ref.at[pl.ds(at + n * BLOCK, BLOCK), :]

    def send_sum(n, src, dst, device):
        go(src, dst, sum_send.at[n], sum_recv.at[n], device)

    def wait_sum(n, here):
        arrive(here, sum_send.at[n], sum_recv.at[n], at_x(1))

    def relay_a(n):
        wait_sum(n, piece(from_a, 0, n))
        rows = slice(n * BLOCK, (n + 1) * BLOCK)
        to_right[rows, :] = (kept_right[rows, :] + from_a[rows, :].astype(F32)).astype(BF)
        send_sum(4 + n, piece(to_right, 0, n), piece(from_left, 0, n), at_x(1))

    def relay_b(n):
        wait_sum(2 + n, piece(from_b, 0, n))
        rows, there = slice(n * BLOCK, (n + 1) * BLOCK), slice(half + n * BLOCK, half + (n + 1) * BLOCK)
        to_left[there, :] = (kept_left[rows, :] + from_b[rows, :].astype(F32)).astype(BF)
        send_sum(6 + n, piece(to_left, half, n), piece(from_right, half, n), at_x(-1))

    first, second = pl.ds(0, half), pl.ds(half, half)
    lax.fori_loop(0, count, far_sums, 0)
    x_turn(3)
    for n in range(2):
        send_sum(n, piece(to_a, 0, n), piece(from_a, 0, n), at_x(1))
        send_sum(2 + n, piece(to_b, 0, n), piece(from_b, 0, n), at_x(-1))
    lax.fori_loop(0, count, near_sums, 0)
    send_sum(8, to_left.at[first, :], from_right.at[first, :], at_x(-1))
    relay_a(0)
    lax.fori_loop(0, count, own_sums, 0)
    relay_a(1)
    send_sum(9, to_right.at[second, :], from_left.at[second, :], at_x(1))
    relay_b(0)
    relay_b(1)
    for c in range(len(pieces)):
        x_wait(2, c)
    lax.fori_loop(0, count, outputs, 0)

    def finish(b):
        for s in range(seqs):
            at = slice((b * seqs + s) * BLOCK, (b * seqs + s + 1) * BLOCK)
            here = slice(b * BLOCK, (b + 1) * BLOCK)
            found = own[at, :] + (from_left[at, :].astype(F32) + from_right[at, :].astype(F32))
            found = found.astype(BF)
            grad_ref[s, here, :] = found
            mix_ref[s, here, :] = (found.astype(F32) * queries[s, here, :]).astype(BF)

    def low_bands(i, carry):
        band_rows(ahead_lines(lines_of(filters_ref, i)), low_band.at[i], HALO)
        return carry

    lax.fori_loop(0, tiles, low_bands, 0)
    wait_sum(8, from_right.at[first, :])
    for n in range(2):
        wait_sum(4 + n, piece(from_left, 0, n))
    finish(0)
    halo(2, mix_ref.at[:, 0:BLOCK, :], mix_ref.at[:, row_count:, :], at_ctx(-1))

    def block_sums(i, b):
        grads = [mix_ref[s, b * BLOCK : (b + 1) * BLOCK, lanes_of(i)] for s in range(seqs)]
        windows = window_pair(product_ref, b * BLOCK, lanes_of(i))
        return filter_sums(jnp.concatenate(grads, axis=1), windows, groups)

    def sums_of(i):
        return pl.ds(pl.multiple_of(i * groups, groups), groups)

    def first_sums(i, carry):
        sums_ref[sums_of(i), :] = block_sums(i, 0)
        return carry

    def second_sums(i, carry):
        sums_ref[sums_of(i), :] += block_sums(i, 1)
        return carry

    lax.fori_loop(0, tiles, first_sums, 0)
    wait_sum(9, from_left.at[second, :])
    for n in range(2):
        wait_sum(6 + n, piece(from_right, half, n))
    finish(1)

    def heads(i, carry):
        low = jnp.dot(low_band[i], window_pair(mix_ref, 0, lanes_of(i)), preferred_element_type=F32)
        pulled = own_group(low, groups, HALO)
        for s in range(seqs):
            here = pulled[:, s * LANES : (s + 1) * LANES]
            key, value = features_of(i, s, (1, 2), HALO)
            grad = grad_ref[s, 0:HALO, lanes_of(i)].astype(F32)
            head[s, 0, :, lanes_of(i)] = (grad * mixed_ref[s, 0:HALO, lanes_of(i)]).astype(BF)
            head[s, 1, :, lanes_of(i)] = (here * value).astype(BF)
            head[s, 2, :, lanes_of(i)] = (here * key).astype(BF)
        return carry

    lax.fori_loop(0, tiles, heads, 0)
    halo(3, head, later_ref, at_ctx(-1))
    lax.fori_loop(0, tiles, second_sums, 0)
    halo_wait(2, mix_ref.at[:, row_count:, :], at_ctx(-1), size - 1)
    halo_wait(3, later_ref, at_ctx(-1), size - 1)
    for sent in started:
        sent.wait_send()


def exchange(out_w, rows, short_w, medium_h, grad_out):
    seqs, row_count, chans = grad_out.shape
    total = seqs * row_count
    depth = out_w.shape[0] * lax.axis_size("ctx")
    tiles = chans // LANES
    groups = medium_h.shape[0] // tiles
    half = (total // 2, chans)
    dma = pltpu.SemaphoreType.DMA
    flops = 4 * total * depth * chans
    padded = (seqs, row_count + BLOCK, chans)
    edge = (seqs, 3, HALO, chans)
    shape = jax.ShapeDtypeStruct
    return pl.pallas_call(
        functools.partial(exchange_kernel, ALONG_Z),
        out_shape=[
            shape(grad_out.shape, BF), shape(grad_out.shape, BF), shape(grad_out.shape, F32),
            shape(padded, BF), shape(edge, BF), shape(edge, BF), shape(medium_h.shape, F32),
        ],
        in_specs=[pl.BlockSpec(memory_space=pltpu.VMEM)] * 5,
        out_specs=[pl.BlockSpec(memory_space=pltpu.VMEM)] * 7,
        scratch_shapes=[
            pltpu.VMEM(padded, BF),
            pltpu.VMEM((depth, chans), BF),
            pltpu.VMEM((total, chans), BF),
            pltpu.VMEM((3, total, chans), BF),
            pltpu.VMEM((total, chans), BF),
            pltpu.VMEM((seqs, row_count, chans), F32),
        ]
        + [pltpu.VMEM(half, BF)] * 4
        + [pltpu.VMEM((total, chans), BF)] * 4
        + [pltpu.VMEM(half, F32)] * 2
        + [
            pltpu.VMEM((total, chans), F32),
            pltpu.VMEM(edge, BF),
            pltpu.VMEM((row_count + HALO, LANES), F32),
            pltpu.VMEM((tiles, groups * BLOCK, 2 * BLOCK), BF),
            pltpu.VMEM((tiles, groups * HALO, 2 * BLOCK), BF),
        ]
        + [dma((ALONG_Z,))] * 8
        + [dma((4 * ALONG_Z,))] * 2
        + [dma((3, 4))] * 2
        + [dma((10,))] * 2
        + [dma((4,))] * 2,
        cost_estimate=pl.CostEstimate(flops=flops, bytes_accessed=8 * total * chans, transcendentals=0),
        compiler_params=pltpu.CompilerParams(
            collective_id=2, has_side_effects=True, vmem_limit_bytes=58 << 20
        ),
    )(out_w, rows, short_w, medium_h, grad_out)


def tiled(kernel, ins, outs, scratch, arrays, tiles, flops=0):
    read = sum(math.prod(a.shape) * a.dtype.itemsize for a in arrays)
    return pl.pallas_call(
        kernel,
        grid=(tiles,),
        in_specs=[pl.BlockSpec(block, index) for block, index in ins],
        out_specs=[pl.BlockSpec(block, index) for block, index, _, _ in outs],
        out_shape=[jax.ShapeDtypeStruct(shape, kind) for _, _, shape, kind in outs],
        scratch_shapes=scratch,
        cost_estimate=pl.CostEstimate(flops=flops, bytes_accessed=read, transcendentals=0),
        compiler_params=pltpu.CompilerParams(vmem_limit_bytes=60 << 20),
    )(*arrays)


def shards(projected, short_w, medium_h, out_w, grad_out):
    seqs, row_count, _, chans = projected.shape
    taps = medium_h.shape[1]
    groups_here = medium_h.shape[0]
    tiles = chans // LANES
    groups = groups_here // tiles
    rows = jnp.swapaxes(projected, 1, 2)

    lane3 = lambda i: (0, 0, i)
    lane4 = lambda i: (0, 0, 0, i)
    front_spec = ((seqs, 3, HALO, LANES), lane4)
    rows_spec = ((seqs, 3, row_count, LANES), lane4)
    taps_spec = ((3, short_w.shape[1], LANES), lane3)
    filters_spec = ((groups_here, taps), lambda i: (0, 0))
    full_spec = ((seqs, row_count, LANES), lane3)
    line_rows = pltpu.VMEM((row_count + HALO, LANES), F32)
    padded_spec = ((seqs, row_count + BLOCK, LANES), lane3)
    bands = pltpu.VMEM((groups * BLOCK, 2 * BLOCK), BF)

    block_out, cotangent, mixed, mix, front, later, filter_part = exchange(
        out_w, rows, short_w, medium_h, grad_out
    )
    grad, short_part = tiled(
        backward_kernel,
        [full_spec, front_spec, rows_spec, taps_spec, filters_spec, full_spec, padded_spec, front_spec],
        [
            (*rows_spec, rows.shape, BF),
            ((1, SUM_ROWS, LANES), lambda i: (i, 0, 0), (tiles, SUM_ROWS, LANES), F32),
        ],
        [
            pltpu.VMEM((3, row_count + HALO, LANES), F32),
            pltpu.VMEM((seqs, row_count, LANES), F32),
            line_rows,
            bands,
        ],
        (cotangent, front, rows, short_w, medium_h, mixed, mix, later),
        tiles,
    )

    seq_total = seqs * lax.axis_size("dp")
    length_total = row_count * lax.axis_size("ctx")
    scales = (
        1.0 / math.sqrt(seq_total * length_total * (LANES // groups)),
        1.0 / math.sqrt(seq_total * length_total),
    )
    sum_rows = groups_here + tiles * SUM_ROWS
    peers = 2 * (lax.axis_size("ctx") // ALONG_Z)
    piece = (sum_rows // peers, LANES)
    filter_grad, short_grad = pl.pallas_call(
        functools.partial(reduce_kernel, ALONG_Z, scales),
        out_shape=[jax.ShapeDtypeStruct((groups_here, taps), F32), jax.ShapeDtypeStruct(short_w.shape, F32)],
        in_specs=[pl.BlockSpec(memory_space=pltpu.VMEM)] * 2,
        out_specs=[pl.BlockSpec(memory_space=pltpu.VMEM)] * 2,
        scratch_shapes=[
            pltpu.VMEM((sum_rows, LANES), F32),
            pltpu.VMEM((peers, *piece), F32),
            pltpu.VMEM(piece, F32),
            pltpu.VMEM((ALONG_Z, *piece), F32),
            pltpu.VMEM(piece, F32),
            pltpu.VMEM((sum_rows, LANES), F32),
        ]
        + [pltpu.SemaphoreType.DMA((8,))] * 6,
        compiler_params=pltpu.CompilerParams(collective_id=1, has_side_effects=True),
    )(filter_part, short_part)
    return (block_out, jnp.swapaxes(grad, 1, 2), filter_grad, short_grad)


def solution(mesh):
    in_specs = (
        P("dp", "ctx", None, "grp"),
        P(None, None, "grp"),
        P("grp", None),
        P("ctx", "grp"),
        P("dp", "ctx", "grp"),
    )
    out_specs = (
        P("dp", "ctx", "grp"),
        P("dp", "ctx", None, "grp"),
        P("grp", None),
        P(None, None, "grp"),
    )
    return jax.shard_map(shards, mesh=mesh, in_specs=in_specs, out_specs=out_specs, check_vma=False)
```
